32 devices in a mesh: dp: 16 (over z, x, core), seq: 2 (over y).
Axes of the slice: x: 2, y: 2, z: 4, core: 2. Of those that a mesh axis runs over, the one named last changes fastest.
Arguments:
- tokens: bfloat16 [16, 1024, 1280], P('dp', 'seq'), may hold values from -6 to 6
- adapter_index: int32 [16], P('dp'), may hold values from 0 to 7
- norm1_gain: bfloat16 [1280], P(('dp', 'seq')), may hold values from 0.5 to 1.5
- norm1_bias: bfloat16 [1280], P(('dp', 'seq')), may hold values from -1.5 to 1.5
- qkv_weight: bfloat16 [1280, 3840], P(('dp', 'seq')), may hold values from -0.15625 to 0.15625
- qkv_bias: bfloat16 [3840], P(('dp', 'seq')), may hold values from -1.5 to 1.5
- proj_weight: bfloat16 [1280, 1280], P(('dp', 'seq')), may hold values from -0.625 to 0.625
- proj_bias: bfloat16 [1280], P(('dp', 'seq')), may hold values from -1.5 to 1.5
- norm2_gain: bfloat16 [1280], P(('dp', 'seq')), may hold values from 0.5 to 1.5
- norm2_bias: bfloat16 [1280], P(('dp', 'seq')), may hold values from -1.5 to 1.5
- fc1_weight: bfloat16 [1280, 5120], P(('dp', 'seq')), may hold values from -0.15625 to 0.15625
- fc1_bias: bfloat16 [5120], P(('dp', 'seq')), may hold values from -1.5 to 1.5
- fc2_weight: bfloat16 [5120, 1280], P(('dp', 'seq')), may hold values from -0.078125 to 0.078125
- fc2_bias: bfloat16 [1280], P(('dp', 'seq')), may hold values from -1.5 to 1.5
- rel_pos_h: bfloat16 [63, 80], replicated, may hold values from -0.8984375 to 0.8984375
- rel_pos_w: bfloat16 [63, 80], replicated, may hold values from -0.8984375 to 0.8984375
- qkv_down: bfloat16 [1280, 128], P(('dp', 'seq')), may hold values from -0.15625 to 0.15625
- qkv_up: bfloat16 [128, 3840], P(None, ('dp', 'seq')), may hold values from -1.5 to 1.5
- proj_down: bfloat16 [1280, 128], P(('dp', 'seq')), may hold values from -0.625 to 0.625
- proj_up: bfloat16 [128, 1280], P(None, ('dp', 'seq')), may hold values from -1.5 to 1.5
- fc1_down: bfloat16 [1280, 128], P(('dp', 'seq')), may hold values from -0.15625 to 0.15625
- fc1_up: bfloat16 [128, 5120], P(None, ('dp', 'seq')), may hold values from -1.5 to 1.5
- fc2_down: bfloat16 [5120, 128], P(('dp', 'seq')), may hold values from -0.078125 to 0.078125
- fc2_up: bfloat16 [128, 1280], P(None, ('dp', 'seq')), may hold values from -1.5 to 1.5
- out_grad: bfloat16 [16, 1024, 1280], P('dp', 'seq'), may hold values from -6 to 6
Outputs:
- block_out: bfloat16 [16, 1024, 1280], P('dp', 'seq')
- input_grad: float32 [16, 1024, 1280], P('dp', 'seq')
- qkv_down_grad: float32 [1280, 128], P(('dp', 'seq'))
- qkv_up_grad: float32 [128, 3840], P(None, ('dp', 'seq'))
- proj_down_grad: float32 [1280, 128], P(('dp', 'seq'))
- proj_up_grad: float32 [128, 1280], P(None, ('dp', 'seq'))
- fc1_down_grad: float32 [1280, 128], P(('dp', 'seq'))
- fc1_up_grad: float32 [128, 5120], P(None, ('dp', 'seq'))
- fc2_down_grad: float32 [5120, 128], P(('dp', 'seq'))
- fc2_up_grad: float32 [128, 1280], P(None, ('dp', 'seq'))
The draws below stay inside these ranges and needn't reach their ends.
All inputs are finite; a program needn't handle non-finite values.
Results may differ from the reference program's by a relative error of at most 0.015.
Values may be sent and summed in bfloat16 or wider, within the bound.
A program may use at most 512 MiB of HBM per device.

```python
import jax
import jax.numpy as jnp
from jax import lax

HEADS = 16
HEAD_DIM = 80
D = 1280
FF = 5120
ADAPTERS = 8
RANK = 16
G = 32
IMAGES = 16
TOKENS = 1024
TABLE = 63


def set_ends(result, rng, low, largest):
    longest = result.shape.index(max(result.shape))
    spots = []
    for shift in (0, 1):
        where = [jax.random.randint(jax.random.fold_in(rng, axis), (), 0, length) for axis, length in enumerate(result.shape)]
        where[longest] = (where[longest] + shift) % result.shape[longest]
        spots.append(tuple(where))
    return result.at[spots[0]].set(low).at[spots[1]].set(largest)


def block_levels(rng, extent, pieces, least, largest):
    level, own = 1.0, jax.random.fold_in(rng, 6)
    for axis_at, blocks in pieces:
        draws = jnp.exp(jax.random.uniform(jax.random.fold_in(own, axis_at), (blocks,), jnp.float32, least / len(pieces), largest / len(pieces)))
        level = level * jnp.repeat(draws, extent[axis_at] // blocks).reshape([-1 if axis == axis_at else 1 for axis in range(len(extent))])
    return level


def bell_draw(rng, dims, scale, bound, split=(), dtype=jnp.bfloat16):
    level = block_levels(rng, dims, split, -0.22, 0.18) if split else 1.0
    result = jax.random.normal(rng, dims, jnp.float32) * scale * level
    return jnp.minimum(jnp.maximum(result, -bound), bound).astype(dtype)


def setup_inputs(seed: int = 0) -> dict:
    seeds = jax.random.split(jax.random.key(seed), 26)
    tokens = bell_draw(seeds[0], (IMAGES, TOKENS, D), 1.0, 6.0, ((0, 16), (1, 2)))
    adapter_index = set_ends(jax.random.randint(seeds[1], (IMAGES,), 0, ADAPTERS), jax.random.fold_in(seeds[1], 1), 0, ADAPTERS - 1).astype(jnp.int32)
    norm1_gain = jnp.clip(1.0 + 0.1 * jax.random.normal(seeds[2], (D,), jnp.float32), 0.5, 1.5).astype(jnp.bfloat16)
    norm1_bias = bell_draw(seeds[3], (D,), 0.3, 1.5, ((0, 32),))
    qkv_weight = bell_draw(seeds[4], (D, 3 * D), D ** -0.5, 0.15625, ((0, 32),))
    qkv_bias = bell_draw(seeds[5], (3 * D,), 0.3, 1.5, ((0, 32),))
    proj_weight = bell_draw(seeds[6], (D, D), (D // 16) ** -0.5, 0.625, ((0, 32),))
    proj_bias = bell_draw(seeds[7], (D,), 0.3, 1.5, ((0, 32),))
    norm2_gain = jnp.clip(1.0 + 0.1 * jax.random.normal(seeds[8], (D,), jnp.float32), 0.5, 1.5).astype(jnp.bfloat16)
    norm2_bias = bell_draw(seeds[9], (D,), 0.3, 1.5, ((0, 32),))
    fc1_weight = bell_draw(seeds[10], (D, FF), D ** -0.5, 0.15625, ((0, 32),))
    fc1_bias = bell_draw(seeds[11], (FF,), 0.3, 1.5, ((0, 32),))
    fc2_weight = bell_draw(seeds[12], (FF, D), FF ** -0.5, 0.078125, ((0, 32),))
    fc2_bias = bell_draw(seeds[13], (D,), 0.3, 1.5, ((0, 32),))
    rel_pos_h = bell_draw(seeds[14], (TABLE, HEAD_DIM), 0.15, 0.8984375)
    rel_pos_w = bell_draw(seeds[15], (TABLE, HEAD_DIM), 0.15, 0.8984375)
    qkv_down = bell_draw(seeds[16], (D, ADAPTERS * RANK), D ** -0.5, 0.15625, ((0, 32),))
    qkv_up = bell_draw(seeds[17], (ADAPTERS * RANK, 3 * D), RANK ** -0.5, 1.5, ((1, 32),))
    proj_down = bell_draw(seeds[18], (D, ADAPTERS * RANK), (D // 16) ** -0.5, 0.625, ((0, 32),))
    proj_up = bell_draw(seeds[19], (ADAPTERS * RANK, D), RANK ** -0.5, 1.5, ((1, 32),))
    fc1_down = bell_draw(seeds[20], (D, ADAPTERS * RANK), D ** -0.5, 0.15625, ((0, 32),))
    fc1_up = bell_draw(seeds[21], (ADAPTERS * RANK, FF), RANK ** -0.5, 1.5, ((1, 32),))
    fc2_down = bell_draw(seeds[22], (FF, ADAPTERS * RANK), FF ** -0.5, 0.078125, ((0, 32),))
    fc2_up = bell_draw(seeds[23], (ADAPTERS * RANK, D), RANK ** -0.5, 1.5, ((1, 32),))
    out_grad = bell_draw(seeds[24], (IMAGES, TOKENS, D), 1.0, 6.0, ((0, 16), (1, 2)))
    return dict(tokens=tokens, adapter_index=adapter_index, norm1_gain=norm1_gain, norm1_bias=norm1_bias, qkv_weight=qkv_weight, qkv_bias=qkv_bias, proj_weight=proj_weight, proj_bias=proj_bias, norm2_gain=norm2_gain, norm2_bias=norm2_bias, fc1_weight=fc1_weight, fc1_bias=fc1_bias, fc2_weight=fc2_weight, fc2_bias=fc2_bias, rel_pos_h=rel_pos_h, rel_pos_w=rel_pos_w, qkv_down=qkv_down, qkv_up=qkv_up, proj_down=proj_down, proj_up=proj_up, fc1_down=fc1_down, fc1_up=fc1_up, fc2_down=fc2_down, fc2_up=fc2_up, out_grad=out_grad)


epsilon = 1e-06
adapter_scale = 0.5
highest = lax.Precision.HIGHEST

@jax.custom_vjp
def low(v):
    return lax.optimization_barrier(v.astype(jnp.bfloat16)).astype(jnp.float32)

@jax.custom_vjp
def low_back(v):
    return v

def low_keep(v):
    return (low(v), None)

def low_pass(kept, grad):
    return (grad,)

def back_keep(v):
    return (v, None)

def back_low(kept, grad):
    return (low(grad),)
low.defvjp(low_keep, low_pass)
low_back.defvjp(back_keep, back_low)

def matmul(left, right):
    return jnp.dot(left, right, precision=highest)

def layer_norm(values, gain, shift):
    average = lax.optimization_barrier(jnp.mean(values, axis=-1, keepdims=True))
    centered = values - average
    variance = lax.optimization_barrier(jnp.mean(centered * centered, axis=-1, keepdims=True))
    return centered * lax.rsqrt(variance + epsilon) * gain + shift

def adapter(source, downward, upward, picked_row):
    middle = low(low_back(matmul(source, downward) * picked_row))
    return adapter_scale * matmul(middle, upward)

def rel_table(lookup):
    places = jnp.arange(G)
    return lookup[places[:, None] - places[None, :] + G - 1]

def one_image(tokens_img, picked_row, frozen, trained, rel_h, rel_w):
    norm1_gain, norm1_bias, qkv_weight, qkv_bias, proj_weight, proj_bias, norm2_gain, norm2_bias, fc1_weight, fc1_bias, fc2_weight, fc2_bias = frozen
    qkv_down, qkv_up, proj_down, proj_up, fc1_down, fc1_up, fc2_down, fc2_up = trained
    length = G * G
    act_one = low(layer_norm(tokens_img, norm1_gain, norm1_bias))
    qkv_rows = matmul(act_one, qkv_weight) + qkv_bias + adapter(act_one, qkv_down, qkv_up, picked_row)
    qkv_rows = low(low_back(qkv_rows))
    queries = qkv_rows[:, :D].reshape(length, HEADS, HEAD_DIM)
    key_rows = qkv_rows[:, D:2 * D].reshape(length, HEADS, HEAD_DIM)
    values = qkv_rows[:, 2 * D:].reshape(length, HEADS, HEAD_DIM)
    scores = jnp.einsum('qnc,knc->nqk', queries, key_rows, precision=highest) * HEAD_DIM ** (-0.5)
    grid_query = queries.reshape(G, G, HEADS, HEAD_DIM)
    along_h = jnp.einsum('xwnc,xkc->nxwk', grid_query, rel_h, precision=highest)
    along_w = jnp.einsum('xwnc,wkc->nxwk', grid_query, rel_w, precision=highest)
    scores = scores.reshape(HEADS, G, G, G, G) + along_h[..., None] + along_w[:, :, :, None, :]
    scores = low_back(scores.reshape(HEADS, length, length))
    shares = low(jax.nn.softmax(scores, axis=-1))
    attended = jnp.einsum('nqk,knc->qnc', shares, values, precision=highest).reshape(length, D)
    attended = low(low_back(attended))
    branch = matmul(attended, proj_weight) + proj_bias + adapter(attended, proj_down, proj_up, picked_row)
    residual = tokens_img + low_back(branch)
    act_two = low(layer_norm(residual, norm2_gain, norm2_bias))
    hidden = matmul(act_two, fc1_weight) + fc1_bias + adapter(act_two, fc1_down, fc1_up, picked_row)
    activated = low(jax.nn.gelu(low_back(hidden), approximate=False))
    return residual + matmul(activated, fc2_weight) + fc2_bias + adapter(activated, fc2_down, fc2_up, picked_row)

def reference(tokens, adapter_index, norm1_gain, norm1_bias, qkv_weight, qkv_bias, proj_weight, proj_bias, norm2_gain, norm2_bias, fc1_weight, fc1_bias, fc2_weight, fc2_bias, rel_pos_h, rel_pos_w, qkv_down, qkv_up, proj_down, proj_up, fc1_down, fc1_up, fc2_down, fc2_up, out_grad):
    frozen = tuple((array.astype(jnp.float32) for array in (norm1_gain, norm1_bias, qkv_weight, qkv_bias, proj_weight, proj_bias, norm2_gain, norm2_bias, fc1_weight, fc1_bias, fc2_weight, fc2_bias)))
    trained = tuple((array.astype(jnp.float32) for array in (qkv_down, qkv_up, proj_down, proj_up, fc1_down, fc1_up, fc2_down, fc2_up)))
    rel_h = rel_table(rel_pos_h.astype(jnp.float32))
    rel_w = rel_table(rel_pos_w.astype(jnp.float32))
    columns = jnp.arange(ADAPTERS * RANK) // RANK
    picked = (columns[None, :] == adapter_index[:, None]).astype(jnp.float32)

    def forward(inputs, adapters):

        def single(tokens_img, picked_row):
            return one_image(tokens_img, picked_row, frozen, adapters, rel_h, rel_w)
        checked = jax.checkpoint(single)
        return lax.map(lambda members: checked(members[0], members[1]), (inputs, picked))
    outputs, pullback = jax.vjp(forward, tokens.astype(jnp.float32), trained)
    input_grad, trained_grad = pullback(out_grad.astype(jnp.float32))
    return (outputs.astype(jnp.bfloat16), input_grad, trained_grad[0], trained_grad[1], trained_grad[2], trained_grad[3], trained_grad[4], trained_grad[5], trained_grad[6], trained_grad[7])
```

```python
import functools

import jax
import jax.numpy as jnp
from jax import lax
from jax.experimental import pallas as pl
from jax.experimental.pallas import tpu as pltpu
from jax.sharding import PartitionSpec as P

HEADS = 16
HEAD_DIM = 80
ADAPTERS = 8
RANK = 16
G = 32
LANES = 128
HALF = HEADS // 2

epsilon = 1e-06
adapter_scale = 0.5
log2e = 1.4426950408889634
score_scale = HEAD_DIM ** (-0.5)
exponent_scale = score_scale * log2e
f32 = jnp.float32
bf16 = jnp.bfloat16


def dot_nn(left, right):
    return lax.dot_general(left, right, (((1,), (0,)), ((), ())), preferred_element_type=f32)


def dot_nt(left, right):
    return lax.dot_general(left, right, (((1,), (1,)), ((), ())), preferred_element_type=f32)


def dot_tn(left, right):
    return lax.dot_general(left, right, (((0,), (0,)), ((), ())), preferred_element_type=f32)


def normalize(values):
    average = jnp.mean(values, axis=-1, keepdims=True)
    centered = values - average
    variance = jnp.mean(centered * centered, axis=-1, keepdims=True)
    inverse = lax.rsqrt(variance + epsilon)
    return centered * inverse, inverse


def norm_back(scaled, normed, inverse):
    return inverse * (
        scaled
        - jnp.mean(scaled, axis=-1, keepdims=True)
        - normed * jnp.mean(scaled * normed, axis=-1, keepdims=True)
    )


def params(semantics, megabytes):
    return pltpu.CompilerParams(
        dimension_semantics=semantics, vmem_limit_bytes=megabytes * 1024 * 1024
    )


def whole(shape):
    zeros = (0,) * len(shape)
    return pl.BlockSpec(shape, lambda *_: zeros)


def qkv_kernel(
    x_ref, gain_ref, shift_ref, weight_ref, bias_ref, down_ref, up_ref, mask_ref,
    heads_ref, mid_ref, act_ref,
):
    part = pl.program_id(0)
    length = x_ref.shape[0]

    @pl.when(part == 0)
    def _():
        normed, _ = normalize(x_ref[...].astype(f32))
        act_ref[...] = (normed * gain_ref[...].astype(f32) + shift_ref[...].astype(f32)).astype(bf16)
        mid_ref[...] = (dot_nn(act_ref[...], down_ref[...]) * mask_ref[...]).astype(bf16)

    rows = min(256, length)
    lane = lax.broadcasted_iota(jnp.int32, (rows, LANES - HEAD_DIM), 1)
    pad = jnp.where((lane == 0) & (part == 2), 1.0, 0.0).astype(bf16)
    for start in range(0, length, rows):
        here = pl.ds(start, rows)
        block = dot_nn(act_ref[here, :], weight_ref[...])
        block = block + bias_ref[...].astype(f32)
        block = block + adapter_scale * dot_nt(mid_ref[here, :], up_ref[...])
        block = block.astype(bf16)
        for head in range(HEADS):
            heads_ref[0, head, here, 0:HEAD_DIM] = block[:, head * HEAD_DIM : (head + 1) * HEAD_DIM]
            heads_ref[0, head, here, HEAD_DIM:LANES] = pad


def qkv_call(tokens, gain, shift, weight, bias, down, up, mask):
    length, features = tokens.shape
    return pl.pallas_call(
        qkv_kernel,
        name="qkv",
        grid=(3,),
        in_specs=[
            whole((length, features)),
            whole((1, features)),
            whole((1, features)),
            pl.BlockSpec((features, features), lambda j: (0, j)),
            pl.BlockSpec((1, features), lambda j: (0, j)),
            whole((features, LANES)),
            pl.BlockSpec((features, LANES), lambda j: (j, 0)),
            whole((1, LANES)),
        ],
        out_specs=[
            pl.BlockSpec((1, HEADS, length, LANES), lambda j: (j, 0, 0, 0)),
            whole((length, LANES)),
        ],
        out_shape=[
            jax.ShapeDtypeStruct((3, HEADS, length, LANES), bf16),
            jax.ShapeDtypeStruct((length, LANES), bf16),
        ],
        scratch_shapes=[pltpu.VMEM((length, features), bf16)],
        compiler_params=params(("arbitrary",), 50),
        cost_estimate=pl.CostEstimate(
            flops=6 * length * features * features,
            bytes_accessed=2 * (3 * features * features + 4 * length * features),
            transcendentals=0,
        ),
    )(tokens, gain, shift, weight, bias, down, up, mask)


def forward_kernel(place_ref, q_ref, k_ref, v_ref, table_ref, spots_ref, att_ref, lse_ref, aux_ref):
    head = pl.program_id(0)
    length = q_ref.shape[2]
    part_len = att_ref.shape[0]
    lane = lax.broadcasted_iota(jnp.int32, (G, LANES), 1)
    first = lane < LANES // 2
    even = (lane // G) % 2 == 0
    raw = dot_nn(q_ref[0, 0], table_ref[...]) * (HEAD_DIM**0.5)
    for row in range(length // G):
        block = raw[row * G : (row + 1) * G, :]
        high = block.astype(bf16).astype(f32)
        mixed_h = jnp.where(first, high[:, :LANES], block[:, :LANES] - high[:, :LANES])
        mixed_w = jnp.where(first, high[:, LANES:], block[:, LANES:] - high[:, LANES:])
        along_h = pltpu.roll(mixed_h, LANES - G + 1 + row, 1)
        along_w = pltpu.roll(mixed_w, 1, 1, stride=1, stride_axis=0)
        aux_ref[0, pl.ds(row * G, G), :] = jnp.where(even, along_h, along_w).astype(bf16)
    here = pl.ds(pl.multiple_of(place_ref[0] * part_len, G), part_len)
    left = jnp.concatenate([q_ref[0, 0, here, :], aux_ref[0, here, :]], axis=1)
    right = jnp.concatenate([k_ref[0, 0], spots_ref[...]], axis=1)
    scores = dot_nt(left, right)
    top = jnp.max(scores, axis=1, keepdims=True)
    shares = jnp.exp2((scores - top) * exponent_scale).astype(bf16)
    mixed = dot_nn(shares, v_ref[0, 0])
    total = mixed[:, HEAD_DIM : HEAD_DIM + 1]
    att = (mixed[:, :HEAD_DIM] / total).astype(bf16)
    logs = top * exponent_scale + jnp.log2(total)
    lse_ref[0] = jnp.transpose(jnp.broadcast_to(logs, (part_len, LANES)))[0:1, :]
    for slot in range(HALF):

        @pl.when(head % HALF == slot)
        def _():
            att_ref[:, slot * HEAD_DIM : (slot + 1) * HEAD_DIM] = att


def forward_call(place, heads, table, spots, part_len):
    length = heads.shape[2]
    features = HEADS * HEAD_DIM

    def part(index):
        return pl.BlockSpec((1, 1, length, LANES), lambda n, s: (index, n, 0, 0))

    return pl.pallas_call(
        forward_kernel,
        name="attend",
        grid_spec=pltpu.PrefetchScalarGridSpec(
            num_scalar_prefetch=1,
            grid=(HEADS,),
            in_specs=[
                part(0),
                part(1),
                part(2),
                whole((LANES, 2 * LANES)),
                whole((length, LANES)),
            ],
            out_specs=[
                pl.BlockSpec((part_len, features // 2), lambda n, s: (0, n // HALF)),
                pl.BlockSpec((1, 1, part_len), lambda n, s: (n, 0, 0)),
                pl.BlockSpec((1, length, LANES), lambda n, s: (n, 0, 0)),
            ],
        ),
        out_shape=[
            jax.ShapeDtypeStruct((part_len, features), bf16),
            jax.ShapeDtypeStruct((HEADS, 1, part_len), f32),
            jax.ShapeDtypeStruct((HEADS, length, LANES), bf16),
        ],
        compiler_params=params(("arbitrary",), 40),
        cost_estimate=pl.CostEstimate(
            flops=4 * HEADS * part_len * length * LANES * 2,
            bytes_accessed=8 * HEADS * length * LANES,
            transcendentals=HEADS * part_len * length,
        ),
    )(place, heads, heads, heads, table, spots)


def head_lanes(source, head, padded):
    padded[:, HEAD_DIM:LANES] = jnp.zeros((padded.shape[0], LANES - HEAD_DIM), bf16)
    for slot in range(HALF):

        @pl.when(head % HALF == slot)
        def _():
            padded[:, 0:HEAD_DIM] = source[:, slot * HEAD_DIM : (slot + 1) * HEAD_DIM]


def own_kernel(
    place_ref, q_ref, aux_ref, k_ref, v_ref, spots_ref, turned_spots_ref, table_ref, grad_ref,
    lse_ref, inner_ref, dq_ref, dk_ref, dv_ref, shares_ref, dscores_ref, padded,
):
    head = pl.program_id(0)
    part_len = q_ref.shape[2]
    head_lanes(grad_ref, head, padded)
    queries = q_ref[0, 0]
    keys = k_ref[0, 0]
    left = jnp.concatenate([keys, spots_ref[...]], axis=1)
    right = jnp.concatenate([queries, aux_ref[0]], axis=1)
    shares = jnp.exp2(dot_nt(left, right) * exponent_scale - lse_ref[0])
    grad_shares = dot_nt(v_ref[0, 0], padded[...])
    shares_ref[...] = shares.astype(bf16)
    dscores_ref[...] = (shares * (grad_shares - inner_ref[0])).astype(bf16)
    flat = dot_tn(jnp.concatenate([keys, turned_spots_ref[...]], axis=1), dscores_ref[...])
    turned = jnp.transpose(flat)
    lane = lax.broadcasted_iota(jnp.int32, (G, LANES), 1)
    first = lane < LANES // 2
    even = (lane // G) % 2 == 0
    start = place_ref[0] * (part_len // G)
    pieces_h, pieces_w = [], []
    for row in range(part_len // G):
        sums = turned[row * G : (row + 1) * G, LANES:]
        high = sums.astype(bf16).astype(f32)
        mixed = jnp.where(first, high, sums - high)
        pieces_h.append(pltpu.roll(jnp.where(even, mixed, 0.0), start + row, 1))
        pieces_w.append(
            pltpu.roll(jnp.where(even, 0.0, mixed), LANES - G, 1, stride=1, stride_axis=0)
        )
    spread = jnp.concatenate(
        [jnp.concatenate(pieces_h, axis=0), jnp.concatenate(pieces_w, axis=0)], axis=1
    ).astype(bf16)
    grad_query = turned[:, :LANES] * score_scale + dot_nn(spread, table_ref[...])
    grad_query = grad_query[:, :HEAD_DIM].astype(bf16)
    for slot in range(HALF):

        @pl.when(head % HALF == slot)
        def _():
            dq_ref[:, slot * HEAD_DIM : (slot + 1) * HEAD_DIM] = grad_query

    here = pl.ds(pl.multiple_of(place_ref[0] * part_len, G), part_len)
    dk_ref[0] = dot_nn(dscores_ref[here, :], queries)
    dv_ref[0] = dot_nn(shares_ref[here, :], padded[...])


def own_call(place, heads, aux, spots, turned_spots, table, grad, lse, inner):
    length = heads.shape[2]
    part_len, features = grad.shape

    def part(index):
        return pl.BlockSpec((1, 1, length, LANES), lambda n, s: (index, n, 0, 0))

    return pl.pallas_call(
        own_kernel,
        name="back_own",
        grid_spec=pltpu.PrefetchScalarGridSpec(
            num_scalar_prefetch=1,
            grid=(HEADS,),
            in_specs=[
                pl.BlockSpec((1, 1, part_len, LANES), lambda n, s: (0, n, s[0], 0)),
                pl.BlockSpec((1, part_len, LANES), lambda n, s: (n, s[0], 0)),
                part(1),
                part(2),
                whole((length, LANES)),
                whole((length, LANES)),
                whole((2 * LANES, LANES)),
                pl.BlockSpec((part_len, features // 2), lambda n, s: (0, n // HALF)),
                pl.BlockSpec((1, 1, part_len), lambda n, s: (n, 0, 0)),
                pl.BlockSpec((1, 1, part_len), lambda n, s: (n, 0, 0)),
            ],
            out_specs=[
                pl.BlockSpec((part_len, features // 2), lambda n, s: (0, n // HALF)),
                pl.BlockSpec((1, part_len, LANES), lambda n, s: (n, 0, 0)),
                pl.BlockSpec((1, part_len, LANES), lambda n, s: (n, 0, 0)),
            ],
            scratch_shapes=[
                pltpu.VMEM((length, part_len), bf16),
                pltpu.VMEM((length, part_len), bf16),
                pltpu.VMEM((part_len, LANES), bf16),
            ],
        ),
        out_shape=[
            jax.ShapeDtypeStruct((part_len, features), bf16),
            jax.ShapeDtypeStruct((HEADS, part_len, LANES), f32),
            jax.ShapeDtypeStruct((HEADS, part_len, LANES), f32),
        ],
        compiler_params=params(("arbitrary",), 40),
        cost_estimate=pl.CostEstimate(
            flops=8 * HEADS * part_len * length * LANES * 2,
            bytes_accessed=12 * HEADS * length * LANES,
            transcendentals=HEADS * part_len * length,
        ),
    )(place, heads, aux, heads, heads, spots, turned_spots, table, grad, lse, inner)


def other_kernel(
    place_ref, q_ref, aux_ref, k_ref, v_ref, spots_ref, grad_ref, lse_ref, inner_ref, dk_in, dv_in,
    dk_ref, dv_ref, dk_sum, dv_sum, padded,
):
    head = pl.program_id(0)
    step = pl.program_id(1)
    head_lanes(grad_ref.at[0], head, padded)
    queries = q_ref[0, 0]
    left = jnp.concatenate([k_ref[0, 0], spots_ref[...]], axis=1)
    right = jnp.concatenate([queries, aux_ref[0]], axis=1)
    shares = jnp.exp2(dot_nt(left, right) * exponent_scale - lse_ref[0, 0])
    grad_shares = dot_nt(v_ref[0, 0], padded[...])
    dscores = (shares * (grad_shares - inner_ref[0, 0])).astype(bf16)

    @pl.when(step == 0)
    def _():
        dk_sum[...] = dk_in[0]
        dv_sum[...] = dv_in[0]

    dk_sum[...] += dot_nn(dscores, queries)
    dv_sum[...] += dot_nn(shares.astype(bf16), padded[...])

    @pl.when(step == pl.num_programs(1) - 1)
    def _():
        grad_key = (dk_sum[:, :HEAD_DIM] * score_scale).astype(bf16)
        grad_value = dv_sum[:, :HEAD_DIM].astype(bf16)
        for slot in range(HALF):

            @pl.when(head % HALF == slot)
            def _():
                dk_ref[:, slot * HEAD_DIM : (slot + 1) * HEAD_DIM] = grad_key
                dv_ref[:, slot * HEAD_DIM : (slot + 1) * HEAD_DIM] = grad_value


def other_call(place, heads, aux, spots, grads, lses, inners, dk, dv):
    length = heads.shape[2]
    blocks, part_len, features = grads.shape
    count = length // part_len

    def theirs(i, s):
        return lax.rem(s[0] + 1 + i, count)

    def given(i, s):
        return theirs(i, s) if blocks > 1 else 0

    def own(index):
        return pl.BlockSpec((1, 1, part_len, LANES), lambda n, i, s: (index, n, s[0], 0))

    stats = pl.BlockSpec((1, 1, 1, part_len), lambda n, i, s: (given(i, s), n, 0, 0))
    sums = pl.BlockSpec((1, part_len, LANES), lambda n, i, s: (n, 0, 0))
    dense = pl.BlockSpec((part_len, features // 2), lambda n, i, s: (0, n // HALF))
    return pl.pallas_call(
        other_kernel,
        name="back_other",
        grid_spec=pltpu.PrefetchScalarGridSpec(
            num_scalar_prefetch=1,
            grid=(HEADS, count - 1),
            in_specs=[
                pl.BlockSpec((1, 1, part_len, LANES), lambda n, i, s: (0, n, theirs(i, s), 0)),
                pl.BlockSpec((1, part_len, LANES), lambda n, i, s: (n, theirs(i, s), 0)),
                own(1),
                own(2),
                pl.BlockSpec((part_len, LANES), lambda n, i, s: (s[0], 0)),
                pl.BlockSpec(
                    (1, part_len, features // 2), lambda n, i, s: (given(i, s), 0, n // HALF)
                ),
                stats,
                stats,
                sums,
                sums,
            ],
            out_specs=[dense, dense],
            scratch_shapes=[
                pltpu.VMEM((part_len, LANES), f32),
                pltpu.VMEM((part_len, LANES), f32),
                pltpu.VMEM((part_len, LANES), bf16),
            ],
        ),
        out_shape=[
            jax.ShapeDtypeStruct((part_len, features), bf16),
            jax.ShapeDtypeStruct((part_len, features), bf16),
        ],
        compiler_params=params(("arbitrary", "arbitrary"), 40),
        cost_estimate=pl.CostEstimate(
            flops=4 * HEADS * part_len * (length - part_len) * LANES * 2,
            bytes_accessed=12 * HEADS * length * LANES,
            transcendentals=HEADS * part_len * (length - part_len),
        ),
    )(place, heads, aux, heads, heads, spots, grads, lses, inners, dk, dv)


def project_kernel(
    att_ref, x_ref, weight_ref, bias_ref, down_ref, up_ref, mask_ref, gain_ref, shift_ref,
    fc1_down_ref, resid_ref, act_ref, mid_ref, mid1_ref,
):
    att = att_ref[...]
    mid_ref[...] = (dot_nn(att, down_ref[...]) * mask_ref[...]).astype(bf16)
    branch = dot_nn(att, weight_ref[...]) + bias_ref[...].astype(f32)
    branch = branch + adapter_scale * dot_nt(mid_ref[...], up_ref[...])
    resid = x_ref[...].astype(f32) + branch
    resid_ref[...] = resid
    normed, _ = normalize(resid)
    act_ref[...] = (normed * gain_ref[...].astype(f32) + shift_ref[...].astype(f32)).astype(bf16)
    mid1_ref[...] = (dot_nn(act_ref[...], fc1_down_ref[...]) * mask_ref[...]).astype(bf16)


def project_call(att, x, weight, bias, down, up, mask, gain, shift, fc1_down):
    rows, features = att.shape
    return pl.pallas_call(
        project_kernel,
        name="project",
        out_shape=[
            jax.ShapeDtypeStruct((rows, features), f32),
            jax.ShapeDtypeStruct((rows, features), bf16),
            jax.ShapeDtypeStruct((rows, LANES), bf16),
            jax.ShapeDtypeStruct((rows, LANES), bf16),
        ],
        compiler_params=params(None, 50),
        cost_estimate=pl.CostEstimate(
            flops=2 * rows * features * features,
            bytes_accessed=2 * features * features + 12 * rows * features,
            transcendentals=0,
        ),
    )(att, x, weight, bias, down, up, mask, gain, shift, fc1_down)


def gelu_parts(hidden):
    size = jnp.abs(hidden) * (0.5**0.5)
    bell = jnp.exp2(hidden * hidden * (-0.5 * log2e))
    t = 1.0 / (1.0 + 0.3275911 * size)
    poly = t * (
        0.254829592
        + t * (-0.284496736 + t * (1.421413741 + t * (-1.453152027 + t * 1.061405429)))
    )
    tail = 0.5 * poly * bell
    cumulative = jnp.where(hidden < 0.0, tail, 1.0 - tail)
    return hidden * cumulative, cumulative + hidden * bell * 0.3989422804014327


def feed_kernel(
    pick_ref, act_ref, resid_ref, og_ref, w1_ref, b1_ref, w2_ref, b2_ref, down1_ref, up1_ref,
    down2_ref, up2_ref, mid1_ref, mask_ref, gain_ref,
    out_ref, grad_ref, branch_ref, gd1_ref, gu1_ref, gd2_ref, gu2_ref,
    total, back, mid2_sum, gm1_sum, gm2, gm2_t, mid1_t,
):
    step = pl.program_id(0)
    picked = pl.ds(pl.multiple_of(pick_ref[0] * RANK, RANK), RANK)
    mask = mask_ref[...]

    @pl.when(step == 0)
    def _():
        total[...] = jnp.zeros_like(total)
        back[...] = jnp.zeros_like(back)
        mid2_sum[...] = jnp.zeros_like(mid2_sum)
        gm1_sum[...] = jnp.zeros_like(gm1_sum)
        middle = adapter_scale * dot_nn(og_ref[...], up2_ref[...]) * mask
        gm2[...] = middle.astype(bf16)
        gm2_t[...] = jnp.transpose(gm2[...].astype(f32)).astype(bf16)
        mid1_t[...] = jnp.transpose(mid1_ref[...].astype(f32)).astype(bf16)

    hidden = dot_nn(act_ref[...], w1_ref[...]) + b1_ref[...].astype(f32)
    hidden = hidden + adapter_scale * dot_nt(mid1_ref[...], up1_ref[...])
    grad_act = dot_nt(og_ref[...], w2_ref[...]) + dot_nt(gm2[...], down2_ref[...])
    value, slope = gelu_parts(hidden)
    activated = value.astype(bf16)
    grad_hidden = (grad_act * slope).astype(bf16)
    total[...] += dot_nn(activated, w2_ref[...])
    mid2_sum[...] += dot_nn(activated, down2_ref[...])
    back[...] += dot_nt(grad_hidden, w1_ref[...])
    gm1_sum[...] += dot_nn(grad_hidden, up1_ref[...])
    gd2_ref[...] = dot_nn(gm2_t[picked, :], activated).astype(bf16)
    gu1_ref[...] = (adapter_scale * dot_nn(mid1_t[picked, :], grad_hidden)).astype(bf16)

    @pl.when(step == pl.num_programs(0) - 1)
    def _():
        mid2 = mid2_sum[...] * mask
        mid2_low = mid2.astype(bf16)
        resid = resid_ref[...]
        final = resid + total[...] + b2_ref[...].astype(f32)
        final = final + adapter_scale * dot_nt(mid2_low, up2_ref[...])
        out_ref[...] = final.astype(bf16)
        gm1 = adapter_scale * gm1_sum[...] * mask
        gm1_low = gm1.astype(bf16)
        upstream = back[...] + dot_nt(gm1_low, down1_ref[...])
        normed, inverse = normalize(resid)
        grad = og_ref[...].astype(f32) + norm_back(
            upstream * gain_ref[...].astype(f32), normed, inverse
        )
        grad_ref[...] = grad
        branch_ref[...] = grad.astype(bf16)
        gm2_t[...] = jnp.transpose(gm1_low.astype(f32)).astype(bf16)
        gd1_ref[...] = dot_nn(gm2_t[picked, :], act_ref[...]).astype(bf16)
        mid1_t[...] = jnp.transpose(mid2_low.astype(f32)).astype(bf16)
        gu2_ref[...] = (adapter_scale * dot_nn(mid1_t[picked, :], og_ref[...])).astype(bf16)


def feed_call(pick, act, resid, og, w1, b1, w2, b2, down1, up1, down2, up2, mid1, mask, gain):
    rows, features = act.shape
    wide = w1.shape[1]
    block = 512
    row_block = pl.BlockSpec((block, LANES), lambda j, s: (j, 0))
    return pl.pallas_call(
        feed_kernel,
        name="feed",
        grid_spec=pltpu.PrefetchScalarGridSpec(
            num_scalar_prefetch=1,
            grid=(wide // block,),
            in_specs=[
                whole((rows, features)),
                whole((rows, features)),
                whole((rows, features)),
                pl.BlockSpec((features, block), lambda j, s: (0, j)),
                pl.BlockSpec((1, block), lambda j, s: (0, j)),
                pl.BlockSpec((block, features), lambda j, s: (j, 0)),
                whole((1, features)),
                whole((features, LANES)),
                row_block,
                row_block,
                whole((features, LANES)),
                whole((rows, LANES)),
                whole((1, LANES)),
                whole((1, features)),
            ],
            out_specs=[
                whole((rows, features)),
                whole((rows, features)),
                whole((rows, features)),
                whole((RANK, features)),
                pl.BlockSpec((RANK, block), lambda j, s: (0, j)),
                pl.BlockSpec((RANK, block), lambda j, s: (0, j)),
                whole((RANK, features)),
            ],
            scratch_shapes=[
                pltpu.VMEM((rows, features), f32),
                pltpu.VMEM((rows, features), f32),
                pltpu.VMEM((rows, LANES), f32),
                pltpu.VMEM((rows, LANES), f32),
                pltpu.VMEM((rows, LANES), bf16),
                pltpu.VMEM((LANES, rows), bf16),
                pltpu.VMEM((LANES, rows), bf16),
            ],
        ),
        out_shape=[
            jax.ShapeDtypeStruct((rows, features), bf16),
            jax.ShapeDtypeStruct((rows, features), f32),
            jax.ShapeDtypeStruct((rows, features), bf16),
            jax.ShapeDtypeStruct((RANK, features), bf16),
            jax.ShapeDtypeStruct((RANK, wide), bf16),
            jax.ShapeDtypeStruct((RANK, wide), bf16),
            jax.ShapeDtypeStruct((RANK, features), bf16),
        ],
        compiler_params=params(("arbitrary",), 58),
        cost_estimate=pl.CostEstimate(
            flops=8 * rows * features * wide,
            bytes_accessed=4 * features * wide + 24 * rows * features,
            transcendentals=2 * rows * wide,
        ),
    )(pick, act, resid, og, w1, b1, w2, b2, down1, up1, down2, up2, mid1, mask, gain)


def unproject_kernel(
    pick_ref, branch_ref, att_ref, weight_ref, down_ref, up_ref, mid_ref, mask_ref, sums_ref,
    grad_ref, inner_ref, gd_ref, gu_ref, turned,
):
    picked = pl.ds(pl.multiple_of(pick_ref[0] * RANK, RANK), RANK)
    branch = branch_ref[...]
    att = att_ref[...]
    middle = (adapter_scale * dot_nn(branch, up_ref[...]) * mask_ref[...]).astype(bf16)
    grad = dot_nt(branch, weight_ref[...]) + dot_nt(middle, down_ref[...])
    grad_ref[...] = grad.astype(bf16)
    product = grad_ref[...].astype(f32) * att.astype(f32)
    high = product.astype(bf16)
    low = (product - high.astype(f32)).astype(bf16)
    inner = dot_nt(sums_ref[...], high) + dot_nt(sums_ref[...], low)
    for head in range(HEADS):
        inner_ref[head] = inner[head : head + 1, :]
    turned[...] = jnp.transpose(middle.astype(f32)).astype(bf16)
    gd_ref[...] = dot_nn(turned[picked, :], att).astype(bf16)
    turned[...] = jnp.transpose(mid_ref[...].astype(f32)).astype(bf16)
    gu_ref[...] = (adapter_scale * dot_nn(turned[picked, :], branch)).astype(bf16)


def unproject_call(pick, branch, att, weight, down, up, mid, mask, sums):
    rows, features = branch.shape
    return pl.pallas_call(
        unproject_kernel,
        name="unproject",
        grid_spec=pltpu.PrefetchScalarGridSpec(
            num_scalar_prefetch=1,
            grid=(1,),
            in_specs=[whole(a.shape) for a in (branch, att, weight, down, up, mid, mask, sums)],
            out_specs=[
                whole((rows, features)),
                whole((HEADS, 1, rows)),
                whole((RANK, features)),
                whole((RANK, features)),
            ],
            scratch_shapes=[pltpu.VMEM((LANES, rows), bf16)],
        ),
        out_shape=[
            jax.ShapeDtypeStruct((rows, features), bf16),
            jax.ShapeDtypeStruct((HEADS, 1, rows), f32),
            jax.ShapeDtypeStruct((RANK, features), bf16),
            jax.ShapeDtypeStruct((RANK, features), bf16),
        ],
        compiler_params=params(("arbitrary",), 50),
        cost_estimate=pl.CostEstimate(
            flops=2 * rows * features * features,
            bytes_accessed=2 * features * features + 8 * rows * features,
            transcendentals=0,
        ),
    )(pick, branch, att, weight, down, up, mid, mask, sums)


def unqkv_kernel(
    pick_ref, dq_ref, dk_ref, dv_ref, weight_ref, down_ref, up_ref, mid_ref, mask_ref, x_ref,
    gain_ref, shift_ref, resid_ref, out_ref, gd_ref, gu_ref, total, gm_sum, mid_t,
):
    step = pl.program_id(0)
    picked = pl.ds(pl.multiple_of(pick_ref[0] * RANK, RANK), RANK)

    @pl.when(step == 0)
    def _():
        total[...] = jnp.zeros_like(total)
        gm_sum[...] = jnp.zeros_like(gm_sum)
        mid_t[...] = jnp.transpose(mid_ref[...].astype(f32)).astype(bf16)

    for index, source in enumerate((dq_ref, dk_ref, dv_ref)):

        @pl.when(step == index)
        def _():
            total[...] += dot_nt(source[...], weight_ref[...])
            gm_sum[...] += dot_nn(source[...], up_ref[...])
            gu_ref[...] = (adapter_scale * dot_nn(mid_t[picked, :], source[...])).astype(bf16)

    @pl.when(step == 2)
    def _():
        middle = (adapter_scale * gm_sum[...] * mask_ref[...]).astype(bf16)
        upstream = total[...] + dot_nt(middle, down_ref[...])
        normed, inverse = normalize(x_ref[...].astype(f32))
        gain = gain_ref[...].astype(f32)
        act = (normed * gain + shift_ref[...].astype(f32)).astype(bf16)
        out_ref[...] = resid_ref[...] + norm_back(upstream * gain, normed, inverse)
        mid_t[...] = jnp.transpose(middle.astype(f32)).astype(bf16)
        gd_ref[...] = dot_nn(mid_t[picked, :], act).astype(bf16)


def unqkv_call(pick, dq, dk, dv, weight, down, up, mid, mask, x, gain, shift, resid):
    rows, features = dq.shape
    return pl.pallas_call(
        unqkv_kernel,
        name="unqkv",
        grid_spec=pltpu.PrefetchScalarGridSpec(
            num_scalar_prefetch=1,
            grid=(3,),
            in_specs=[
                whole((rows, features)),
                whole((rows, features)),
                whole((rows, features)),
                pl.BlockSpec((features, features), lambda j, s: (0, j)),
                whole((features, LANES)),
                pl.BlockSpec((features, LANES), lambda j, s: (j, 0)),
                whole((rows, LANES)),
                whole((1, LANES)),
                whole((rows, features)),
                whole((1, features)),
                whole((1, features)),
                whole((rows, features)),
            ],
            out_specs=[
                whole((rows, features)),
                whole((RANK, features)),
                pl.BlockSpec((RANK, features), lambda j, s: (0, j)),
            ],
            scratch_shapes=[
                pltpu.VMEM((rows, features), f32),
                pltpu.VMEM((rows, LANES), f32),
                pltpu.VMEM((LANES, rows), bf16),
            ],
        ),
        out_shape=[
            jax.ShapeDtypeStruct((rows, features), f32),
            jax.ShapeDtypeStruct((RANK, features), bf16),
            jax.ShapeDtypeStruct((RANK, 3 * features), bf16),
        ],
        compiler_params=params(("arbitrary",), 50),
        cost_estimate=pl.CostEstimate(
            flops=6 * rows * features * features,
            bytes_accessed=6 * features * features + 20 * rows * features,
            transcendentals=0,
        ),
    )(pick, dq, dk, dv, weight, down, up, mid, mask, x, gain, shift, resid)


def position_tables(rel_h, rel_w, length):
    wide = ((0, LANES // 2 - (2 * G - 1)), (0, LANES - HEAD_DIM))
    h = jnp.pad(rel_h, wide)
    w = jnp.pad(rel_w, wide)
    h_back = jnp.pad(rel_h[::-1], wide)
    w_back = jnp.pad(rel_w[::-1], wide)
    forward = jnp.concatenate([h_back, h_back, w_back, w_back], axis=0).T
    backward = jnp.concatenate([h, h, w, w], axis=0)
    spot = jnp.arange(length, dtype=jnp.int32)[:, None]
    lane = jnp.arange(LANES, dtype=jnp.int32)[None, :]
    at = jnp.where((lane // G) % 2 == 0, spot // G, spot % G)
    spots = (lane % G == at).astype(bf16)
    turned = (lane % G == G - 1 - at).astype(bf16)
    return forward, backward, spots, turned


def collect_kernel(lines, chunks, rows_of, count, *refs):
    sources, tokens = refs[:count], refs[count]
    targets, image = refs[count + 1 : 2 * count + 1], refs[2 * count + 1]
    local, sends, arrivals = refs[2 * count + 2 :]
    dp = lax.axis_index("dp")
    seq = lax.axis_index("seq")
    line, column, core = dp // 4, (dp // 2) % 2, dp % 2

    def device(z, x, c, y):
        return (z * 4 + x * 2 + c, y)

    def back(k):
        return lax.rem(line + lines - k, lines)

    ahead = [device(lax.rem(line + k, lines), column, core, seq) for k in range(1, lines)]
    across = device(line, 1 - column, core, seq)
    partner = device(line, column, core, 1 - seq)
    sibling = device(line, column, 1 - core, seq)
    peers = ahead + [across, partner, sibling]

    barrier = pltpu.get_barrier_semaphore()
    for peer in peers:
        pl.semaphore_signal(
            barrier, inc=1, device_id=peer, device_id_type=pl.DeviceIdType.MESH
        )
    pl.semaphore_wait(barrier, len(peers))

    outgoing = []
    used = [0]

    def block(chunk, owner, half):
        array, row, height, col, width = chunk
        by_columns = width >= 2 * LANES
        start = (owner[0] * 2 + owner[1]) * rows_of[array] + row
        if half is not None:
            if by_columns:
                cut = (width // 2 + LANES - 1) // LANES * LANES
                col, width = (col, cut) if half == 0 else (col + cut, width - cut)
            else:
                cut = (height // 2 + 7) // 8 * 8
                start, height = (start, cut) if half == 0 else (start + cut, height - cut)
        if height == 0 or width == 0:
            return None
        return targets[array].at[pl.ds(pl.multiple_of(start, 8), height), pl.ds(col, width)]

    def send(source, target, peer, slot):
        copy = pltpu.make_async_remote_copy(
            src_ref=source,
            dst_ref=target,
            send_sem=sends.at[used[0]],
            recv_sem=arrivals.at[slot],
            device_id=peer,
            device_id_type=pl.DeviceIdType.MESH,
        )
        used[0] += 1
        copy.start()
        outgoing.append(copy)

    def arrive(place, slot):
        pltpu.make_async_copy(place, place, arrivals.at[slot]).wait()

    here = (dp, seq)
    Z, X, Y, S, XD, YD, SX, SY, SD = range(9)
    per = 9 * lines

    def slot(number, kind, k):
        return number * per + kind * lines + k

    keep = []
    part_len = tokens.shape[0]
    mine = image.at[pl.ds(pl.multiple_of(seq * part_len, 8), part_len), :]
    theirs = image.at[pl.ds(pl.multiple_of((1 - seq) * part_len, 8), part_len), :]
    token_slot = len(chunks) * per
    for number, chunk in enumerate(chunks):
        array, row, height, col, width = chunk
        own = sources[array].at[pl.ds(row, height), pl.ds(col, width)]
        place = block(chunk, here, None)
        for k in range(1, lines):
            send(own, place, ahead[k - 1], slot(number, Z, k))
        send(own, place, across, slot(number, X, 0))
        send(own, place, partner, slot(number, Y, 0))
        send(own, place, sibling, slot(number, S, 0))
        copy = pltpu.make_async_copy(own, place, local.at[number])
        copy.start()
        keep.append(copy)
        if number == 0:
            send(tokens, mine, partner, token_slot)
            copy = pltpu.make_async_copy(tokens, mine, local.at[len(chunks)])
            copy.start()
            keep.append(copy)

    def stage_one(number):
        chunk = chunks[number]
        for k in range(1, lines):
            place = block(chunk, device(back(k), column, core, seq), None)
            arrive(place, slot(number, Z, k))
            send(place, place, across, slot(number, X, k))
            send(place, place, partner, slot(number, Y, k))
            send(place, place, sibling, slot(number, S, k))

    def stage_two(number):
        chunk = chunks[number]
        for k in range(lines):
            owner = device(back(k), 1 - column, core, seq)
            place = block(chunk, owner, None)
            arrive(place, slot(number, X, k))
            half = block(chunk, owner, 0)
            send(half, half, partner, slot(number, YD, k))
            send(place, place, sibling, slot(number, SX, k))
            owner = device(back(k), column, core, 1 - seq)
            place = block(chunk, owner, None)
            arrive(place, slot(number, Y, k))
            half = block(chunk, owner, 1)
            if half is not None:
                send(half, half, across, slot(number, XD, k))
            send(place, place, sibling, slot(number, SY, k))

    def stage_three(number):
        chunk = chunks[number]
        for k in range(lines):
            owner = device(back(k), 1 - column, core, 1 - seq)
            place = block(chunk, owner, None)
            arrive(block(chunk, owner, 0), slot(number, YD, k))
            half = block(chunk, owner, 1)
            if half is not None:
                arrive(half, slot(number, XD, k))
            send(place, place, sibling, slot(number, SD, k))

    def stage_four(number):
        chunk = chunks[number]
        for k in range(lines):
            for kind, x, y in (
                (S, column, seq),
                (SX, 1 - column, seq),
                (SY, column, 1 - seq),
                (SD, 1 - column, 1 - seq),
            ):
                place = block(chunk, device(back(k), x, 1 - core, y), None)
                arrive(place, slot(number, kind, k))

    stages = (stage_one, stage_two, stage_three, stage_four)
    for tick in range(len(chunks) + len(stages) - 1):
        for lag, stage in enumerate(stages):
            if 0 <= tick - lag < len(chunks):
                stage(tick - lag)
    arrive(theirs, token_slot)
    for copy in keep:
        copy.wait()
    for copy in outgoing:
        copy.wait_send()


def collect_chunks(arrays):
    chunks = []
    for index, array in enumerate(arrays):
        height, width = array.shape
        wide = width
        while height * wide * 2 > 120_000 and wide % (4 * LANES) == 0 and wide > 1280:
            wide = next(w for w in range(wide - LANES, 0, -LANES) if width % w == 0)
        tall = height
        while tall * wide * 2 > 120_000 and tall % 16 == 0:
            tall //= 2
        for row in range(0, height, tall):
            for col in range(0, width, wide):
                chunks.append((index, row, tall, col, wide))
    return chunks


def collect(mesh_shape, arrays, tokens):
    axes = ("dp", "seq")
    lines = mesh_shape["dp"] // 4
    usable = mesh_shape["seq"] == 2 and mesh_shape["dp"] == 4 * lines and 2 <= lines <= 4
    if not usable or any(a.shape[0] % 8 for a in arrays):
        gathered = [lax.all_gather(a, axes, axis=0, tiled=True) for a in arrays]
        return gathered, lax.all_gather(tokens, "seq", axis=0, tiled=True)
    devices = mesh_shape["dp"] * 2
    chunks = collect_chunks(arrays)
    anywhere = pl.BlockSpec(memory_space=pl.ANY)
    count = len(arrays)
    slots = len(chunks) * 9 * lines + 1
    out = pl.pallas_call(
        functools.partial(
            collect_kernel, lines, chunks, [a.shape[0] for a in arrays], count
        ),
        name="collect",
        in_specs=[anywhere] * (count + 1),
        out_specs=[anywhere] * (count + 1),
        out_shape=[
            jax.ShapeDtypeStruct((devices * a.shape[0], a.shape[1]), a.dtype) for a in arrays
        ]
        + [jax.ShapeDtypeStruct((2 * tokens.shape[0], tokens.shape[1]), tokens.dtype)],
        scratch_shapes=[
            pltpu.SemaphoreType.DMA((len(chunks) + 1,)),
            pltpu.SemaphoreType.DMA((slots,)),
            pltpu.SemaphoreType.DMA((slots,)),
        ],
        compiler_params=pltpu.CompilerParams(collective_id=1, has_side_effects=True),
    )(*arrays, tokens)
    return list(out[:count]), out[count]


def gather_rows(arrays, axes):
    return [lax.all_gather(a, axes, axis=0, tiled=True) for a in arrays]


def per_device(
    mesh_shape,
    tokens,
    adapter_index,
    norm1_gain,
    norm1_bias,
    qkv_weight,
    qkv_bias,
    proj_weight,
    proj_bias,
    norm2_gain,
    norm2_bias,
    fc1_weight,
    fc1_bias,
    fc2_weight,
    fc2_bias,
    rel_pos_h,
    rel_pos_w,
    qkv_down,
    qkv_up,
    proj_down,
    proj_up,
    fc1_down,
    fc1_up,
    fc2_down,
    fc2_up,
    out_grad,
):
    axes = ("dp", "seq")
    part_count = mesh_shape["seq"]
    devices = mesh_shape["dp"] * part_count
    images, part_len, features = tokens.shape
    length = part_len * part_count
    own_tokens = tokens[0]
    og = out_grad[0]
    place = lax.axis_index("seq").astype(jnp.int32).reshape(1)
    pick = adapter_index

    small = [
        norm1_gain, norm1_bias, qkv_bias, proj_bias, norm2_gain, norm2_bias, fc1_bias, fc2_bias,
        adapter_index.astype(bf16),
    ]
    small_sizes = [a.shape[0] for a in small]
    pack_small = jnp.concatenate(small)
    pack_small = jnp.pad(pack_small, (0, 8 * LANES - pack_small.shape[0])).reshape(8, LANES)
    adapters = [qkv_down, proj_down, fc1_down, fc2_down, qkv_up.T, proj_up.T, fc1_up.T, fc2_up.T]
    widths = [a.shape[0] for a in adapters]
    pack_adapters = jnp.concatenate(adapters, axis=0)

    w_fc1, w_fc2 = gather_rows([fc1_weight, fc2_weight], axes)
    (w_qkv, w_proj, all_adapters, all_small), image_tokens = collect(
        mesh_shape, [qkv_weight, proj_weight, pack_adapters, pack_small], own_tokens
    )

    all_small = all_small.reshape(devices, 8 * LANES)
    vectors, at = [], 0
    for size in small_sizes:
        vectors.append(all_small[:, at : at + size].reshape(1, devices * size))
        at += size
    g1, s1, b_qkv, b_proj, g2, s2, b_fc1, b_fc2, picks = vectors
    all_adapters = all_adapters.reshape(devices, sum(widths), LANES)
    maps, at = [], 0
    for size in widths:
        maps.append(all_adapters[:, at : at + size].reshape(devices * size, LANES))
        at += size
    d_qkv, d_proj, d_fc1, d_fc2, u_qkv, u_proj, u_fc1, u_fc2 = maps

    columns = jnp.arange(LANES, dtype=jnp.int32) // RANK
    mask = (columns[None, :] == adapter_index[:, None]).astype(f32)
    forward_table, back_table, spots, turned_spots = position_tables(rel_pos_h, rel_pos_w, length)
    head_of = jnp.arange(features, dtype=jnp.int32)[None, :] // HEAD_DIM
    head_sums = (head_of == jnp.arange(HEADS, dtype=jnp.int32)[:, None]).astype(bf16)

    heads, mid_qkv = qkv_call(image_tokens, g1, s1, w_qkv, b_qkv, d_qkv, u_qkv, mask)
    att, lse, aux = forward_call(place, heads, forward_table, spots, part_len)
    resid, act_two, mid_proj, mid_fc1 = project_call(
        att, own_tokens, w_proj, b_proj, d_proj, u_proj, mask, g2, s2, d_fc1
    )
    block_out, grad_resid, grad_branch, gd_fc1, gu_fc1, gd_fc2, gu_fc2 = feed_call(
        pick, act_two, resid, og, w_fc1, b_fc1, w_fc2, b_fc2, d_fc1, u_fc1, d_fc2, u_fc2,
        mid_fc1, mask, g2,
    )
    grad_att, inner, gd_proj, gu_proj = unproject_call(
        pick, grad_branch, att, w_proj, d_proj, u_proj, mid_proj, mask, head_sums
    )
    if part_count == 2:
        swap = [(0, 1), (1, 0)]
        their_grad, their_lse, their_inner = (
            lax.ppermute(a, "seq", swap)[None] for a in (grad_att, lse, inner)
        )
    else:
        their_grad, their_lse, their_inner = (
            lax.all_gather(a, "seq", axis=0) for a in (grad_att, lse, inner)
        )
    dq, dk_own, dv_own = own_call(
        place, heads, aux, spots, turned_spots, back_table, grad_att, lse, inner
    )
    dk, dv = other_call(
        place, heads, aux, spots, their_grad, their_lse, their_inner, dk_own, dv_own
    )
    mid_own = lax.dynamic_slice_in_dim(mid_qkv, place[0] * part_len, part_len, 0)
    input_grad, gd_qkv, gu_qkv = unqkv_call(
        pick, dq, dk, dv, w_qkv, d_qkv, u_qkv, mid_own, mask, own_tokens, g1, s1, grad_resid
    )

    terms = [gd_qkv, gd_proj, gd_fc1, gd_fc2, gu_qkv, gu_proj, gu_fc1, gu_fc2]
    sent = jnp.concatenate([t.reshape(RANK, devices, -1) for t in terms], axis=2)
    sent = jnp.transpose(sent, (1, 0, 2))
    received = lax.all_to_all(sent, axes, 0, 0, tiled=True)
    source = picks.reshape(mesh_shape["dp"], part_count)[:, :1]
    source = jnp.broadcast_to(source, (mesh_shape["dp"], part_count)).reshape(1, devices)
    chosen = (jnp.arange(ADAPTERS, dtype=jnp.int32)[:, None] == source.astype(jnp.int32)).astype(
        bf16
    )
    summed = jnp.einsum("ad,drc->arc", chosen, received, preferred_element_type=f32)
    summed = summed.reshape(ADAPTERS * RANK, -1)
    pieces, at = [], 0
    for size in widths:
        pieces.append(summed[:, at : at + size])
        at += size
    return (
        block_out[None],
        input_grad[None],
        pieces[0].T,
        pieces[4],
        pieces[1].T,
        pieces[5],
        pieces[2].T,
        pieces[6],
        pieces[3].T,
        pieces[7],
    )


def solution(mesh):
    both = ("dp", "seq")
    return jax.shard_map(
        functools.partial(per_device, dict(mesh.shape)),
        mesh=mesh,
        in_specs=(
            P("dp", "seq", None),
            P("dp"),
            P(both),
            P(both),
            P(both, None),
            P(both),
            P(both, None),
            P(both),
            P(both),
            P(both),
            P(both, None),
            P(both),
            P(both, None),
            P(both),
            P(),
            P(),
            P(both, None),
            P(None, both),
            P(both, None),
            P(None, both),
            P(both, None),
            P(None, both),
            P(both, None),
            P(None, both),
            P("dp", "seq", None),
        ),
        out_specs=(
            P("dp", "seq", None),
            P("dp", "seq", None),
            P(both, None),
            P(None, both),
            P(both, None),
            P(None, both),
            P(both, None),
            P(None, both),
            P(both, None),
            P(None, both),
        ),
        check_vma=False,
    )
```

```python
import functools

import jax
import jax.numpy as jnp
import numpy as np
from jax import lax
from jax.experimental import pallas as pl
from jax.experimental.pallas import tpu as pltpu
from jax.sharding import PartitionSpec as P

HEADS = 16
HEAD_DIM = 80
ADAPTERS = 8
RANK = 16
G = 32
LANES = 128
VECTORS = 8
HALF = HEADS // 2

epsilon = 1e-06
adapter_scale = 0.5
log2e = 1.4426950408889634
score_scale = HEAD_DIM ** (-0.5)
exponent_scale = score_scale * log2e
f32 = jnp.float32
bf16 = jnp.bfloat16


def dot_nn(left, right):
    return lax.dot_general(left, right, (((1,), (0,)), ((), ())), preferred_element_type=f32)


def dot_nt(left, right):
    return lax.dot_general(left, right, (((1,), (1,)), ((), ())), preferred_element_type=f32)


def dot_tn(left, right):
    return lax.dot_general(left, right, (((0,), (0,)), ((), ())), preferred_element_type=f32)


def normalize(values):
    average = jnp.mean(values, axis=-1, keepdims=True)
    centered = values - average
    variance = jnp.mean(centered * centered, axis=-1, keepdims=True)
    inverse = lax.rsqrt(variance + epsilon)
    return centered * inverse, inverse


def norm_back(scaled, normed, inverse):
    return inverse * (
        scaled
        - jnp.mean(scaled, axis=-1, keepdims=True)
        - normed * jnp.mean(scaled * normed, axis=-1, keepdims=True)
    )


def chosen_rows(mask, middle):
    rank = lax.broadcasted_iota(jnp.int32, (RANK, LANES), 0)
    column = lax.broadcasted_iota(jnp.int32, (RANK, LANES), 1)
    pick = jnp.where(column % RANK == rank, jnp.broadcast_to(mask, (RANK, LANES)), 0.0)
    return dot_nt(pick.astype(bf16), middle).astype(bf16)


def params(semantics, megabytes):
    return pltpu.CompilerParams(
        dimension_semantics=semantics, vmem_limit_bytes=megabytes * 1024 * 1024
    )


def whole(shape):
    zeros = (0,) * len(shape)
    return pl.BlockSpec(shape, lambda *_: zeros)


Z, X, Y, S, XD, YD, SX, SY, SD = range(9)


class Courier:
    def __init__(self, lines, chunks, rows_of, sources, targets, local, sends, arrivals):
        self.lines = lines
        self.chunks = chunks
        self.rows_of = rows_of
        self.sources, self.targets = sources, targets
        self.local, self.sends, self.arrivals = local, sends, arrivals
        dp = lax.axis_index("dp")
        self.seq = lax.axis_index("seq")
        self.dp = dp
        self.line, self.column, self.core = dp // 4, (dp // 2) % 2, dp % 2
        line, column, core, seq = self.line, self.column, self.core, self.seq
        self.ahead = [
            self.device(lax.rem(line + k, lines), column, core, seq) for k in range(1, lines)
        ]
        self.across = self.device(line, 1 - column, core, seq)
        self.partner = self.device(line, column, core, 1 - seq)
        self.sibling = self.device(line, column, 1 - core, seq)

    @staticmethod
    def device(z, x, c, y):
        return (z * 4 + x * 2 + c, y)

    def owner(self, k, x, c, y):
        return self.device(lax.rem(self.line + self.lines - k, self.lines), x, c, y)

    def greet(self):
        peers = self.ahead + [self.across, self.partner, self.sibling]
        barrier = pltpu.get_barrier_semaphore()
        for peer in peers:
            pl.semaphore_signal(
                barrier, inc=1, device_id=peer, device_id_type=pl.DeviceIdType.MESH
            )
        pl.semaphore_wait(barrier, len(peers))

    def slot(self, number, kind, k):
        return (number * 9 + kind) * self.lines + k

    def part(self, number, half):
        _, row, height, col, width, share = self.chunks[number]
        if half is None:
            return row, height, col, width
        if width >= 2 * LANES:
            cut = width // LANES * share // 4 * LANES
            return (row, height, col, cut) if half == 0 else (row, height, col + cut, width - cut)
        cut = height // 8 * share // 4 * 8
        return (row, cut, col, width) if half == 0 else (row + cut, height - cut, col, width)

    def place(self, number, owner, half=None):
        array = self.chunks[number][0]
        row, height, col, width = self.part(number, half)
        if height == 0 or width == 0:
            return None
        start = (owner[0] * 2 + owner[1]) * self.rows_of[array] + row
        return self.targets[array].at[pl.ds(pl.multiple_of(start, 8), height), pl.ds(col, width)]

    def like(self, number, half=None):
        array = self.chunks[number][0]
        row, height, col, width = self.part(number, half)
        if height == 0 or width == 0:
            return None
        return self.targets[array].at[pl.ds(row, height), pl.ds(col, width)]

    def send(self, source, target, peer, number, kind, k):
        at = self.slot(number, kind, k)
        pltpu.make_async_remote_copy(
            src_ref=source,
            dst_ref=target,
            send_sem=self.sends.at[at],
            recv_sem=self.arrivals.at[at],
            device_id=peer,
            device_id_type=pl.DeviceIdType.MESH,
        ).start()

    def arrive(self, place, number, kind, k):
        pltpu.make_async_copy(place, place, self.arrivals.at[self.slot(number, kind, k)]).wait()

    def start(self, number):
        array, row, height, col, width, _ = self.chunks[number]
        own = self.sources[array].at[pl.ds(row, height), pl.ds(col, width)]
        place = self.place(number, (self.dp, self.seq))
        for k in range(1, self.lines):
            self.send(own, place, self.ahead[k - 1], number, Z, k)
        self.send(own, place, self.across, number, X, 0)
        self.send(own, place, self.partner, number, Y, 0)
        self.send(own, place, self.sibling, number, S, 0)
        pltpu.make_async_copy(own, place, self.local.at[number]).start()

    def stage_one(self, number, k):
        place = self.place(number, self.owner(k, self.column, self.core, self.seq))
        self.arrive(place, number, Z, k)
        self.send(place, place, self.across, number, X, k)
        self.send(place, place, self.partner, number, Y, k)
        self.send(place, place, self.sibling, number, S, k)

    def stage_two(self, number, k):
        owner = self.owner(k, 1 - self.column, self.core, self.seq)
        place = self.place(number, owner)
        self.arrive(place, number, X, k)
        half = self.place(number, owner, 0)
        if half is not None:
            self.send(half, half, self.partner, number, YD, k)
        self.send(place, place, self.sibling, number, SX, k)
        owner = self.owner(k, self.column, self.core, 1 - self.seq)
        place = self.place(number, owner)
        self.arrive(place, number, Y, k)
        half = self.place(number, owner, 1)
        if half is not None:
            self.send(half, half, self.across, number, XD, k)
        self.send(place, place, self.sibling, number, SY, k)

    def stage_three(self, number, k):
        owner = self.owner(k, 1 - self.column, self.core, 1 - self.seq)
        for half, kind in ((0, YD), (1, XD)):
            piece = self.place(number, owner, half)
            if piece is not None:
                self.arrive(piece, number, kind, k)
        place = self.place(number, owner)
        self.send(place, place, self.sibling, number, SD, k)

    def stage_four(self, number, k):
        for kind, x, y in (
            (S, self.column, self.seq),
            (SX, 1 - self.column, self.seq),
            (SY, self.column, 1 - self.seq),
            (SD, 1 - self.column, 1 - self.seq),
        ):
            place = self.place(number, self.owner(k, x, 1 - self.core, y))
            self.arrive(place, number, kind, k)

    def steps(self):
        stages = (self.stage_one, self.stage_two, self.stage_three, self.stage_four)
        order = []
        for tick in range(len(self.chunks) + 3):
            for lag, stage in enumerate(stages):
                if 0 <= tick - lag < len(self.chunks):
                    for k in range(1 if lag == 0 else 0, self.lines):
                        order.append(functools.partial(stage, tick - lag, k))
        return order

    def finish(self):
        for number in range(len(self.chunks)):
            like = self.like(number)
            pltpu.make_async_copy(like, like, self.local.at[number]).wait()
            for kind in range(9):
                half = {YD: 0, XD: 1}.get(kind)
                like = self.like(number, half)
                for k in range(self.lines):
                    if like is not None and not (kind == Z and k == 0):
                        sem = self.sends.at[self.slot(number, kind, k)]
                        pltpu.make_async_copy(like, like, sem).wait()


def cut_chunks(arrays, share=2):
    chunks = []
    for index, array in enumerate(arrays):
        height, width = array.shape
        wide, tall = width, height
        if height * wide * 2 > 120_000 and wide > 1280:
            wide = next(w for w in range(1280, 0, -LANES) if width % w == 0)
        while tall * wide * 2 > 120_000 and tall % 16 == 0:
            tall //= 2
        for row in range(0, height, tall):
            for col in range(0, width, wide):
                chunks.append((index, row, tall, col, wide, share))
    return chunks


def courier_lines(mesh_shape, arrays):
    lines = mesh_shape["dp"] // 4
    fits = mesh_shape["seq"] == 2 and mesh_shape["dp"] == 4 * lines and 2 <= lines <= 4
    return lines if fits and not any(a.shape[0] % 8 for a in arrays) else None


def courier_scratch(lines, chunks):
    slots = len(chunks) * 9 * lines
    return [
        pltpu.SemaphoreType.DMA((len(chunks),)),
        pltpu.SemaphoreType.DMA((slots,)),
        pltpu.SemaphoreType.DMA((slots,)),
    ]


def gathered_shapes(devices, arrays):
    return [jax.ShapeDtypeStruct((devices * a.shape[0], a.shape[1]), a.dtype) for a in arrays]


def collect_kernel(lines, chunks, rows_of, count, *refs):
    sources, tokens = refs[:count], refs[count]
    targets, other = refs[count + 1 : 2 * count + 1], refs[2 * count + 1]
    local, sends, arrivals, token_sem = refs[2 * count + 2 :]
    courier = Courier(lines, chunks, rows_of, sources, targets, local, sends, arrivals)
    courier.greet()
    passed = pltpu.make_async_remote_copy(
        src_ref=tokens,
        dst_ref=other,
        send_sem=token_sem.at[0],
        recv_sem=token_sem.at[1],
        device_id=courier.partner,
        device_id_type=pl.DeviceIdType.MESH,
    )
    for number in range(len(chunks)):
        courier.start(number)
    passed.start()
    for step in courier.steps():
        step()
    passed.wait()
    courier.finish()


def collect(mesh_shape, arrays, tokens):
    axes = ("dp", "seq")
    lines = courier_lines(mesh_shape, arrays)
    if lines is None:
        gathered = [lax.all_gather(a, axes, axis=0, tiled=True) for a in arrays]
        return gathered, [lax.all_gather(tokens, "seq", axis=0, tiled=True)]
    chunks = cut_chunks(arrays, 1)
    anywhere = pl.BlockSpec(memory_space=pl.ANY)
    count = len(arrays)
    out = pl.pallas_call(
        functools.partial(collect_kernel, lines, chunks, [a.shape[0] for a in arrays], count),
        name="collect",
        in_specs=[anywhere] * (count + 1),
        out_specs=[anywhere] * (count + 1),
        out_shape=gathered_shapes(mesh_shape["dp"] * 2, arrays)
        + [jax.ShapeDtypeStruct(tokens.shape, tokens.dtype)],
        scratch_shapes=courier_scratch(lines, chunks) + [pltpu.SemaphoreType.DMA((2,))],
        compiler_params=pltpu.CompilerParams(collective_id=1, has_side_effects=True),
    )(*arrays, tokens)
    return list(out[:count]), [tokens, out[count]]


def qkv_part(part, blocks, gain_ref, shift_ref, weight_ref, bias_ref, down_ref, up_ref, mask_ref,
             heads, mid_ref, act_ref, pause):
    length = act_ref.shape[0]

    @pl.when(part == 0)
    def _():
        part_len = length // len(blocks)
        for index, block in enumerate(blocks):
            place = 0
            if len(blocks) == 2:
                seq = lax.axis_index("seq")
                place = pl.multiple_of((seq if index == 0 else 1 - seq) * part_len, G)
            normed, _ = normalize(block[...].astype(f32))
            act = normed * gain_ref[...].astype(f32) + shift_ref[...].astype(f32)
            act_ref[pl.ds(place, part_len), :] = act.astype(bf16)
        mid_ref[...] = (dot_nn(act_ref[...], down_ref[...]) * mask_ref[...]).astype(bf16)

    rows = min(256, length)
    lane = lax.broadcasted_iota(jnp.int32, (rows, LANES - HEAD_DIM), 1)
    pad = jnp.where((lane == 0) & (part == 2), 1.0, 0.0).astype(bf16)
    for start in range(0, length, rows):
        here = pl.ds(start, rows)
        block = dot_nn(act_ref[here, :], weight_ref[...])
        block = block + bias_ref[...].astype(f32)
        block = block + adapter_scale * dot_nt(mid_ref[here, :], up_ref[...])
        block = block.astype(bf16)
        for head in range(HEADS):
            heads[part, head, here, 0:HEAD_DIM] = block[:, head * HEAD_DIM : (head + 1) * HEAD_DIM]
            heads[part, head, here, HEAD_DIM:LANES] = pad
        pause(start // rows)


def attend_head(head, own, heads, table_ref, spots_ref, att_ref, lse_ref, aux_ref, pause):
    pause(0)
    length = heads.shape[2]
    part_len = att_ref.shape[0]
    lane = lax.broadcasted_iota(jnp.int32, (G, LANES), 1)
    first = lane < LANES // 2
    even = (lane // G) % 2 == 0
    raw = dot_nn(heads[0, head], table_ref[...]) * (HEAD_DIM**0.5)
    for row in range(length // G):
        block = raw[row * G : (row + 1) * G, :]
        high = block.astype(bf16).astype(f32)
        mixed_h = jnp.where(first, high[:, :LANES], block[:, :LANES] - high[:, :LANES])
        mixed_w = jnp.where(first, high[:, LANES:], block[:, LANES:] - high[:, LANES:])
        along_h = pltpu.roll(mixed_h, LANES - G + 1 + row, 1)
        along_w = pltpu.roll(mixed_w, 1, 1, stride=1, stride_axis=0)
        aux_ref[0, pl.ds(row * G, G), :] = jnp.where(even, along_h, along_w).astype(bf16)
    pause(1)
    left = jnp.concatenate([heads[0, head, own, :], aux_ref[0, own, :]], axis=1)
    right = jnp.concatenate([heads[1, head], spots_ref[...]], axis=1)
    scores = dot_nt(left, right)
    top = jnp.max(scores, axis=1, keepdims=True)
    shares = jnp.exp2((scores - top) * exponent_scale).astype(bf16)
    mixed = dot_nn(shares, heads[2, head])
    total = mixed[:, HEAD_DIM : HEAD_DIM + 1]
    att = (mixed[:, :HEAD_DIM] / total).astype(bf16)
    logs = top * exponent_scale + jnp.log2(total)
    lse_ref[0] = jnp.transpose(jnp.broadcast_to(logs, (part_len, LANES)))[0:1, :]
    for slot in range(HALF):

        @pl.when(head % HALF == slot)
        def _():
            att_ref[:, slot * HEAD_DIM : (slot + 1) * HEAD_DIM] = att


def front_kernel(
    lines, chunks, rows_of, count, pair,
    gain_ref, shift_ref, weight_ref, bias_ref, down_ref, up_ref, mask_ref, table_ref,
    spots_ref, *refs,
):
    blocks, refs = refs[:pair], refs[pair:]
    sources = refs[:count]
    heads_out, mid_ref, att_ref, lse_ref, aux_ref = refs[count : count + 5]
    targets = refs[count + 5 : 2 * count + 5]
    heads, act_ref, out_sem = refs[2 * count + 5 : 2 * count + 8]
    step = pl.program_id(0)
    last = pl.num_programs(0) - 1
    courier = None
    plan = {}
    if count:
        courier = Courier(lines, chunks, rows_of, sources, targets, *refs[2 * count + 8 :])

        @pl.when(step == 0)
        def _():
            courier.greet()
            for number in range(len(chunks)):
                courier.start(number)

        pieces = act_ref.shape[0] // min(256, act_ref.shape[0])
        places = [(part, piece, 7.0 / pieces) for part in range(3) for piece in range(pieces)]
        places += [(3 + head, piece, 1.0) for head in range(HEADS) for piece in range(2)]
        work = courier.steps()
        whole_time = sum(p[2] for p in places)
        done, spent = 0, 0.0
        for at, piece, time in places:
            spent += time
            upto = min(len(work), int(len(work) * spent / whole_time + 1e-6))
            plan[at, piece] = work[done:upto]
            done = upto

    def pause(first, count_of):
        def run(piece):
            for at in range(first, first + count_of):
                items = plan.get((at, piece))
                if items:

                    @pl.when(step == at)
                    def _():
                        for item in items:
                            item()

        return run

    @pl.when(step < 3)
    def _():
        qkv_part(
            step, blocks, gain_ref, shift_ref, weight_ref, bias_ref, down_ref, up_ref, mask_ref,
            heads, mid_ref, act_ref, pause(0, 3),
        )
        pltpu.make_async_copy(heads.at[step], heads_out.at[step], out_sem.at[step]).start()

    part_len = att_ref.shape[0]
    own = pl.ds(pl.multiple_of(lax.axis_index("seq") * part_len, G), part_len)

    @pl.when(step >= 3)
    def _():
        attend_head(
            step - 3, own, heads, table_ref, spots_ref, att_ref, lse_ref, aux_ref, pause(3, HEADS)
        )

    @pl.when(step == last)
    def _():
        for part in range(3):
            pltpu.make_async_copy(heads.at[part], heads_out.at[part], out_sem.at[part]).wait()
        if courier is not None:
            courier.finish()


def front_call(
    mesh_shape, part_len, tokens, gain, shift, weight, bias, down, up, mask, table, spots, arrays
):
    length = sum(t.shape[0] for t in tokens)
    features = weight.shape[0]
    lines = courier_lines(mesh_shape, arrays)
    later = []
    if lines is None:
        axes = ("dp", "seq")
        later = [lax.all_gather(a, axes, axis=0, tiled=True) for a in arrays]
        arrays = []
    chunks = cut_chunks(arrays)
    count = len(arrays)
    anywhere = pl.BlockSpec(memory_space=pl.ANY)

    def head(i):
        return jnp.maximum(i - 3, 0)

    def part(i):
        return jnp.minimum(i, 2)

    def fixed(shape):
        zeros = (0,) * len(shape)
        return pl.BlockSpec(shape, lambda i: zeros, pipeline_mode=pl.Buffered(1))

    options = dict(collective_id=2, has_side_effects=True) if count else {}
    out = pl.pallas_call(
        functools.partial(
            front_kernel, lines, chunks, [a.shape[0] for a in arrays], count, len(tokens)
        ),
        name="front",
        grid=(3 + HEADS,),
        in_specs=[
            fixed((1, features)),
            fixed((1, features)),
            pl.BlockSpec((features, features), lambda i: (0, part(i))),
            pl.BlockSpec((1, features), lambda i: (0, part(i))),
            fixed((features, LANES)),
            pl.BlockSpec((features, LANES), lambda i: (part(i), 0)),
            fixed((1, LANES)),
            fixed((LANES, 2 * LANES)),
            fixed((length, LANES)),
        ]
        + [fixed(t.shape) for t in tokens]
        + [anywhere] * count,
        out_specs=[
            anywhere,
            whole((length, LANES)),
            pl.BlockSpec((part_len, features // 2), lambda i: (0, head(i) // HALF)),
            pl.BlockSpec((1, 1, part_len), lambda i: (head(i), 0, 0)),
            pl.BlockSpec((1, length, LANES), lambda i: (head(i), 0, 0)),
        ]
        + [anywhere] * count,
        out_shape=[
            jax.ShapeDtypeStruct((3, HEADS, length, LANES), bf16),
            jax.ShapeDtypeStruct((length, LANES), bf16),
            jax.ShapeDtypeStruct((part_len, features), bf16),
            jax.ShapeDtypeStruct((HEADS, 1, part_len), f32),
            jax.ShapeDtypeStruct((HEADS, length, LANES), bf16),
        ]
        + gathered_shapes(mesh_shape["dp"] * mesh_shape["seq"], arrays),
        scratch_shapes=[
            pltpu.VMEM((3, HEADS, length, LANES), bf16),
            pltpu.VMEM((length, features), bf16),
            pltpu.SemaphoreType.DMA((3,)),
        ]
        + (courier_scratch(lines, chunks) if count else []),
        compiler_params=pltpu.CompilerParams(
            dimension_semantics=("arbitrary",), vmem_limit_bytes=58 * 1024 * 1024, **options
        ),
        cost_estimate=pl.CostEstimate(
            flops=6 * length * features * features
            + 8 * HEADS * part_len * length * LANES,
            bytes_accessed=2 * (3 * features * features + 8 * length * features),
            transcendentals=HEADS * part_len * length,
        ),
    )(gain, shift, weight, bias, down, up, mask, table, spots, *tokens, *arrays)
    return out[:5], list(out[5:]) + later


def head_lanes(source, head, padded):
    padded[:, HEAD_DIM:LANES] = jnp.zeros((padded.shape[0], LANES - HEAD_DIM), bf16)
    for slot in range(HALF):

        @pl.when(head % HALF == slot)
        def _():
            padded[:, 0:HEAD_DIM] = source[:, slot * HEAD_DIM : (slot + 1) * HEAD_DIM]


def own_kernel(
    place_ref, q_ref, aux_ref, k_ref, v_ref, spots_ref, turned_spots_ref, table_ref, grad_ref,
    lse_ref, inner_ref, dq_ref, dk_ref, dv_ref, shares_ref, dscores_ref, padded,
):
    head = pl.program_id(0)
    part_len = q_ref.shape[2]
    head_lanes(grad_ref, head, padded)
    queries = q_ref[0, 0]
    keys = k_ref[0, 0]
    left = jnp.concatenate([keys, spots_ref[...]], axis=1)
    right = jnp.concatenate([queries, aux_ref[0]], axis=1)
    shares = jnp.exp2(dot_nt(left, right) * exponent_scale - lse_ref[0])
    grad_shares = dot_nt(v_ref[0, 0], padded[...])
    shares_ref[...] = shares.astype(bf16)
    dscores_ref[...] = (shares * (grad_shares - inner_ref[0])).astype(bf16)
    flat = dot_tn(jnp.concatenate([keys, turned_spots_ref[...]], axis=1), dscores_ref[...])
    turned = jnp.transpose(flat)
    lane = lax.broadcasted_iota(jnp.int32, (G, LANES), 1)
    first = lane < LANES // 2
    even = (lane // G) % 2 == 0
    start = place_ref[0] * (part_len // G)
    pieces_h, pieces_w = [], []
    for row in range(part_len // G):
        sums = turned[row * G : (row + 1) * G, LANES:]
        high = sums.astype(bf16).astype(f32)
        mixed = jnp.where(first, high, sums - high)
        pieces_h.append(pltpu.roll(jnp.where(even, mixed, 0.0), start + row, 1))
        pieces_w.append(
            pltpu.roll(jnp.where(even, 0.0, mixed), LANES - G, 1, stride=1, stride_axis=0)
        )
    spread = jnp.concatenate(
        [jnp.concatenate(pieces_h, axis=0), jnp.concatenate(pieces_w, axis=0)], axis=1
    ).astype(bf16)
    grad_query = turned[:, :LANES] * score_scale + dot_nn(spread, table_ref[...])
    grad_query = grad_query[:, :HEAD_DIM].astype(bf16)
    for slot in range(HALF):

        @pl.when(head % HALF == slot)
        def _():
            dq_ref[:, slot * HEAD_DIM : (slot + 1) * HEAD_DIM] = grad_query

    here = pl.ds(pl.multiple_of(place_ref[0] * part_len, G), part_len)
    dk_ref[0] = dot_nn(dscores_ref[here, :], queries)
    dv_ref[0] = dot_nn(shares_ref[here, :], padded[...])


def own_call(place, heads, aux, spots, turned_spots, table, grad, lse, inner):
    length = heads.shape[2]
    part_len, features = grad.shape

    def part(index):
        return pl.BlockSpec((1, 1, length, LANES), lambda n, s: (index, n, 0, 0))

    return pl.pallas_call(
        own_kernel,
        name="back_own",
        grid_spec=pltpu.PrefetchScalarGridSpec(
            num_scalar_prefetch=1,
            grid=(HEADS,),
            in_specs=[
                pl.BlockSpec((1, 1, part_len, LANES), lambda n, s: (0, n, s[0], 0)),
                pl.BlockSpec((1, part_len, LANES), lambda n, s: (n, s[0], 0)),
                part(1),
                part(2),
                whole((length, LANES)),
                whole((length, LANES)),
                whole((2 * LANES, LANES)),
                pl.BlockSpec((part_len, features // 2), lambda n, s: (0, n // HALF)),
                pl.BlockSpec((1, 1, part_len), lambda n, s: (n, 0, 0)),
                pl.BlockSpec((1, 1, part_len), lambda n, s: (n, 0, 0)),
            ],
            out_specs=[
                pl.BlockSpec((part_len, features // 2), lambda n, s: (0, n // HALF)),
                pl.BlockSpec((1, part_len, LANES), lambda n, s: (n, 0, 0)),
                pl.BlockSpec((1, part_len, LANES), lambda n, s: (n, 0, 0)),
            ],
            scratch_shapes=[
                pltpu.VMEM((length, part_len), bf16),
                pltpu.VMEM((length, part_len), bf16),
                pltpu.VMEM((part_len, LANES), bf16),
            ],
        ),
        out_shape=[
            jax.ShapeDtypeStruct((part_len, features), bf16),
            jax.ShapeDtypeStruct((HEADS, part_len, LANES), f32),
            jax.ShapeDtypeStruct((HEADS, part_len, LANES), f32),
        ],
        compiler_params=params(("arbitrary",), 40),
        cost_estimate=pl.CostEstimate(
            flops=8 * HEADS * part_len * length * LANES * 2,
            bytes_accessed=12 * HEADS * length * LANES,
            transcendentals=HEADS * part_len * length,
        ),
    )(place, heads, aux, heads, heads, spots, turned_spots, table, grad, lse, inner)


def other_kernel(
    place_ref, q_ref, aux_ref, k_ref, v_ref, spots_ref, grad_ref, lse_ref, inner_ref, dk_in, dv_in,
    dk_ref, dv_ref, dk_sum, dv_sum, padded,
):
    head = pl.program_id(0)
    step = pl.program_id(1)
    head_lanes(grad_ref.at[0], head, padded)
    queries = q_ref[0, 0]
    left = jnp.concatenate([k_ref[0, 0], spots_ref[...]], axis=1)
    right = jnp.concatenate([queries, aux_ref[0]], axis=1)
    shares = jnp.exp2(dot_nt(left, right) * exponent_scale - lse_ref[0, 0])
    grad_shares = dot_nt(v_ref[0, 0], padded[...])
    dscores = (shares * (grad_shares - inner_ref[0, 0])).astype(bf16)

    @pl.when(step == 0)
    def _():
        dk_sum[...] = dk_in[0]
        dv_sum[...] = dv_in[0]

    dk_sum[...] += dot_nn(dscores, queries)
    dv_sum[...] += dot_nn(shares.astype(bf16), padded[...])

    @pl.when(step == pl.num_programs(1) - 1)
    def _():
        grad_key = (dk_sum[:, :HEAD_DIM] * score_scale).astype(bf16)
        grad_value = dv_sum[:, :HEAD_DIM].astype(bf16)
        for slot in range(HALF):

            @pl.when(head % HALF == slot)
            def _():
                dk_ref[:, slot * HEAD_DIM : (slot + 1) * HEAD_DIM] = grad_key
                dv_ref[:, slot * HEAD_DIM : (slot + 1) * HEAD_DIM] = grad_value


def other_call(place, heads, aux, spots, grads, lses, inners, dk, dv):
    length = heads.shape[2]
    blocks, part_len, features = grads.shape
    count = length // part_len

    def theirs(i, s):
        return lax.rem(s[0] + 1 + i, count)

    def given(i, s):
        return theirs(i, s) if blocks > 1 else 0

    def own(index):
        return pl.BlockSpec((1, 1, part_len, LANES), lambda n, i, s: (index, n, s[0], 0))

    stats = pl.BlockSpec((1, 1, 1, part_len), lambda n, i, s: (given(i, s), n, 0, 0))
    sums = pl.BlockSpec((1, part_len, LANES), lambda n, i, s: (n, 0, 0))
    dense = pl.BlockSpec((part_len, features // 2), lambda n, i, s: (0, n // HALF))
    return pl.pallas_call(
        other_kernel,
        name="back_other",
        grid_spec=pltpu.PrefetchScalarGridSpec(
            num_scalar_prefetch=1,
            grid=(HEADS, count - 1),
            in_specs=[
                pl.BlockSpec((1, 1, part_len, LANES), lambda n, i, s: (0, n, theirs(i, s), 0)),
                pl.BlockSpec((1, part_len, LANES), lambda n, i, s: (n, theirs(i, s), 0)),
                own(1),
                own(2),
                pl.BlockSpec((part_len, LANES), lambda n, i, s: (s[0], 0)),
                pl.BlockSpec(
                    (1, part_len, features // 2), lambda n, i, s: (given(i, s), 0, n // HALF)
                ),
                stats,
                stats,
                sums,
                sums,
            ],
            out_specs=[dense, dense],
            scratch_shapes=[
                pltpu.VMEM((part_len, LANES), f32),
                pltpu.VMEM((part_len, LANES), f32),
                pltpu.VMEM((part_len, LANES), bf16),
            ],
        ),
        out_shape=[
            jax.ShapeDtypeStruct((part_len, features), bf16),
            jax.ShapeDtypeStruct((part_len, features), bf16),
        ],
        compiler_params=params(("arbitrary", "arbitrary"), 40),
        cost_estimate=pl.CostEstimate(
            flops=4 * HEADS * part_len * (length - part_len) * LANES * 2,
            bytes_accessed=12 * HEADS * length * LANES,
            transcendentals=HEADS * part_len * (length - part_len),
        ),
    )(place, heads, aux, heads, heads, spots, grads, lses, inners, dk, dv)


def gelu_parts(hidden):
    size = jnp.abs(hidden) * (0.5**0.5)
    bell = jnp.exp2(hidden * hidden * (-0.5 * log2e))
    t = 1.0 / (1.0 + 0.3275911 * size)
    poly = t * (
        0.254829592
        + t * (-0.284496736 + t * (1.421413741 + t * (-1.453152027 + t * 1.061405429)))
    )
    tail = 0.5 * poly * bell
    cumulative = jnp.where(hidden < 0.0, tail, 1.0 - tail)
    return hidden * cumulative, cumulative + hidden * bell * 0.3989422804014327


def before_kernel(
    att_ref, x_ref, og_ref, wp_ref, bp_ref, dp_ref, up_ref, mask_ref, gain_ref, shift_ref,
    w2_ref, down1_ref, down2_ref, up2_ref,
    resid_ref, act_ref, midp_ref, mid1_ref, gm2_ref, grad_act_ref,
):
    mask = mask_ref[...]

    @pl.when(pl.program_id(0) == 0)
    def _():
        att = att_ref[...]
        midp_ref[...] = (dot_nn(att, dp_ref[...]) * mask).astype(bf16)
        branch = dot_nn(att, wp_ref[...]) + bp_ref[...]
        branch = branch + adapter_scale * dot_nt(midp_ref[...], up_ref[...])
        resid = x_ref[...].astype(f32) + branch
        resid_ref[...] = resid
        normed, _ = normalize(resid)
        act_ref[...] = (normed * gain_ref[...] + shift_ref[...]).astype(bf16)
        mid1_ref[...] = (dot_nn(act_ref[...], down1_ref[...]) * mask).astype(bf16)
        middle = adapter_scale * dot_nn(og_ref[...], up2_ref[...]) * mask
        gm2_ref[...] = middle.astype(bf16)

    grad_act_ref[...] = dot_nt(og_ref[...], w2_ref[...]) + dot_nt(gm2_ref[...], down2_ref[...])


def before_call(att, x, og, wp, bp, dp, up, mask, gain, shift, w2, down1, down2, up2):
    rows, features = att.shape
    wide = w2.shape[0]
    block = 1024

    def fixed(shape):
        zeros = (0,) * len(shape)
        return pl.BlockSpec(shape, lambda j: zeros, pipeline_mode=pl.Buffered(1))

    ins = [att, x, og, wp, bp, dp, up, mask, gain, shift, w2, down1, down2, up2]
    specs = [fixed(a.shape) for a in ins]
    specs[10] = pl.BlockSpec((block, features), lambda j: (j, 0))
    specs[12] = pl.BlockSpec((block, LANES), lambda j: (j, 0))
    shapes = [
        jax.ShapeDtypeStruct((rows, features), f32),
        jax.ShapeDtypeStruct((rows, features), bf16),
        jax.ShapeDtypeStruct((rows, LANES), bf16),
        jax.ShapeDtypeStruct((rows, LANES), bf16),
        jax.ShapeDtypeStruct((rows, LANES), bf16),
        jax.ShapeDtypeStruct((rows, wide), f32),
    ]
    return pl.pallas_call(
        before_kernel,
        name="before",
        grid=(wide // block,),
        in_specs=specs,
        out_specs=[fixed(a.shape) for a in shapes[:5]]
        + [pl.BlockSpec((rows, block), lambda j: (0, j))],
        out_shape=shapes,
        compiler_params=params(("arbitrary",), 56),
        cost_estimate=pl.CostEstimate(
            flops=2 * rows * features * (wide + features),
            bytes_accessed=2 * features * wide + 4 * rows * wide + 16 * rows * features,
            transcendentals=0,
        ),
    )(*ins)


def feed_kernel(
    resid_ref, act_ref, mid1_ref, gm2_ref, grad_act_ref, og_ref, mask_ref, gain_ref,
    w1_ref, b1_ref, w2_ref, b2_ref, down1_ref, up1_ref, down2_ref, up2_ref,
    out_ref, grad_ref, branch_ref, gd1_ref, gu1_ref, gd2_ref, gu2_ref,
    total, back, mid2_sum, gm1_sum, gm2_t, mid1_t,
):
    step = pl.program_id(0)
    steps = pl.num_programs(0)
    mask = mask_ref[...]

    @pl.when(step == 0)
    def _():
        total[...] = jnp.zeros_like(total)
        back[...] = jnp.zeros_like(back)
        mid2_sum[...] = jnp.zeros_like(mid2_sum)
        gm1_sum[...] = jnp.zeros_like(gm1_sum)
        gm2_t[...] = chosen_rows(mask, gm2_ref[...])
        mid1_t[...] = chosen_rows(mask, mid1_ref[...])

    weight = w1_ref[...]
    hidden = dot_nn(act_ref[...], weight) + b1_ref[...]
    hidden = hidden + adapter_scale * dot_nt(mid1_ref[...], up1_ref[...])
    value, slope = gelu_parts(hidden)
    activated = value.astype(bf16)
    grad_hidden = (grad_act_ref[...] * slope).astype(bf16)
    total[...] += dot_nn(activated, w2_ref[...])
    mid2_sum[...] += dot_nn(activated, down2_ref[...])
    back[...] += dot_nt(grad_hidden, weight)
    gm1_sum[...] += dot_nn(grad_hidden, up1_ref[...])
    gd2_ref[...] = dot_nn(gm2_t[...], activated).astype(bf16)
    gu1_ref[...] = (adapter_scale * dot_nn(mid1_t[...], grad_hidden)).astype(bf16)

    @pl.when(step == steps - 1)
    def _():
        mid2 = mid2_sum[...] * mask
        mid2_low = mid2.astype(bf16)
        resid = resid_ref[...]
        final = resid + total[...] + b2_ref[...]
        final = final + adapter_scale * dot_nt(mid2_low, up2_ref[...])
        out_ref[...] = final.astype(bf16)
        gm1 = adapter_scale * gm1_sum[...] * mask
        gm1_low = gm1.astype(bf16)
        upstream = back[...] + dot_nt(gm1_low, down1_ref[...])
        normed, inverse = normalize(resid)
        grad = og_ref[...].astype(f32) + norm_back(upstream * gain_ref[...], normed, inverse)
        grad_ref[...] = grad
        branch_ref[...] = grad.astype(bf16)
        gd1_ref[...] = dot_nn(chosen_rows(mask, gm1_low), act_ref[...]).astype(bf16)
        gu2_ref[...] = (adapter_scale * dot_nn(chosen_rows(mask, mid2_low), og_ref[...])).astype(bf16)


def feed_call(
    resid, act, mid1, gm2, grad_act, og, mask, gain, w1, b1, w2, b2, down1, up1, down2, up2
):
    rows, features = act.shape
    wide = b1.shape[1]
    block = 512

    def fixed(shape):
        zeros = (0,) * len(shape)
        return pl.BlockSpec(shape, lambda j: zeros, pipeline_mode=pl.Buffered(1))

    def by_columns(height):
        return pl.BlockSpec((height, block), lambda j: (0, j))

    def by_rows(width):
        return pl.BlockSpec((block, width), lambda j: (j, 0))

    ins = [
        resid, act, mid1, gm2, grad_act, og, mask, gain, w1, b1, w2, b2, down1, up1, down2, up2
    ]
    specs = [fixed(a.shape) for a in ins]
    specs[4] = by_columns(rows)
    specs[8] = by_columns(features)
    specs[9] = by_columns(1)
    specs[10] = by_rows(features)
    specs[13] = by_rows(LANES)
    specs[14] = by_rows(LANES)
    return pl.pallas_call(
        feed_kernel,
        name="feed",
        grid=(wide // block,),
        in_specs=specs,
        out_specs=[
            fixed((rows, features)),
            fixed((rows, features)),
            fixed((rows, features)),
            fixed((RANK, features)),
            by_columns(RANK),
            by_columns(RANK),
            fixed((RANK, features)),
        ],
        scratch_shapes=[
            pltpu.VMEM((rows, features), f32),
            pltpu.VMEM((rows, features), f32),
            pltpu.VMEM((rows, LANES), f32),
            pltpu.VMEM((rows, LANES), f32),
            pltpu.VMEM((RANK, rows), bf16),
            pltpu.VMEM((RANK, rows), bf16),
        ],
        out_shape=[
            jax.ShapeDtypeStruct((rows, features), bf16),
            jax.ShapeDtypeStruct((rows, features), f32),
            jax.ShapeDtypeStruct((rows, features), bf16),
            jax.ShapeDtypeStruct((RANK, features), bf16),
            jax.ShapeDtypeStruct((RANK, wide), bf16),
            jax.ShapeDtypeStruct((RANK, wide), bf16),
            jax.ShapeDtypeStruct((RANK, features), bf16),
        ],
        compiler_params=params(("arbitrary",), 58),
        cost_estimate=pl.CostEstimate(
            flops=6 * rows * features * wide,
            bytes_accessed=4 * features * wide + 4 * rows * wide + 24 * rows * features,
            transcendentals=2 * rows * wide,
        ),
    )(*ins)


def unproject_kernel(
    branch_ref, att_ref, weight_ref, down_ref, up_ref, mid_ref, mask_ref, sums_ref,
    grad_ref, inner_ref, gd_ref, gu_ref,
):
    branch = branch_ref[...]
    att = att_ref[...]
    middle = (adapter_scale * dot_nn(branch, up_ref[...]) * mask_ref[...]).astype(bf16)
    grad = dot_nt(branch, weight_ref[...]) + dot_nt(middle, down_ref[...])
    grad_ref[...] = grad.astype(bf16)
    product = grad_ref[...].astype(f32) * att.astype(f32)
    high = product.astype(bf16)
    low = (product - high.astype(f32)).astype(bf16)
    inner = dot_nt(sums_ref[...], high) + dot_nt(sums_ref[...], low)
    for head in range(HEADS):
        inner_ref[head] = inner[head : head + 1, :]
    gd_ref[...] = dot_nn(chosen_rows(mask_ref[...], middle), att).astype(bf16)
    own_t = chosen_rows(mask_ref[...], mid_ref[...])
    gu_ref[...] = (adapter_scale * dot_nn(own_t, branch)).astype(bf16)


def unproject_call(branch, att, weight, down, up, mid, mask, sums):
    rows, features = branch.shape
    return pl.pallas_call(
        unproject_kernel,
        name="unproject",
        out_shape=[
            jax.ShapeDtypeStruct((rows, features), bf16),
            jax.ShapeDtypeStruct((HEADS, 1, rows), f32),
            jax.ShapeDtypeStruct((RANK, features), bf16),
            jax.ShapeDtypeStruct((RANK, features), bf16),
        ],
        compiler_params=params(None, 50),
        cost_estimate=pl.CostEstimate(
            flops=2 * rows * features * features,
            bytes_accessed=2 * features * features + 8 * rows * features,
            transcendentals=0,
        ),
    )(branch, att, weight, down, up, mid, mask, sums)


def close_kernel(
    shape, widths, dq_ref, dk_ref, dv_ref, weight_ref, down_ref, up_ref, mid_ref,
    mask_ref, x_ref, gain_ref, shift_ref, *refs,
):
    count, parts = shape
    devices = count * parts
    remote = courier_lines(dict(dp=count, seq=parts), []) is not None
    terms, refs = refs[:6], refs[6:]
    if remote:
        packs_ref, part_ref = refs[:2]
        grads, refs = refs[2:10], refs[10:]
    else:
        part_ref, out_ref = refs[:2]
        refs = refs[2:]
    total, normed_ref, grad_up, grad_down, stage = refs[:5]
    step = pl.program_id(0)
    features = x_ref.shape[1]
    if remote:
        landed, sends, arrivals = refs[5:]
        me = lax.axis_index("dp") * parts + lax.axis_index("seq")
        barrier = pltpu.get_barrier_semaphore()

        def peer(k):
            at = lax.rem(me + k, devices)
            return (at // parts, at % parts)

        def rows(at):
            return pl.ds(pl.multiple_of(at * RANK, RANK), RANK)

        def copy_to(k):
            at = lax.rem(me + k, devices)
            return pltpu.make_async_remote_copy(
                src_ref=stage.at[rows(at), :],
                dst_ref=landed.at[rows(me), :],
                send_sem=sends.at[k],
                recv_sem=arrivals.at[k],
                device_id=peer(k),
                device_id_type=pl.DeviceIdType.MESH,
            )

    @pl.when(step == 0)
    def _():
        if remote:

            def greet(k, carry):
                pl.semaphore_signal(
                    barrier, inc=1, device_id=peer(k), device_id_type=pl.DeviceIdType.MESH
                )
                return carry

            lax.fori_loop(1, devices, greet, 0)
        total[...] = jnp.zeros_like(total)
        own_t = chosen_rows(mask_ref[...], mid_ref[...])
        middle = jnp.zeros((x_ref.shape[0], LANES), f32)
        for index, source in enumerate((dq_ref, dk_ref, dv_ref)):
            at = pl.ds(index * features, features)
            middle += dot_nn(source[...], up_ref[at, :])
            grad_up[:, at] = (adapter_scale * dot_nn(own_t, source[...])).astype(bf16)
        middle = (adapter_scale * middle * mask_ref[...]).astype(bf16)
        normed, _ = normalize(x_ref[...].astype(f32))
        normed_ref[...] = normed
        act = (normed * gain_ref[...].astype(f32) + shift_ref[...].astype(f32)).astype(bf16)
        total[...] = dot_nt(middle, down_ref[...])
        grad_down[...] = dot_nn(chosen_rows(mask_ref[...], middle), act).astype(bf16)
        at = 0
        for source, width in zip((grad_down, *terms[:3], grad_up, *terms[3:]), widths):
            for device in range(devices):
                stage[device * RANK : (device + 1) * RANK, at : at + width] = source[
                    :, device * width : (device + 1) * width
                ]
            at += width
        if remote:
            pl.semaphore_wait(barrier, devices - 1)

            def send(k, carry):
                copy_to(k).start()
                return carry

            lax.fori_loop(1, devices, send, 0)
            landed[rows(me), :] = stage[rows(me), :]
        else:
            out_ref[...] = stage[...]

    for index, source in enumerate((dq_ref, dk_ref, dv_ref)):

        @pl.when(step == index)
        def _():
            total[...] += dot_nt(source[...], weight_ref[...])

    @pl.when(step == 2)
    def _():
        _, inverse = normalize(x_ref[...].astype(f32))
        scaled = total[...] * gain_ref[...].astype(f32)
        part_ref[...] = norm_back(scaled, normed_ref[...], inverse)
        if remote:
            row = lax.broadcasted_iota(jnp.int32, (devices * RANK, packs_ref.shape[0]), 0)
            column = lax.broadcasted_iota(jnp.int32, (devices * RANK, packs_ref.shape[0]), 1)
            chosen = (column == row // RANK * (packs_ref.shape[0] // devices) + VECTORS).astype(bf16)
            adapter = dot_nn(chosen, packs_ref[:, :LANES])[:, 0:1]
            row = lax.broadcasted_iota(jnp.int32, (devices * RANK, LANES), 0)
            column = lax.broadcasted_iota(jnp.int32, (devices * RANK, LANES), 1)
            same = (column // RANK).astype(f32) == adapter
            spread = jnp.where(same & (row % RANK == column % RANK), 1.0, 0.0).astype(bf16)

            def wait(k, carry):
                copy_to(k).wait()
                return carry

            lax.fori_loop(1, devices, wait, 0)
            sums = dot_tn(landed[...], spread)
            at = 0
            for target, width in zip(grads, widths):
                target[...] = sums[at : at + width, :]
                at += width


def close_call(
    mesh_shape, widths, dq, dk, dv, weight, down, up, mid, mask, x, gain, shift, terms,
    packs,
):
    rows, features = dq.shape
    devices = mesh_shape["dp"] * mesh_shape["seq"]
    remote = courier_lines(mesh_shape, []) is not None
    span = sum(widths)

    def fixed(shape):
        zeros = (0,) * len(shape)
        return pl.BlockSpec(shape, lambda j: zeros, pipeline_mode=pl.Buffered(1))

    ins = [dq, dk, dv, weight, down, up, mid, mask, x, gain, shift, *terms]
    specs = [fixed(a.shape) for a in ins]
    specs[3] = pl.BlockSpec((features, features), lambda j: (0, j))
    shapes = [jax.ShapeDtypeStruct((rows, features), f32)]
    scratch = [
        pltpu.VMEM((rows, features), f32),
        pltpu.VMEM((rows, features), f32),
        pltpu.VMEM((RANK, 3 * features), bf16),
        pltpu.VMEM((RANK, features), bf16),
        pltpu.VMEM((devices * RANK, span), bf16),
    ]
    options = {}
    if remote:
        ins.append(packs)
        specs.append(fixed(packs.shape))
        shapes += [jax.ShapeDtypeStruct((width, LANES), f32) for width in widths]
        scratch += [
            pltpu.VMEM((devices * RANK, span), bf16),
            pltpu.SemaphoreType.DMA((devices,)),
            pltpu.SemaphoreType.DMA((devices,)),
        ]
        options = dict(collective_id=4, has_side_effects=True)
    else:
        shapes.append(jax.ShapeDtypeStruct((devices * RANK, span), bf16))
    out = pl.pallas_call(
        functools.partial(close_kernel, (mesh_shape["dp"], mesh_shape["seq"]), widths),
        name="close",
        grid=(3,),
        in_specs=specs,
        out_specs=[fixed(a.shape) for a in shapes],
        scratch_shapes=scratch,
        out_shape=shapes,
        compiler_params=pltpu.CompilerParams(
            dimension_semantics=("arbitrary",), vmem_limit_bytes=56 * 1024 * 1024, **options
        ),
        cost_estimate=pl.CostEstimate(
            flops=6 * rows * features * features,
            bytes_accessed=6 * features * features + 20 * rows * features,
            transcendentals=0,
        ),
    )(*ins)
    if remote:
        return out[0], out[1:]
    received = lax.all_to_all(
        out[1].reshape(devices, RANK, span), ("dp", "seq"), 0, 0, tiled=True
    ).reshape(devices * RANK, span)
    rank = np.arange(devices * RANK)[:, None] % RANK
    column = np.arange(LANES)[None, :]
    source = packs.reshape(devices, -1, packs.shape[1])[:, VECTORS, 0].astype(jnp.int32)
    images = jnp.broadcast_to(source[:, None], (devices, RANK)).reshape(devices * RANK, 1)
    spread = ((images == column // RANK) & (rank == column % RANK)).astype(bf16)
    sums = dot_tn(received, spread)
    grads, at = [], 0
    for width in widths:
        grads.append(sums[at : at + width])
        at += width
    return out[0], grads


def position_tables(rel_h, rel_w, length):
    wide = ((0, LANES // 2 - (2 * G - 1)), (0, LANES - HEAD_DIM))
    h = jnp.pad(rel_h, wide)
    w = jnp.pad(rel_w, wide)
    h_back = jnp.pad(rel_h[::-1], wide)
    w_back = jnp.pad(rel_w[::-1], wide)
    forward = jnp.concatenate([h_back, h_back, w_back, w_back], axis=0).T
    backward = jnp.concatenate([h, h, w, w], axis=0)
    spot = np.arange(length)[:, None]
    lane = np.arange(LANES)[None, :]
    at = np.where((lane // G) % 2 == 0, spot // G, spot % G)
    spots = jnp.asarray(lane % G == at, bf16)
    turned = jnp.asarray(lane % G == G - 1 - at, bf16)
    return forward, backward, spots, turned


def vectors_kernel(devices, sizes, source, target):
    rows = source.shape[0] // devices
    target[...] = jnp.zeros_like(target)
    packs = source[...].astype(f32)
    for line, size in enumerate(sizes):
        for device in range(devices):
            at = device * rows + line
            target[line : line + 1, device * size : (device + 1) * size] = packs[
                at : at + 1, 0:size
            ]


def vectors_call(gathered, devices, sizes):
    return pl.pallas_call(
        functools.partial(vectors_kernel, devices, sizes),
        name="vectors",
        out_shape=jax.ShapeDtypeStruct((VECTORS, devices * max(sizes)), f32),
        compiler_params=params(None, 16),
    )(gathered)


def per_device(
    mesh_shape,
    tokens,
    adapter_index,
    norm1_gain,
    norm1_bias,
    qkv_weight,
    qkv_bias,
    proj_weight,
    proj_bias,
    norm2_gain,
    norm2_bias,
    fc1_weight,
    fc1_bias,
    fc2_weight,
    fc2_bias,
    rel_pos_h,
    rel_pos_w,
    qkv_down,
    qkv_up,
    proj_down,
    proj_up,
    fc1_down,
    fc1_up,
    fc2_down,
    fc2_up,
    out_grad,
):
    axes = ("dp", "seq")
    part_count = mesh_shape["seq"]
    devices = mesh_shape["dp"] * part_count
    images, part_len, features = tokens.shape
    length = part_len * part_count
    own_tokens = tokens[0]
    og = out_grad[0]
    place = lax.axis_index("seq").astype(jnp.int32).reshape(1)

    small = [
        norm1_gain, norm1_bias, qkv_bias, proj_bias, norm2_gain, norm2_bias, fc1_bias, fc2_bias,
        adapter_index.astype(bf16),
    ]
    sizes = [a.shape[0] for a in small]
    pack = jnp.concatenate([jnp.pad(a, (0, 2 * LANES - a.shape[0])) for a in small])
    pack = jnp.pad(pack.reshape(len(small), 2 * LANES), ((0, 16 - len(small)), (0, 0)))

    columns = jnp.arange(LANES, dtype=jnp.int32) // RANK
    mask = (columns[None, :] == adapter_index[:, None]).astype(f32)
    forward_table, back_table, spots, turned_spots = position_tables(rel_pos_h, rel_pos_w, length)
    head_of = np.arange(features)[None, :] // HEAD_DIM
    head_sums = jnp.asarray(head_of == np.arange(HEADS)[:, None], bf16)

    w_fc2 = lax.all_gather(fc2_weight, axes, axis=0, tiled=True)
    w_fc1 = lax.all_gather(fc1_weight, axes, axis=0, tiled=True)
    (w_qkv, d_qkv, u_qkv, all_small), image_tokens = collect(
        mesh_shape, [qkv_weight, qkv_down, qkv_up.T, pack], own_tokens
    )
    vectors = vectors_call(all_small, devices, sizes[:VECTORS])
    g1, s1, b_qkv, b_proj, g2, s2, b_fc1, b_fc2 = (
        vectors[i : i + 1, : devices * sizes[i]] for i in range(VECTORS)
    )
    (heads, mid_qkv, att, lse, aux), rest = front_call(
        mesh_shape, part_len, image_tokens, g1, s1, w_qkv, b_qkv, d_qkv, u_qkv, mask,
        forward_table, spots,
        [proj_weight, proj_down, fc1_down, fc2_down, proj_up.T, fc1_up.T, fc2_up.T],
    )
    w_proj, d_proj, d_fc1, d_fc2, u_proj, u_fc1, u_fc2 = rest
    resid, act_two, mid_proj, mid_fc1, gm_fc2, grad_act = before_call(
        att, own_tokens, og, w_proj, b_proj, d_proj, u_proj, mask, g2, s2, w_fc2, d_fc1, d_fc2,
        u_fc2,
    )
    block_out, grad_resid, grad_branch, gd_fc1, gu_fc1, gd_fc2, gu_fc2 = feed_call(
        resid, act_two, mid_fc1, gm_fc2, grad_act, og, mask, g2, w_fc1, b_fc1, w_fc2, b_fc2,
        d_fc1, u_fc1, d_fc2, u_fc2,
    )
    grad_att, inner, gd_proj, gu_proj = unproject_call(
        grad_branch, att, w_proj, d_proj, u_proj, mid_proj, mask, head_sums
    )
    if part_count == 2:
        swap = [(0, 1), (1, 0)]
        their_grad, their_lse, their_inner = (
            lax.ppermute(a, "seq", swap)[None] for a in (grad_att, lse, inner)
        )
    else:
        their_grad, their_lse, their_inner = (
            lax.all_gather(a, "seq", axis=0) for a in (grad_att, lse, inner)
        )
    dq, dk_own, dv_own = own_call(
        place, heads, aux, spots, turned_spots, back_table, grad_att, lse, inner
    )
    dk, dv = other_call(
        place, heads, aux, spots, their_grad, their_lse, their_inner, dk_own, dv_own
    )
    mid_own = lax.dynamic_slice_in_dim(mid_qkv, place[0] * part_len, part_len, 0)
    widths = [a.shape[0] for a in (qkv_down, proj_down, fc1_down, fc2_down)]
    widths += [a.shape[1] for a in (qkv_up, proj_up, fc1_up, fc2_up)]
    last_part, grads = close_call(
        mesh_shape, widths, dq, dk, dv, w_qkv, d_qkv, u_qkv, mid_own, mask, own_tokens, g1,
        s1, [gd_proj, gd_fc1, gd_fc2, gu_proj, gu_fc1, gu_fc2], all_small,
    )
    return (
        block_out[None],
        (grad_resid + last_part)[None],
        grads[0],
        grads[4].T,
        grads[1],
        grads[5].T,
        grads[2],
        grads[6].T,
        grads[3],
        grads[7].T,
    )


def solution(mesh):
    both = ("dp", "seq")
    return jax.shard_map(
        functools.partial(per_device, dict(mesh.shape)),
        mesh=mesh,
        in_specs=(
            P("dp", "seq", None),
            P("dp"),
            P(both),
            P(both),
            P(both, None),
            P(both),
            P(both, None),
            P(both),
            P(both),
            P(both),
            P(both, None),
            P(both),
            P(both, None),
            P(both),
            P(),
            P(),
            P(both, None),
            P(None, both),
            P(both, None),
            P(None, both),
            P(both, None),
            P(None, both),
            P(both, None),
            P(None, both),
            P("dp", "seq", None),
        ),
        out_specs=(
            P("dp", "seq", None),
            P("dp", "seq", None),
            P(both, None),
            P(None, both),
            P(both, None),
            P(None, both),
            P(both, None),
            P(None, both),
            P(both, None),
            P(None, both),
        ),
        check_vma=False,
    )
```

```python
import functools

import jax
import jax.numpy as jnp
import numpy as np
from jax import lax
from jax.experimental import pallas as pl
from jax.experimental.pallas import tpu as pltpu
from jax.sharding import PartitionSpec as P

HEADS = 16
HEAD_DIM = 80
ADAPTERS = 8
RANK = 16
G = 32
LANES = 128
VECTORS = 8
HALF = HEADS // 2

epsilon = 1e-06
adapter_scale = 0.5
log2e = 1.4426950408889634
score_scale = HEAD_DIM ** (-0.5)
exponent_scale = score_scale * log2e
f32 = jnp.float32
bf16 = jnp.bfloat16


def dot_nn(left, right):
    return lax.dot_general(left, right, (((1,), (0,)), ((), ())), preferred_element_type=f32)


def dot_nt(left, right):
    return lax.dot_general(left, right, (((1,), (1,)), ((), ())), preferred_element_type=f32)


def dot_tn(left, right):
    return lax.dot_general(left, right, (((0,), (0,)), ((), ())), preferred_element_type=f32)


def normalize(values):
    average = jnp.mean(values, axis=-1, keepdims=True)
    centered = values - average
    variance = jnp.mean(centered * centered, axis=-1, keepdims=True)
    inverse = lax.rsqrt(variance + epsilon)
    return centered * inverse, inverse


def norm_back(scaled, normed, inverse):
    return inverse * (
        scaled
        - jnp.mean(scaled, axis=-1, keepdims=True)
        - normed * jnp.mean(scaled * normed, axis=-1, keepdims=True)
    )


def chosen_rows(mask, middle):
    rank = lax.broadcasted_iota(jnp.int32, (RANK, LANES), 0)
    column = lax.broadcasted_iota(jnp.int32, (RANK, LANES), 1)
    pick = jnp.where(column % RANK == rank, jnp.broadcast_to(mask, (RANK, LANES)), 0.0)
    return dot_nt(pick.astype(bf16), middle).astype(bf16)


def params(semantics, megabytes):
    return pltpu.CompilerParams(
        dimension_semantics=semantics, vmem_limit_bytes=megabytes * 1024 * 1024
    )


def whole(shape):
    zeros = (0,) * len(shape)
    return pl.BlockSpec(shape, lambda *_: zeros)


Z, X, Y, S, XD, YD, SX, SY, SD = range(9)


class Courier:
    def __init__(self, lines, chunks, rows_of, sources, targets, local, sends, arrivals):
        self.lines = lines
        self.chunks = chunks
        self.rows_of = rows_of
        self.sources, self.targets = sources, targets
        self.local, self.sends, self.arrivals = local, sends, arrivals
        dp = lax.axis_index("dp")
        self.seq = lax.axis_index("seq")
        self.dp = dp
        self.line, self.column, self.core = dp // 4, (dp // 2) % 2, dp % 2
        line, column, core, seq = self.line, self.column, self.core, self.seq
        self.ahead = [
            self.device(lax.rem(line + k, lines), column, core, seq) for k in range(1, lines)
        ]
        self.across = self.device(line, 1 - column, core, seq)
        self.partner = self.device(line, column, core, 1 - seq)
        self.sibling = self.device(line, column, 1 - core, seq)

    @staticmethod
    def device(z, x, c, y):
        return (z * 4 + x * 2 + c, y)

    def owner(self, k, x, c, y):
        return self.device(lax.rem(self.line + self.lines - k, self.lines), x, c, y)

    def greet(self):
        peers = self.ahead + [self.across, self.partner, self.sibling]
        barrier = pltpu.get_barrier_semaphore()
        for peer in peers:
            pl.semaphore_signal(
                barrier, inc=1, device_id=peer, device_id_type=pl.DeviceIdType.MESH
            )
        pl.semaphore_wait(barrier, len(peers))

    def slot(self, number, kind, k):
        return (number * 9 + kind) * self.lines + k

    def part(self, number, half):
        _, row, height, col, width, share = self.chunks[number]
        if half is None:
            return row, height, col, width
        if width >= 2 * LANES:
            cut = width // LANES * share // 4 * LANES
            return (row, height, col, cut) if half == 0 else (row, height, col + cut, width - cut)
        cut = height // 8 * share // 4 * 8
        return (row, cut, col, width) if half == 0 else (row + cut, height - cut, col, width)

    def place(self, number, owner, half=None):
        array = self.chunks[number][0]
        row, height, col, width = self.part(number, half)
        if height == 0 or width == 0:
            return None
        start = (owner[0] * 2 + owner[1]) * self.rows_of[array] + row
        return self.targets[array].at[pl.ds(pl.multiple_of(start, 8), height), pl.ds(col, width)]

    def like(self, number, half=None):
        array = self.chunks[number][0]
        row, height, col, width = self.part(number, half)
        if height == 0 or width == 0:
            return None
        return self.targets[array].at[pl.ds(row, height), pl.ds(col, width)]

    def send(self, source, target, peer, number, kind, k):
        at = self.slot(number, kind, k)
        pltpu.make_async_remote_copy(
            src_ref=source,
            dst_ref=target,
            send_sem=self.sends.at[at],
            recv_sem=self.arrivals.at[at],
            device_id=peer,
            device_id_type=pl.DeviceIdType.MESH,
        ).start()

    def arrive(self, place, number, kind, k):
        pltpu.make_async_copy(place, place, self.arrivals.at[self.slot(number, kind, k)]).wait()

    def start(self, number):
        array, row, height, col, width, _ = self.chunks[number]
        own = self.sources[array].at[pl.ds(row, height), pl.ds(col, width)]
        place = self.place(number, (self.dp, self.seq))
        for k in range(1, self.lines):
            self.send(own, place, self.ahead[k - 1], number, Z, k)
        self.send(own, place, self.across, number, X, 0)
        self.send(own, place, self.partner, number, Y, 0)
        self.send(own, place, self.sibling, number, S, 0)
        pltpu.make_async_copy(own, place, self.local.at[number]).start()

    def stage_one(self, number, k):
        place = self.place(number, self.owner(k, self.column, self.core, self.seq))
        self.arrive(place, number, Z, k)
        self.send(place, place, self.across, number, X, k)
        self.send(place, place, self.partner, number, Y, k)
        self.send(place, place, self.sibling, number, S, k)

    def stage_two(self, number, k):
        owner = self.owner(k, 1 - self.column, self.core, self.seq)
        place = self.place(number, owner)
        self.arrive(place, number, X, k)
        half = self.place(number, owner, 0)
        if half is not None:
            self.send(half, half, self.partner, number, YD, k)
        self.send(place, place, self.sibling, number, SX, k)
        owner = self.owner(k, self.column, self.core, 1 - self.seq)
        place = self.place(number, owner)
        self.arrive(place, number, Y, k)
        half = self.place(number, owner, 1)
        if half is not None:
            self.send(half, half, self.across, number, XD, k)
        self.send(place, place, self.sibling, number, SY, k)

    def stage_three(self, number, k):
        owner = self.owner(k, 1 - self.column, self.core, 1 - self.seq)
        for half, kind in ((0, YD), (1, XD)):
            piece = self.place(number, owner, half)
            if piece is not None:
                self.arrive(piece, number, kind, k)
        place = self.place(number, owner)
        self.send(place, place, self.sibling, number, SD, k)

    def stage_four(self, number, k):
        for kind, x, y in (
            (S, self.column, self.seq),
            (SX, 1 - self.column, self.seq),
            (SY, self.column, 1 - self.seq),
            (SD, 1 - self.column, 1 - self.seq),
        ):
            place = self.place(number, self.owner(k, x, 1 - self.core, y))
            self.arrive(place, number, kind, k)

    def steps(self):
        stages = (self.stage_one, self.stage_two, self.stage_three, self.stage_four)
        order = []
        for tick in range(len(self.chunks) + 3):
            for lag, stage in enumerate(stages):
                if 0 <= tick - lag < len(self.chunks):
                    for k in range(1 if lag == 0 else 0, self.lines):
                        order.append(functools.partial(stage, tick - lag, k))
        return order

    def finish(self):
        for number in range(len(self.chunks)):
            like = self.like(number)
            pltpu.make_async_copy(like, like, self.local.at[number]).wait()
            for kind in range(9):
                half = {YD: 0, XD: 1}.get(kind)
                like = self.like(number, half)
                for k in range(self.lines):
                    if like is not None and not (kind == Z and k == 0):
                        sem = self.sends.at[self.slot(number, kind, k)]
                        pltpu.make_async_copy(like, like, sem).wait()


def cut_chunks(arrays, share=2):
    chunks = []
    for index, array in enumerate(arrays):
        height, width = array.shape
        wide, tall = width, height
        if height * wide * 2 > 120_000 and wide > 1280:
            wide = next(w for w in range(1280, 0, -LANES) if width % w == 0)
        while tall * wide * 2 > 120_000 and tall % 16 == 0:
            tall //= 2
        for row in range(0, height, tall):
            for col in range(0, width, wide):
                chunks.append((index, row, tall, col, wide, share))
    return chunks


def courier_lines(mesh_shape, arrays):
    lines = mesh_shape["dp"] // 4
    fits = mesh_shape["seq"] == 2 and mesh_shape["dp"] == 4 * lines and 2 <= lines <= 4
    return lines if fits and not any(a.shape[0] % 8 for a in arrays) else None


def courier_scratch(lines, chunks):
    slots = len(chunks) * 9 * lines
    return [
        pltpu.SemaphoreType.DMA((len(chunks),)),
        pltpu.SemaphoreType.DMA((slots,)),
        pltpu.SemaphoreType.DMA((slots,)),
    ]


def gathered_shapes(devices, arrays):
    return [jax.ShapeDtypeStruct((devices * a.shape[0], a.shape[1]), a.dtype) for a in arrays]


def collect_kernel(lines, chunks, rows_of, count, *refs):
    sources, tokens = refs[:count], refs[count]
    targets, other = refs[count + 1 : 2 * count + 1], refs[2 * count + 1]
    local, sends, arrivals, token_sem = refs[2 * count + 2 :]
    courier = Courier(lines, chunks, rows_of, sources, targets, local, sends, arrivals)
    courier.greet()
    passed = pltpu.make_async_remote_copy(
        src_ref=tokens,
        dst_ref=other,
        send_sem=token_sem.at[0],
        recv_sem=token_sem.at[1],
        device_id=courier.partner,
        device_id_type=pl.DeviceIdType.MESH,
    )
    for number in range(len(chunks)):
        courier.start(number)
    passed.start()
    for step in courier.steps():
        step()
    passed.wait()
    courier.finish()


def collect(mesh_shape, arrays, tokens):
    axes = ("dp", "seq")
    lines = courier_lines(mesh_shape, arrays)
    if lines is None:
        gathered = [lax.all_gather(a, axes, axis=0, tiled=True) for a in arrays]
        return gathered, [lax.all_gather(tokens, "seq", axis=0, tiled=True)]
    chunks = cut_chunks(arrays, 1)
    anywhere = pl.BlockSpec(memory_space=pl.ANY)
    count = len(arrays)
    out = pl.pallas_call(
        functools.partial(collect_kernel, lines, chunks, [a.shape[0] for a in arrays], count),
        name="collect",
        in_specs=[anywhere] * (count + 1),
        out_specs=[anywhere] * (count + 1),
        out_shape=gathered_shapes(mesh_shape["dp"] * 2, arrays)
        + [jax.ShapeDtypeStruct(tokens.shape, tokens.dtype)],
        scratch_shapes=courier_scratch(lines, chunks) + [pltpu.SemaphoreType.DMA((2,))],
        compiler_params=pltpu.CompilerParams(collective_id=1, has_side_effects=True),
    )(*arrays, tokens)
    return list(out[:count]), [tokens, out[count]]


def qkv_part(part, blocks, gain_ref, shift_ref, weight_ref, bias_ref, down_ref, up_ref, mask_ref,
             heads, mid_ref, act_ref, pause):
    length = act_ref.shape[0]

    @pl.when(part == 0)
    def _():
        part_len = length // len(blocks)
        for index, block in enumerate(blocks):
            place = 0
            if len(blocks) == 2:
                seq = lax.axis_index("seq")
                place = pl.multiple_of((seq if index == 0 else 1 - seq) * part_len, G)
            normed, _ = normalize(block[...].astype(f32))
            act = normed * gain_ref[...].astype(f32) + shift_ref[...].astype(f32)
            act_ref[pl.ds(place, part_len), :] = act.astype(bf16)
        mid_ref[...] = (dot_nn(act_ref[...], down_ref[...]) * mask_ref[...]).astype(bf16)

    rows = min(256, length)
    lane = lax.broadcasted_iota(jnp.int32, (rows, LANES - HEAD_DIM), 1)
    pad = jnp.where((lane == 0) & (part == 2), 1.0, 0.0).astype(bf16)
    for start in range(0, length, rows):
        here = pl.ds(start, rows)
        block = dot_nn(act_ref[here, :], weight_ref[...])
        block = block + bias_ref[...].astype(f32)
        block = block + adapter_scale * dot_nt(mid_ref[here, :], up_ref[...])
        block = block.astype(bf16)
        for head in range(HEADS):
            heads[part, head, here, 0:HEAD_DIM] = block[:, head * HEAD_DIM : (head + 1) * HEAD_DIM]
            heads[part, head, here, HEAD_DIM:LANES] = pad
        pause(start // rows)


def attend_head(head, own, heads, table_ref, spots_ref, att_ref, lse_ref, aux_ref, pause):
    pause(0)
    length = heads.shape[2]
    part_len = att_ref.shape[0]
    lane = lax.broadcasted_iota(jnp.int32, (G, LANES), 1)
    first = lane < LANES // 2
    even = (lane // G) % 2 == 0
    raw = dot_nn(heads[0, head], table_ref[...]) * (HEAD_DIM**0.5)
    for row in range(length // G):
        block = raw[row * G : (row + 1) * G, :]
        high = block.astype(bf16).astype(f32)
        mixed_h = jnp.where(first, high[:, :LANES], block[:, :LANES] - high[:, :LANES])
        mixed_w = jnp.where(first, high[:, LANES:], block[:, LANES:] - high[:, LANES:])
        along_h = pltpu.roll(mixed_h, LANES - G + 1 + row, 1)
        along_w = pltpu.roll(mixed_w, 1, 1, stride=1, stride_axis=0)
        aux_ref[0, pl.ds(row * G, G), :] = jnp.where(even, along_h, along_w).astype(bf16)
    pause(1)
    left = jnp.concatenate([heads[0, head, own, :], aux_ref[0, own, :]], axis=1)
    right = jnp.concatenate([heads[1, head], spots_ref[...]], axis=1)
    scores = dot_nt(left, right)
    top = jnp.max(scores, axis=1, keepdims=True)
    shares = jnp.exp2((scores - top) * exponent_scale).astype(bf16)
    mixed = dot_nn(shares, heads[2, head])
    total = mixed[:, HEAD_DIM : HEAD_DIM + 1]
    att = (mixed[:, :HEAD_DIM] / total).astype(bf16)
    logs = top * exponent_scale + jnp.log2(total)
    lse_ref[0] = jnp.transpose(jnp.broadcast_to(logs, (part_len, LANES)))[0:1, :]
    for slot in range(HALF):

        @pl.when(head % HALF == slot)
        def _():
            att_ref[:, slot * HEAD_DIM : (slot + 1) * HEAD_DIM] = att


def front_kernel(
    lines, chunks, rows_of, count, pair,
    gain_ref, shift_ref, weight_ref, bias_ref, down_ref, up_ref, mask_ref, table_ref,
    spots_ref, *refs,
):
    blocks, refs = refs[:pair], refs[pair:]
    sources = refs[:count]
    heads_out, mid_ref, att_ref, lse_ref, aux_ref = refs[count : count + 5]
    targets = refs[count + 5 : 2 * count + 5]
    heads, act_ref, out_sem = refs[2 * count + 5 : 2 * count + 8]
    step = pl.program_id(0)
    last = pl.num_programs(0) - 1
    courier = None
    plan = {}
    if count:
        courier = Courier(lines, chunks, rows_of, sources, targets, *refs[2 * count + 8 :])

        @pl.when(step == 0)
        def _():
            courier.greet()
            for number in range(len(chunks)):
                courier.start(number)

        pieces = act_ref.shape[0] // min(256, act_ref.shape[0])
        places = [(part, piece, 7.0 / pieces) for part in range(3) for piece in range(pieces)]
        places += [(3 + head, piece, 1.0) for head in range(HEADS) for piece in range(2)]
        work = courier.steps()
        whole_time = sum(p[2] for p in places)
        done, spent = 0, 0.0
        for at, piece, time in places:
            spent += time
            upto = min(len(work), int(len(work) * spent / whole_time + 1e-6))
            plan[at, piece] = work[done:upto]
            done = upto

    def pause(first, count_of):
        def run(piece):
            for at in range(first, first + count_of):
                items = plan.get((at, piece))
                if items:

                    @pl.when(step == at)
                    def _():
                        for item in items:
                            item()

        return run

    @pl.when(step < 3)
    def _():
        qkv_part(
            step, blocks, gain_ref, shift_ref, weight_ref, bias_ref, down_ref, up_ref, mask_ref,
            heads, mid_ref, act_ref, pause(0, 3),
        )
        pltpu.make_async_copy(heads.at[step], heads_out.at[step], out_sem.at[step]).start()

    part_len = att_ref.shape[0]
    own = pl.ds(pl.multiple_of(lax.axis_index("seq") * part_len, G), part_len)

    @pl.when(step >= 3)
    def _():
        attend_head(
            step - 3, own, heads, table_ref, spots_ref, att_ref, lse_ref, aux_ref, pause(3, HEADS)
        )

    @pl.when(step == last)
    def _():
        for part in range(3):
            pltpu.make_async_copy(heads.at[part], heads_out.at[part], out_sem.at[part]).wait()
        if courier is not None:
            courier.finish()


def front_call(
    mesh_shape, part_len, tokens, gain, shift, weight, bias, down, up, mask, table, spots, arrays
):
    length = sum(t.shape[0] for t in tokens)
    features = weight.shape[0]
    lines = courier_lines(mesh_shape, arrays)
    later = []
    if lines is None:
        axes = ("dp", "seq")
        later = [lax.all_gather(a, axes, axis=0, tiled=True) for a in arrays]
        arrays = []
    chunks = cut_chunks(arrays)
    count = len(arrays)
    anywhere = pl.BlockSpec(memory_space=pl.ANY)

    def head(i):
        return jnp.maximum(i - 3, 0)

    def part(i):
        return jnp.minimum(i, 2)

    def fixed(shape):
        zeros = (0,) * len(shape)
        return pl.BlockSpec(shape, lambda i: zeros, pipeline_mode=pl.Buffered(1))

    options = dict(collective_id=2, has_side_effects=True) if count else {}
    out = pl.pallas_call(
        functools.partial(
            front_kernel, lines, chunks, [a.shape[0] for a in arrays], count, len(tokens)
        ),
        name="front",
        grid=(3 + HEADS,),
        in_specs=[
            fixed((1, features)),
            fixed((1, features)),
            pl.BlockSpec((features, features), lambda i: (0, part(i))),
            pl.BlockSpec((1, features), lambda i: (0, part(i))),
            fixed((features, LANES)),
            pl.BlockSpec((features, LANES), lambda i: (part(i), 0)),
            fixed((1, LANES)),
            fixed((LANES, 2 * LANES)),
            fixed((length, LANES)),
        ]
        + [fixed(t.shape) for t in tokens]
        + [anywhere] * count,
        out_specs=[
            anywhere,
            whole((length, LANES)),
            pl.BlockSpec((part_len, features // 2), lambda i: (0, head(i) // HALF)),
            pl.BlockSpec((1, 1, part_len), lambda i: (head(i), 0, 0)),
            pl.BlockSpec((1, length, LANES), lambda i: (head(i), 0, 0)),
        ]
        + [anywhere] * count,
        out_shape=[
            jax.ShapeDtypeStruct((3, HEADS, length, LANES), bf16),
            jax.ShapeDtypeStruct((length, LANES), bf16),
            jax.ShapeDtypeStruct((part_len, features), bf16),
            jax.ShapeDtypeStruct((HEADS, 1, part_len), f32),
            jax.ShapeDtypeStruct((HEADS, length, LANES), bf16),
        ]
        + gathered_shapes(mesh_shape["dp"] * mesh_shape["seq"], arrays),
        scratch_shapes=[
            pltpu.VMEM((3, HEADS, length, LANES), bf16),
            pltpu.VMEM((length, features), bf16),
            pltpu.SemaphoreType.DMA((3,)),
        ]
        + (courier_scratch(lines, chunks) if count else []),
        compiler_params=pltpu.CompilerParams(
            dimension_semantics=("arbitrary",), vmem_limit_bytes=58 * 1024 * 1024, **options
        ),
        cost_estimate=pl.CostEstimate(
            flops=6 * length * features * features
            + 8 * HEADS * part_len * length * LANES,
            bytes_accessed=2 * (3 * features * features + 8 * length * features),
            transcendentals=HEADS * part_len * length,
        ),
    )(gain, shift, weight, bias, down, up, mask, table, spots, *tokens, *arrays)
    return out[:5], list(out[5:]) + later


def own_kernel(
    place_ref, q_ref, aux_ref, k_ref, v_ref, spots_ref, turned_spots_ref, table_ref, grad_ref,
    lse_ref, inner_ref, dq_ref, dk_ref, dv_ref, shares_ref, dscores_ref, padded,
):
    part_len = q_ref.shape[2]
    lane = lax.broadcasted_iota(jnp.int32, (G, LANES), 1)
    start = place_ref[0] * (part_len // G)
    here = pl.ds(pl.multiple_of(place_ref[0] * part_len, G), part_len)
    for slot in range(HALF):
        cols = slice(slot * HEAD_DIM, (slot + 1) * HEAD_DIM)
        spare = slot % 2
        padded[spare, :, HEAD_DIM:LANES] = jnp.zeros((part_len, LANES - HEAD_DIM), bf16)
        padded[spare, :, 0:HEAD_DIM] = grad_ref[:, cols]
        queries = q_ref[0, slot]
        keys = k_ref[0, slot]
        left = jnp.concatenate([keys, spots_ref[...]], axis=1)
        right = jnp.concatenate([queries, aux_ref[slot]], axis=1)
        shares = jnp.exp2(dot_nt(left, right) * exponent_scale - lse_ref[slot])
        grad_shares = dot_nt(v_ref[0, slot], padded[spare])
        shares_ref[spare] = shares.astype(bf16)
        dscores_ref[spare] = (shares * (grad_shares - inner_ref[slot])).astype(bf16)
        flat = dot_tn(
            jnp.concatenate([keys, turned_spots_ref[...]], axis=1), dscores_ref[spare]
        )
        turned = jnp.transpose(flat)
        spread = []
        for row in range(part_len // G):
            sums = turned[row * G : (row + 1) * G, LANES:]
            along_h = pltpu.roll(jnp.where(lane < G, sums, 0.0), start + row, 1)
            along_w = pltpu.roll(
                jnp.where((lane >= G) & (lane < 2 * G), sums, 0.0), G, 1, stride=1, stride_axis=0
            )
            spread.append((along_h + along_w).astype(bf16))
        spread = jnp.concatenate(spread, axis=0)
        grad_query = turned[:, :LANES] * score_scale + dot_nn(spread, table_ref[...])
        dq_ref[:, cols] = grad_query[:, :HEAD_DIM].astype(bf16)
        dk_ref[slot] = dot_nn(dscores_ref[spare, here, :], queries)
        dv_ref[slot] = dot_nn(shares_ref[spare, here, :], padded[spare])


def own_call(place, heads, aux, spots, turned_spots, table, grad, lse, inner):
    length = heads.shape[2]
    part_len, features = grad.shape

    def part(index):
        return pl.BlockSpec((1, HALF, length, LANES), lambda n, s: (index, n, 0, 0))

    return pl.pallas_call(
        own_kernel,
        name="back_own",
        grid_spec=pltpu.PrefetchScalarGridSpec(
            num_scalar_prefetch=1,
            grid=(HEADS // HALF,),
            in_specs=[
                pl.BlockSpec((1, HALF, part_len, LANES), lambda n, s: (0, n, s[0], 0)),
                pl.BlockSpec((HALF, part_len, LANES), lambda n, s: (n, s[0], 0)),
                part(1),
                part(2),
                whole((length, LANES)),
                whole((length, LANES)),
                whole((LANES, LANES)),
                pl.BlockSpec((part_len, features // 2), lambda n, s: (0, n)),
                pl.BlockSpec((HALF, 1, part_len), lambda n, s: (n, 0, 0)),
                pl.BlockSpec((HALF, 1, part_len), lambda n, s: (n, 0, 0)),
            ],
            out_specs=[
                pl.BlockSpec((part_len, features // 2), lambda n, s: (0, n)),
                pl.BlockSpec((HALF, part_len, LANES), lambda n, s: (n, 0, 0)),
                pl.BlockSpec((HALF, part_len, LANES), lambda n, s: (n, 0, 0)),
            ],
            scratch_shapes=[
                pltpu.VMEM((2, length, part_len), bf16),
                pltpu.VMEM((2, length, part_len), bf16),
                pltpu.VMEM((2, part_len, LANES), bf16),
            ],
        ),
        out_shape=[
            jax.ShapeDtypeStruct((part_len, features), bf16),
            jax.ShapeDtypeStruct((HEADS, part_len, LANES), f32),
            jax.ShapeDtypeStruct((HEADS, part_len, LANES), f32),
        ],
        compiler_params=params(("arbitrary",), 60),
        cost_estimate=pl.CostEstimate(
            flops=8 * HEADS * part_len * length * LANES * 2,
            bytes_accessed=12 * HEADS * length * LANES,
            transcendentals=HEADS * part_len * length,
        ),
    )(place, heads, aux, heads, heads, spots, turned_spots, table, grad, lse, inner)


def other_kernel(
    steps, place_ref, q_ref, aux_ref, k_ref, v_ref, spots_ref, grad_ref, lse_ref, inner_ref,
    dk_in, dv_in, dk_ref, dv_ref, padded, *sums,
):
    step = pl.program_id(1)
    part_len = q_ref.shape[2]
    if sums:
        dk_sum, dv_sum = sums

        @pl.when(step == 0)
        def _():
            dk_sum[...] = dk_in[...]
            dv_sum[...] = dv_in[...]

    for slot in range(HALF):
        cols = slice(slot * HEAD_DIM, (slot + 1) * HEAD_DIM)
        spare = slot % 2
        padded[spare, :, HEAD_DIM:LANES] = jnp.zeros((part_len, LANES - HEAD_DIM), bf16)
        padded[spare, :, 0:HEAD_DIM] = grad_ref[0, :, cols]
        queries = q_ref[0, slot]
        left = jnp.concatenate([k_ref[0, slot], spots_ref[...]], axis=1)
        right = jnp.concatenate([queries, aux_ref[slot]], axis=1)
        shares = jnp.exp2(dot_nt(left, right) * exponent_scale - lse_ref[0, slot])
        grad_shares = dot_nt(v_ref[0, slot], padded[spare])
        dscores = (shares * (grad_shares - inner_ref[0, slot])).astype(bf16)
        grad_key = dot_nn(dscores, queries)
        grad_value = dot_nn(shares.astype(bf16), padded[spare])
        if sums:
            dk_sum[slot] += grad_key
            dv_sum[slot] += grad_value
        else:
            grad_key = (grad_key + dk_in[slot])[:, :HEAD_DIM] * score_scale
            grad_value = (grad_value + dv_in[slot])[:, :HEAD_DIM]
            dk_ref[:, cols] = grad_key.astype(bf16)
            dv_ref[:, cols] = grad_value.astype(bf16)

    if sums:

        @pl.when(step == steps - 1)
        def _():
            for slot in range(HALF):
                cols = slice(slot * HEAD_DIM, (slot + 1) * HEAD_DIM)
                dk_ref[:, cols] = (dk_sum[slot, :, :HEAD_DIM] * score_scale).astype(bf16)
                dv_ref[:, cols] = dv_sum[slot, :, :HEAD_DIM].astype(bf16)


def other_call(place, heads, aux, spots, grads, lses, inners, dk, dv):
    length = heads.shape[2]
    blocks, part_len, features = grads.shape
    count = length // part_len

    def theirs(i, s):
        return lax.rem(s[0] + 1 + i, count)

    def given(i, s):
        return theirs(i, s) if blocks > 1 else 0

    def own(index):
        return pl.BlockSpec((1, HALF, part_len, LANES), lambda n, i, s: (index, n, s[0], 0))

    stats = pl.BlockSpec((1, HALF, 1, part_len), lambda n, i, s: (given(i, s), n, 0, 0))
    sums = pl.BlockSpec((HALF, part_len, LANES), lambda n, i, s: (n, 0, 0))
    dense = pl.BlockSpec((part_len, features // 2), lambda n, i, s: (0, n))
    return pl.pallas_call(
        functools.partial(other_kernel, count - 1),
        name="back_other",
        grid_spec=pltpu.PrefetchScalarGridSpec(
            num_scalar_prefetch=1,
            grid=(HEADS // HALF, count - 1),
            in_specs=[
                pl.BlockSpec((1, HALF, part_len, LANES), lambda n, i, s: (0, n, theirs(i, s), 0)),
                pl.BlockSpec((HALF, part_len, LANES), lambda n, i, s: (n, theirs(i, s), 0)),
                own(1),
                own(2),
                pl.BlockSpec((part_len, LANES), lambda n, i, s: (s[0], 0)),
                pl.BlockSpec(
                    (1, part_len, features // 2), lambda n, i, s: (given(i, s), 0, n)
                ),
                stats,
                stats,
                sums,
                sums,
            ],
            out_specs=[dense, dense],
            scratch_shapes=[pltpu.VMEM((2, part_len, LANES), bf16)]
            + [pltpu.VMEM((HALF, part_len, LANES), f32)] * (2 if count > 2 else 0),
        ),
        out_shape=[
            jax.ShapeDtypeStruct((part_len, features), bf16),
            jax.ShapeDtypeStruct((part_len, features), bf16),
        ],
        compiler_params=params(("arbitrary", "arbitrary"), 60),
        cost_estimate=pl.CostEstimate(
            flops=4 * HEADS * part_len * (length - part_len) * LANES * 2,
            bytes_accessed=12 * HEADS * length * LANES,
            transcendentals=HEADS * part_len * (length - part_len),
        ),
    )(place, heads, aux, heads, heads, spots, grads, lses, inners, dk, dv)


def gelu_parts(hidden):
    size = jnp.abs(hidden) * (0.5**0.5)
    bell = jnp.exp2(hidden * hidden * (-0.5 * log2e))
    t = 1.0 / (1.0 + 0.3275911 * size)
    poly = t * (
        0.254829592
        + t * (-0.284496736 + t * (1.421413741 + t * (-1.453152027 + t * 1.061405429)))
    )
    tail = 0.5 * poly * bell
    cumulative = jnp.where(hidden < 0.0, tail, 1.0 - tail)
    return hidden * cumulative, cumulative + hidden * bell * 0.3989422804014327


def before_kernel(
    att_ref, x_ref, og_ref, wp_ref, bp_ref, dp_ref, up_ref, mask_ref, gain_ref, shift_ref,
    w2_ref, down1_ref, down2_ref, up2_ref,
    resid_ref, act_ref, midp_ref, mid1_ref, gm2_ref, grad_act_ref,
):
    mask = mask_ref[...]

    @pl.when(pl.program_id(0) == 0)
    def _():
        att = att_ref[...]
        midp_ref[...] = (dot_nn(att, dp_ref[...]) * mask).astype(bf16)
        branch = dot_nn(att, wp_ref[...]) + bp_ref[...]
        branch = branch + adapter_scale * dot_nt(midp_ref[...], up_ref[...])
        resid = x_ref[...].astype(f32) + branch
        resid_ref[...] = resid
        normed, _ = normalize(resid)
        act_ref[...] = (normed * gain_ref[...] + shift_ref[...]).astype(bf16)
        mid1_ref[...] = (dot_nn(act_ref[...], down1_ref[...]) * mask).astype(bf16)
        middle = adapter_scale * dot_nn(og_ref[...], up2_ref[...]) * mask
        gm2_ref[...] = middle.astype(bf16)

    grad_act_ref[...] = dot_nt(og_ref[...], w2_ref[...]) + dot_nt(gm2_ref[...], down2_ref[...])


def before_call(att, x, og, wp, bp, dp, up, mask, gain, shift, w2, down1, down2, up2):
    rows, features = att.shape
    wide = w2.shape[0]
    block = 1024

    def fixed(shape):
        zeros = (0,) * len(shape)
        return pl.BlockSpec(shape, lambda j: zeros, pipeline_mode=pl.Buffered(1))

    ins = [att, x, og, wp, bp, dp, up, mask, gain, shift, w2, down1, down2, up2]
    specs = [fixed(a.shape) for a in ins]
    specs[10] = pl.BlockSpec((block, features), lambda j: (j, 0))
    specs[12] = pl.BlockSpec((block, LANES), lambda j: (j, 0))
    shapes = [
        jax.ShapeDtypeStruct((rows, features), f32),
        jax.ShapeDtypeStruct((rows, features), bf16),
        jax.ShapeDtypeStruct((rows, LANES), bf16),
        jax.ShapeDtypeStruct((rows, LANES), bf16),
        jax.ShapeDtypeStruct((rows, LANES), bf16),
        jax.ShapeDtypeStruct((rows, wide), f32),
    ]
    return pl.pallas_call(
        before_kernel,
        name="before",
        grid=(wide // block,),
        in_specs=specs,
        out_specs=[fixed(a.shape) for a in shapes[:5]]
        + [pl.BlockSpec((rows, block), lambda j: (0, j))],
        out_shape=shapes,
        compiler_params=params(("arbitrary",), 56),
        cost_estimate=pl.CostEstimate(
            flops=2 * rows * features * (wide + features),
            bytes_accessed=2 * features * wide + 4 * rows * wide + 16 * rows * features,
            transcendentals=0,
        ),
    )(*ins)


def feed_kernel(
    act_ref, mid1_ref, gm2_ref, grad_act_ref, mask_ref, gain_ref,
    w1_ref, b1_ref, w2_ref, b2_ref, down1_ref, up1_ref, down2_ref, up2_ref,
    dp_ref, up_ref, midp_ref, sums_ref, *refs,
):
    late = refs[:4]
    (out_ref, grad_ref, grad_att_ref, inner_ref, gd1_ref, gu1_ref, gd2_ref, gu2_ref, gdp_ref,
     gup_ref) = refs[4:14]
    total, back, mid2_sum, gm1_sum, gm2_t, mid1_t, late_sem = refs[14:21]
    held = refs[21:]
    resid_ref, og_ref, att_ref, wp_ref = held

    step = pl.program_id(0)
    steps = pl.num_programs(0)
    mask = mask_ref[...]

    def copies():
        return [
            pltpu.make_async_copy(source, target, late_sem.at[index])
            for index, (source, target) in enumerate(zip(late, held))
        ]

    @pl.when(step == 0)
    def _():
        for copy in copies():
            copy.start()
        total[...] = jnp.zeros_like(total)
        back[...] = jnp.zeros_like(back)
        mid2_sum[...] = jnp.zeros_like(mid2_sum)
        gm1_sum[...] = jnp.zeros_like(gm1_sum)
        gm2_t[...] = chosen_rows(mask, gm2_ref[...])
        mid1_t[...] = chosen_rows(mask, mid1_ref[...])

    weight = w1_ref[...]
    hidden = dot_nn(act_ref[...], weight) + b1_ref[...]
    hidden = hidden + adapter_scale * dot_nt(mid1_ref[...], up1_ref[...])
    value, slope = gelu_parts(hidden)
    activated = value.astype(bf16)
    grad_hidden = (grad_act_ref[...] * slope).astype(bf16)
    total[...] += dot_nn(activated, w2_ref[...])
    mid2_sum[...] += dot_nn(activated, down2_ref[...])
    back[...] += dot_nt(grad_hidden, weight)
    gm1_sum[...] += dot_nn(grad_hidden, up1_ref[...])
    gd2_ref[...] = dot_nn(gm2_t[...], activated).astype(bf16)
    gu1_ref[...] = (adapter_scale * dot_nn(mid1_t[...], grad_hidden)).astype(bf16)

    @pl.when(step == steps - 1)
    def _():
        for copy in copies():
            copy.wait()
        mid2 = mid2_sum[...] * mask
        mid2_low = mid2.astype(bf16)
        resid = resid_ref[...]
        final = resid + total[...] + b2_ref[...]
        final = final + adapter_scale * dot_nt(mid2_low, up2_ref[...])
        out_ref[...] = final.astype(bf16)
        gm1 = adapter_scale * gm1_sum[...] * mask
        gm1_low = gm1.astype(bf16)
        upstream = back[...] + dot_nt(gm1_low, down1_ref[...])
        normed, inverse = normalize(resid)
        grad = og_ref[...].astype(f32) + norm_back(upstream * gain_ref[...], normed, inverse)
        grad_ref[...] = grad
        branch = grad.astype(bf16)
        gd1_ref[...] = dot_nn(chosen_rows(mask, gm1_low), act_ref[...]).astype(bf16)
        gu2_ref[...] = (adapter_scale * dot_nn(chosen_rows(mask, mid2_low), og_ref[...])).astype(bf16)
        middle = (adapter_scale * dot_nn(branch, up_ref[...]) * mask).astype(bf16)
        grad_att = dot_nt(branch, wp_ref[...]) + dot_nt(middle, dp_ref[...])
        grad_att_ref[...] = grad_att.astype(bf16)
        product = grad_att_ref[...].astype(f32) * att_ref[...].astype(f32)
        high = product.astype(bf16)
        low = (product - high.astype(f32)).astype(bf16)
        inner = dot_nt(sums_ref[...], high) + dot_nt(sums_ref[...], low)
        for head in range(HEADS):
            inner_ref[head] = inner[head : head + 1, :]
        gdp_ref[...] = dot_nn(chosen_rows(mask, middle), att_ref[...]).astype(bf16)
        own_t = chosen_rows(mask, midp_ref[...])
        gup_ref[...] = (adapter_scale * dot_nn(own_t, branch)).astype(bf16)


def feed_call(
    act, mid1, gm2, grad_act, mask, gain, w1, b1, w2, b2, down1, up1, down2, up2, dp, up, midp,
    sums, late,
):
    rows, features = act.shape
    wide = b1.shape[1]
    block = 512

    def fixed(shape):
        zeros = (0,) * len(shape)
        return pl.BlockSpec(shape, lambda j: zeros, pipeline_mode=pl.Buffered(1))

    def by_columns(height):
        return pl.BlockSpec((height, block), lambda j: (0, j))

    def by_rows(width):
        return pl.BlockSpec((block, width), lambda j: (j, 0))

    ins = [
        act, mid1, gm2, grad_act, mask, gain, w1, b1, w2, b2, down1, up1, down2, up2, dp, up,
        midp, sums,
    ]
    specs = [fixed(a.shape) for a in ins]
    specs[3] = by_columns(rows)
    specs[6] = by_columns(features)
    specs[7] = by_columns(1)
    specs[8] = by_rows(features)
    specs[11] = by_rows(LANES)
    specs[12] = by_rows(LANES)
    specs += [pl.BlockSpec(memory_space=pl.ANY)] * len(late)
    return pl.pallas_call(
        feed_kernel,
        name="feed",
        grid=(wide // block,),
        in_specs=specs,
        out_specs=[
            fixed((rows, features)),
            fixed((rows, features)),
            fixed((rows, features)),
            fixed((HEADS, 1, rows)),
            fixed((RANK, features)),
            by_columns(RANK),
            by_columns(RANK),
            fixed((RANK, features)),
            fixed((RANK, features)),
            fixed((RANK, features)),
        ],
        scratch_shapes=[
            pltpu.VMEM((rows, features), f32),
            pltpu.VMEM((rows, features), f32),
            pltpu.VMEM((rows, LANES), f32),
            pltpu.VMEM((rows, LANES), f32),
            pltpu.VMEM((RANK, rows), bf16),
            pltpu.VMEM((RANK, rows), bf16),
            pltpu.SemaphoreType.DMA((len(late),)),
        ]
        + [pltpu.VMEM(a.shape, a.dtype) for a in late],
        out_shape=[
            jax.ShapeDtypeStruct((rows, features), bf16),
            jax.ShapeDtypeStruct((rows, features), f32),
            jax.ShapeDtypeStruct((rows, features), bf16),
            jax.ShapeDtypeStruct((HEADS, 1, rows), f32),
            jax.ShapeDtypeStruct((RANK, features), bf16),
            jax.ShapeDtypeStruct((RANK, wide), bf16),
            jax.ShapeDtypeStruct((RANK, wide), bf16),
            jax.ShapeDtypeStruct((RANK, features), bf16),
            jax.ShapeDtypeStruct((RANK, features), bf16),
            jax.ShapeDtypeStruct((RANK, features), bf16),
        ],
        compiler_params=params(("arbitrary",), 60),
        cost_estimate=pl.CostEstimate(
            flops=6 * rows * features * wide,
            bytes_accessed=4 * features * wide + 4 * rows * wide + 24 * rows * features,
            transcendentals=2 * rows * wide,
        ),
    )(*ins, *late)


def close_kernel(
    shape, widths, dq_ref, dk_ref, dv_ref, weight_ref, down_ref, up_ref, mid_ref,
    mask_ref, x_ref, gain_ref, shift_ref, *refs,
):
    count, parts = shape
    devices = count * parts
    remote = courier_lines(dict(dp=count, seq=parts), []) is not None
    terms, refs = refs[:6], refs[6:]
    part_ref, out_ref = refs[:2]
    refs = refs[2:]
    total, grad_up, grad_down, stage = refs[:4]
    step = pl.program_id(0)
    features = x_ref.shape[1]
    if remote:
        landed, sends, arrivals = refs[4:]
        me = lax.axis_index("dp") * parts + lax.axis_index("seq")
        barrier = pltpu.get_barrier_semaphore()

        def peer(k):
            at = lax.rem(me + k, devices)
            return (at // parts, at % parts)

        def rows(at):
            return pl.ds(pl.multiple_of(at * RANK, RANK), RANK)

        def copy_to(k):
            at = lax.rem(me + k, devices)
            return pltpu.make_async_remote_copy(
                src_ref=stage.at[rows(at), :],
                dst_ref=landed.at[rows(me), :],
                send_sem=sends.at[k],
                recv_sem=arrivals.at[k],
                device_id=peer(k),
                device_id_type=pl.DeviceIdType.MESH,
            )

    @pl.when(step == 0)
    def _():
        if remote:

            def greet(k, carry):
                pl.semaphore_signal(
                    barrier, inc=1, device_id=peer(k), device_id_type=pl.DeviceIdType.MESH
                )
                return carry

            lax.fori_loop(1, devices, greet, 0)
        total[...] = jnp.zeros_like(total)
        own_t = chosen_rows(mask_ref[...], mid_ref[...])
        middle = jnp.zeros((x_ref.shape[0], LANES), f32)
        for index, source in enumerate((dq_ref, dk_ref, dv_ref)):
            at = pl.ds(index * features, features)
            middle += dot_nn(source[...], up_ref[at, :])
            grad_up[:, at] = (adapter_scale * dot_nn(own_t, source[...])).astype(bf16)
        middle = (adapter_scale * middle * mask_ref[...]).astype(bf16)
        normed, _ = normalize(x_ref[...].astype(f32))
        act = (normed * gain_ref[...].astype(f32) + shift_ref[...].astype(f32)).astype(bf16)
        total[...] = dot_nt(middle, down_ref[...])
        grad_down[...] = dot_nn(chosen_rows(mask_ref[...], middle), act).astype(bf16)
        at = 0
        for source, width in zip((grad_down, *terms[:3], grad_up, *terms[3:]), widths):
            for device in range(devices):
                stage[device * RANK : (device + 1) * RANK, at : at + width] = source[
                    :, device * width : (device + 1) * width
                ]
            at += width
        if remote:
            pl.semaphore_wait(barrier, devices - 1)

            def send(k, carry):
                copy_to(k).start()
                return carry

            lax.fori_loop(1, devices, send, 0)
            landed[rows(me), :] = stage[rows(me), :]
        else:
            out_ref[...] = stage[...]

    for index, source in enumerate((dq_ref, dk_ref, dv_ref)):

        @pl.when(step == index)
        def _():
            total[...] += dot_nt(source[...], weight_ref[...])

    @pl.when(step == 2)
    def _():
        part_ref[...] = total[...]
        if remote:

            def wait(k, carry):
                copy_to(k).wait()
                return carry

            lax.fori_loop(1, devices, wait, 0)
            out_ref[...] = landed[...]


def close_call(
    mesh_shape, widths, dq, dk, dv, weight, down, up, mid, mask, x, gain, shift, terms,
):
    rows, features = dq.shape
    devices = mesh_shape["dp"] * mesh_shape["seq"]
    remote = courier_lines(mesh_shape, []) is not None
    span = sum(widths)

    def fixed(shape):
        zeros = (0,) * len(shape)
        return pl.BlockSpec(shape, lambda j: zeros, pipeline_mode=pl.Buffered(1))

    ins = [dq, dk, dv, weight, down, up, mid, mask, x, gain, shift, *terms]
    specs = [fixed(a.shape) for a in ins]
    specs[3] = pl.BlockSpec((features, features), lambda j: (0, j))
    shapes = [
        jax.ShapeDtypeStruct((rows, features), f32),
        jax.ShapeDtypeStruct((devices * RANK, span), bf16),
    ]
    scratch = [
        pltpu.VMEM((rows, features), f32),
        pltpu.VMEM((RANK, 3 * features), bf16),
        pltpu.VMEM((RANK, features), bf16),
        pltpu.VMEM((devices * RANK, span), bf16),
    ]
    options = {}
    if remote:
        scratch += [
            pltpu.VMEM((devices * RANK, span), bf16),
            pltpu.SemaphoreType.DMA((devices,)),
            pltpu.SemaphoreType.DMA((devices,)),
        ]
        options = dict(collective_id=4, has_side_effects=True)
    out = pl.pallas_call(
        functools.partial(close_kernel, (mesh_shape["dp"], mesh_shape["seq"]), widths),
        name="close",
        grid=(3,),
        in_specs=specs,
        out_specs=[fixed(a.shape) for a in shapes],
        scratch_shapes=scratch,
        out_shape=shapes,
        compiler_params=pltpu.CompilerParams(
            dimension_semantics=("arbitrary",), vmem_limit_bytes=56 * 1024 * 1024, **options
        ),
        cost_estimate=pl.CostEstimate(
            flops=6 * rows * features * features,
            bytes_accessed=6 * features * features + 20 * rows * features,
            transcendentals=0,
        ),
    )(*ins)
    if remote:
        return out
    landed = lax.all_to_all(
        out[1].reshape(devices, RANK, span), ("dp", "seq"), 0, 0, tiled=True
    ).reshape(devices * RANK, span)
    return out[0], landed


def last_kernel(
    devices, widths, upstream_ref, x_ref, gain_ref, resid_ref, landed_ref, packs_ref, out_ref,
    *grads,
):
    normed, inverse = normalize(x_ref[...].astype(f32))
    out_ref[...] = resid_ref[...] + norm_back(
        upstream_ref[...] * gain_ref[...].astype(f32), normed, inverse
    )

    @pl.when(pl.program_id(0) == 0)
    def _():
        every = packs_ref.shape[0]
        row = lax.broadcasted_iota(jnp.int32, (devices * RANK, every), 0)
        column = lax.broadcasted_iota(jnp.int32, (devices * RANK, every), 1)
        chosen = (column == row // RANK * (every // devices) + VECTORS).astype(bf16)
        adapter = dot_nn(chosen, packs_ref[:, :LANES])[:, 0:1]
        row = lax.broadcasted_iota(jnp.int32, (devices * RANK, LANES), 0)
        column = lax.broadcasted_iota(jnp.int32, (devices * RANK, LANES), 1)
        same = (column // RANK).astype(f32) == adapter
        spread = jnp.where(same & (row % RANK == column % RANK), 1.0, 0.0).astype(bf16)
        sums = dot_tn(landed_ref[...], spread)
        at = 0
        for target, width in zip(grads, widths):
            target[...] = sums[at : at + width, :]
            at += width


def last_call(devices, widths, upstream, x, gain, resid, landed, packs):
    rows, features = x.shape
    tall = rows // 4 if rows % 64 == 0 else rows
    by_rows = pl.BlockSpec((tall, features), lambda i: (i, 0))
    return pl.pallas_call(
        functools.partial(last_kernel, devices, widths),
        name="last",
        grid=(rows // tall,),
        in_specs=[
            by_rows,
            by_rows,
            whole((1, features)),
            by_rows,
            whole(landed.shape),
            whole(packs.shape),
        ],
        out_specs=[by_rows] + [whole((width, LANES)) for width in widths],
        out_shape=[jax.ShapeDtypeStruct((rows, features), f32)]
        + [jax.ShapeDtypeStruct((width, LANES), f32) for width in widths],
        compiler_params=params(("arbitrary",), 50),
    )(upstream, x, gain, resid, landed, packs)


def position_tables(rel_h, rel_w, length):
    wide = ((0, LANES // 2 - (2 * G - 1)), (0, LANES - HEAD_DIM))
    h = jnp.pad(rel_h, wide)
    w = jnp.pad(rel_w, wide)
    h_back = jnp.pad(rel_h[::-1], wide)
    w_back = jnp.pad(rel_w[::-1], wide)
    forward = jnp.concatenate([h_back, h_back, w_back, w_back], axis=0).T
    backward = jnp.concatenate([h, w], axis=0)
    spot = np.arange(length)[:, None]
    lane = np.arange(LANES)[None, :]
    at = np.where((lane // G) % 2 == 0, spot // G, spot % G)
    spots = jnp.asarray(lane % G == at, bf16)
    turned = jnp.asarray(lane % G == G - 1 - at, bf16)
    return forward, backward, spots, turned


def vectors_kernel(devices, sizes, source, target):
    rows = source.shape[0] // devices
    target[...] = jnp.zeros_like(target)
    packs = source[...].astype(f32)
    for line, size in enumerate(sizes):
        for device in range(devices):
            at = device * rows + line
            target[line : line + 1, device * size : (device + 1) * size] = packs[
                at : at + 1, 0:size
            ]


def vectors_call(gathered, devices, sizes):
    return pl.pallas_call(
        functools.partial(vectors_kernel, devices, sizes),
        name="vectors",
        out_shape=jax.ShapeDtypeStruct((VECTORS, devices * max(sizes)), f32),
        compiler_params=params(None, 16),
    )(gathered)


def per_device(
    mesh_shape,
    tokens,
    adapter_index,
    norm1_gain,
    norm1_bias,
    qkv_weight,
    qkv_bias,
    proj_weight,
    proj_bias,
    norm2_gain,
    norm2_bias,
    fc1_weight,
    fc1_bias,
    fc2_weight,
    fc2_bias,
    rel_pos_h,
    rel_pos_w,
    qkv_down,
    qkv_up,
    proj_down,
    proj_up,
    fc1_down,
    fc1_up,
    fc2_down,
    fc2_up,
    out_grad,
):
    axes = ("dp", "seq")
    part_count = mesh_shape["seq"]
    devices = mesh_shape["dp"] * part_count
    images, part_len, features = tokens.shape
    length = part_len * part_count
    own_tokens = tokens[0]
    og = out_grad[0]
    place = lax.axis_index("seq").astype(jnp.int32).reshape(1)

    small = [
        norm1_gain, norm1_bias, qkv_bias, proj_bias, norm2_gain, norm2_bias, fc1_bias, fc2_bias,
        adapter_index.astype(bf16),
    ]
    sizes = [a.shape[0] for a in small]
    pack = jnp.concatenate([jnp.pad(a, (0, 2 * LANES - a.shape[0])) for a in small])
    pack = jnp.pad(pack.reshape(len(small), 2 * LANES), ((0, 16 - len(small)), (0, 0)))

    columns = jnp.arange(LANES, dtype=jnp.int32) // RANK
    mask = (columns[None, :] == adapter_index[:, None]).astype(f32)
    forward_table, back_table, spots, turned_spots = position_tables(rel_pos_h, rel_pos_w, length)
    head_of = np.arange(features)[None, :] // HEAD_DIM
    head_sums = jnp.asarray(head_of == np.arange(HEADS)[:, None], bf16)

    w_fc2 = lax.all_gather(fc2_weight, axes, axis=0, tiled=True)
    w_fc1 = lax.all_gather(fc1_weight, axes, axis=0, tiled=True)
    (w_qkv, d_qkv, u_qkv, all_small), image_tokens = collect(
        mesh_shape, [qkv_weight, qkv_down, qkv_up.T, pack], own_tokens
    )
    vectors = vectors_call(all_small, devices, sizes[:VECTORS])
    g1, s1, b_qkv, b_proj, g2, s2, b_fc1, b_fc2 = (
        vectors[i : i + 1, : devices * sizes[i]] for i in range(VECTORS)
    )
    (heads, mid_qkv, att, lse, aux), rest = front_call(
        mesh_shape, part_len, image_tokens, g1, s1, w_qkv, b_qkv, d_qkv, u_qkv, mask,
        forward_table, spots,
        [proj_weight, proj_down, fc1_down, fc2_down, proj_up.T, fc1_up.T, fc2_up.T],
    )
    w_proj, d_proj, d_fc1, d_fc2, u_proj, u_fc1, u_fc2 = rest
    resid, act_two, mid_proj, mid_fc1, gm_fc2, grad_act = before_call(
        att, own_tokens, og, w_proj, b_proj, d_proj, u_proj, mask, g2, s2, w_fc2, d_fc1, d_fc2,
        u_fc2,
    )
    (block_out, grad_resid, grad_att, inner, gd_fc1, gu_fc1, gd_fc2, gu_fc2, gd_proj,
     gu_proj) = feed_call(
        act_two, mid_fc1, gm_fc2, grad_act, mask, g2, w_fc1, b_fc1, w_fc2, b_fc2, d_fc1, u_fc1,
        d_fc2, u_fc2, d_proj, u_proj, mid_proj, head_sums, [resid, og, att, w_proj],
    )
    if part_count == 2:
        swap = [(0, 1), (1, 0)]
        their_grad, their_lse, their_inner = (
            lax.ppermute(a, "seq", swap)[None] for a in (grad_att, lse, inner)
        )
    else:
        their_grad, their_lse, their_inner = (
            lax.all_gather(a, "seq", axis=0) for a in (grad_att, lse, inner)
        )
    dq, dk_own, dv_own = own_call(
        place, heads, aux, spots, turned_spots, back_table, grad_att, lse, inner
    )
    dk, dv = other_call(
        place, heads, aux, spots, their_grad, their_lse, their_inner, dk_own, dv_own
    )
    mid_own = lax.dynamic_slice_in_dim(mid_qkv, place[0] * part_len, part_len, 0)
    widths = [a.shape[0] for a in (qkv_down, proj_down, fc1_down, fc2_down)]
    widths += [a.shape[1] for a in (qkv_up, proj_up, fc1_up, fc2_up)]
    upstream, landed = close_call(
        mesh_shape, widths, dq, dk, dv, w_qkv, d_qkv, u_qkv, mid_own, mask, own_tokens, g1, s1,
        [gd_proj, gd_fc1, gd_fc2, gu_proj, gu_fc1, gu_fc2],
    )
    input_grad, *grads = last_call(
        devices, widths, upstream, own_tokens, g1, grad_resid, landed, all_small
    )
    return (
        block_out[None],
        input_grad[None],
        grads[0],
        grads[4].T,
        grads[1],
        grads[5].T,
        grads[2],
        grads[6].T,
        grads[3],
        grads[7].T,
    )


def solution(mesh):
    both = ("dp", "seq")
    return jax.shard_map(
        functools.partial(per_device, dict(mesh.shape)),
        mesh=mesh,
        in_specs=(
            P("dp", "seq", None),
            P("dp"),
            P(both),
            P(both),
            P(both, None),
            P(both),
            P(both, None),
            P(both),
            P(both),
            P(both),
            P(both, None),
            P(both),
            P(both, None),
            P(both),
            P(),
            P(),
            P(both, None),
            P(None, both),
            P(both, None),
            P(None, both),
            P(both, None),
            P(None, both),
            P(both, None),
            P(None, both),
            P("dp", "seq", None),
        ),
        out_specs=(
            P("dp", "seq", None),
            P("dp", "seq", None),
            P(both, None),
            P(None, both),
            P(both, None),
            P(None, both),
            P(both, None),
            P(None, both),
            P(both, None),
            P(None, both),
        ),
        check_vma=False,
    )
```

```python
import functools

import jax
import jax.numpy as jnp
import numpy as np
from jax import lax
from jax.experimental import pallas as pl
from jax.experimental.pallas import tpu as pltpu
from jax.sharding import PartitionSpec as P

HEADS = 16
HEAD_DIM = 80
ADAPTERS = 8
RANK = 16
G = 32
LANES = 128
VECTORS = 8
HALF = HEADS // 2

epsilon = 1e-06
adapter_scale = 0.5
log2e = 1.4426950408889634
score_scale = HEAD_DIM ** (-0.5)
exponent_scale = score_scale * log2e
f32 = jnp.float32
bf16 = jnp.bfloat16


def dot_nn(left, right):
    return lax.dot_general(left, right, (((1,), (0,)), ((), ())), preferred_element_type=f32)


def dot_nt(left, right):
    return lax.dot_general(left, right, (((1,), (1,)), ((), ())), preferred_element_type=f32)


def dot_tn(left, right):
    return lax.dot_general(left, right, (((0,), (0,)), ((), ())), preferred_element_type=f32)


def normalize(values):
    average = jnp.mean(values, axis=-1, keepdims=True)
    centered = values - average
    variance = jnp.mean(centered * centered, axis=-1, keepdims=True)
    inverse = lax.rsqrt(variance + epsilon)
    return centered * inverse, inverse


def norm_back(scaled, normed, inverse):
    return inverse * (
        scaled
        - jnp.mean(scaled, axis=-1, keepdims=True)
        - normed * jnp.mean(scaled * normed, axis=-1, keepdims=True)
    )


def chosen_rows(mask, middle):
    rank = lax.broadcasted_iota(jnp.int32, (RANK, LANES), 0)
    column = lax.broadcasted_iota(jnp.int32, (RANK, LANES), 1)
    pick = jnp.where(column % RANK == rank, jnp.broadcast_to(mask, (RANK, LANES)), 0.0)
    return dot_nt(pick.astype(bf16), middle).astype(bf16)


def params(semantics, megabytes):
    return pltpu.CompilerParams(
        dimension_semantics=semantics, vmem_limit_bytes=megabytes * 1024 * 1024
    )


def whole(shape):
    zeros = (0,) * len(shape)
    return pl.BlockSpec(shape, lambda *_: zeros)


Z, X, Y, S, XD, YD, SX, SY, SD = range(9)


class Courier:
    def __init__(self, lines, chunks, rows_of, sources, targets, local, sends, arrivals):
        self.lines = lines
        self.chunks = chunks
        self.rows_of = rows_of
        self.sources, self.targets = sources, targets
        self.local, self.sends, self.arrivals = local, sends, arrivals
        dp = lax.axis_index("dp")
        self.seq = lax.axis_index("seq")
        self.dp = dp
        self.line, self.column, self.core = dp // 4, (dp // 2) % 2, dp % 2
        line, column, core, seq = self.line, self.column, self.core, self.seq
        self.ahead = [
            self.device(lax.rem(line + k, lines), column, core, seq) for k in range(1, lines)
        ]
        self.across = self.device(line, 1 - column, core, seq)
        self.partner = self.device(line, column, core, 1 - seq)
        self.sibling = self.device(line, column, 1 - core, seq)

    @staticmethod
    def device(z, x, c, y):
        return (z * 4 + x * 2 + c, y)

    def owner(self, k, x, c, y):
        return self.device(lax.rem(self.line + self.lines - k, self.lines), x, c, y)

    def greet(self):
        peers = self.ahead + [self.across, self.partner, self.sibling]
        barrier = pltpu.get_barrier_semaphore()
        for peer in peers:
            pl.semaphore_signal(
                barrier, inc=1, device_id=peer, device_id_type=pl.DeviceIdType.MESH
            )
        pl.semaphore_wait(barrier, len(peers))

    def slot(self, number, kind, k):
        return (number * 9 + kind) * self.lines + k

    def part(self, number, half):
        _, row, height, col, width, share = self.chunks[number]
        if half is None:
            return row, height, col, width
        if width >= 2 * LANES:
            cut = width // LANES * share // 4 * LANES
            return (row, height, col, cut) if half == 0 else (row, height, col + cut, width - cut)
        cut = height // 8 * share // 4 * 8
        return (row, cut, col, width) if half == 0 else (row + cut, height - cut, col, width)

    def place(self, number, owner, half=None):
        array = self.chunks[number][0]
        row, height, col, width = self.part(number, half)
        if height == 0 or width == 0:
            return None
        start = (owner[0] * 2 + owner[1]) * self.rows_of[array] + row
        return self.targets[array].at[pl.ds(pl.multiple_of(start, 8), height), pl.ds(col, width)]

    def like(self, number, half=None):
        array = self.chunks[number][0]
        row, height, col, width = self.part(number, half)
        if height == 0 or width == 0:
            return None
        return self.targets[array].at[pl.ds(row, height), pl.ds(col, width)]

    def send(self, source, target, peer, number, kind, k):
        at = self.slot(number, kind, k)
        pltpu.make_async_remote_copy(
            src_ref=source,
            dst_ref=target,
            send_sem=self.sends.at[at],
            recv_sem=self.arrivals.at[at],
            device_id=peer,
            device_id_type=pl.DeviceIdType.MESH,
        ).start()

    def arrive(self, place, number, kind, k):
        pltpu.make_async_copy(place, place, self.arrivals.at[self.slot(number, kind, k)]).wait()

    def start(self, number):
        array, row, height, col, width, _ = self.chunks[number]
        own = self.sources[array].at[pl.ds(row, height), pl.ds(col, width)]
        place = self.place(number, (self.dp, self.seq))
        for k in range(1, self.lines):
            self.send(own, place, self.ahead[k - 1], number, Z, k)
        self.send(own, place, self.across, number, X, 0)
        self.send(own, place, self.partner, number, Y, 0)
        self.send(own, place, self.sibling, number, S, 0)
        pltpu.make_async_copy(own, place, self.local.at[number]).start()

    def stage_one(self, number, k):
        place = self.place(number, self.owner(k, self.column, self.core, self.seq))
        self.arrive(place, number, Z, k)
        self.send(place, place, self.across, number, X, k)
        self.send(place, place, self.partner, number, Y, k)
        self.send(place, place, self.sibling, number, S, k)

    def stage_two(self, number, k):
        owner = self.owner(k, 1 - self.column, self.core, self.seq)
        place = self.place(number, owner)
        self.arrive(place, number, X, k)
        half = self.place(number, owner, 0)
        if half is not None:
            self.send(half, half, self.partner, number, YD, k)
        self.send(place, place, self.sibling, number, SX, k)
        owner = self.owner(k, self.column, self.core, 1 - self.seq)
        place = self.place(number, owner)
        self.arrive(place, number, Y, k)
        half = self.place(number, owner, 1)
        if half is not None:
            self.send(half, half, self.across, number, XD, k)
        self.send(place, place, self.sibling, number, SY, k)

    def stage_three(self, number, k):
        owner = self.owner(k, 1 - self.column, self.core, 1 - self.seq)
        for half, kind in ((0, YD), (1, XD)):
            piece = self.place(number, owner, half)
            if piece is not None:
                self.arrive(piece, number, kind, k)
        place = self.place(number, owner)
        self.send(place, place, self.sibling, number, SD, k)

    def stage_four(self, number, k):
        for kind, x, y in (
            (S, self.column, self.seq),
            (SX, 1 - self.column, self.seq),
            (SY, self.column, 1 - self.seq),
            (SD, 1 - self.column, 1 - self.seq),
        ):
            place = self.place(number, self.owner(k, x, 1 - self.core, y))
            self.arrive(place, number, kind, k)

    def steps(self):
        stages = (self.stage_one, self.stage_two, self.stage_three, self.stage_four)
        order = []
        for tick in range(len(self.chunks) + 3):
            for lag, stage in enumerate(stages):
                if 0 <= tick - lag < len(self.chunks):
                    for k in range(1 if lag == 0 else 0, self.lines):
                        order.append(functools.partial(stage, tick - lag, k))
        return order

    def finish(self):
        for number in range(len(self.chunks)):
            like = self.like(number)
            pltpu.make_async_copy(like, like, self.local.at[number]).wait()
            for kind in range(9):
                half = {YD: 0, XD: 1}.get(kind)
                like = self.like(number, half)
                for k in range(self.lines):
                    if like is not None and not (kind == Z and k == 0):
                        sem = self.sends.at[self.slot(number, kind, k)]
                        pltpu.make_async_copy(like, like, sem).wait()


def cut_chunks(arrays, share=2):
    chunks = []
    for index, array in enumerate(arrays):
        height, width = array.shape
        wide, tall = width, height
        if height * wide * 2 > 120_000 and wide > 1280:
            wide = next(w for w in range(1280, 0, -LANES) if width % w == 0)
        while tall * wide * 2 > 120_000 and tall % 16 == 0:
            tall //= 2
        for row in range(0, height, tall):
            for col in range(0, width, wide):
                chunks.append((index, row, tall, col, wide, share))
    return chunks


def courier_lines(mesh_shape, arrays):
    lines = mesh_shape["dp"] // 4
    fits = mesh_shape["seq"] == 2 and mesh_shape["dp"] == 4 * lines and 2 <= lines <= 4
    return lines if fits and not any(a.shape[0] % 8 for a in arrays) else None


def courier_scratch(lines, chunks):
    slots = len(chunks) * 9 * lines
    return [
        pltpu.SemaphoreType.DMA((len(chunks),)),
        pltpu.SemaphoreType.DMA((slots,)),
        pltpu.SemaphoreType.DMA((slots,)),
    ]


def gathered_shapes(devices, arrays):
    return [jax.ShapeDtypeStruct((devices * a.shape[0], a.shape[1]), a.dtype) for a in arrays]


def collect_kernel(lines, chunks, rows_of, count, *refs):
    courier = Courier(lines, chunks, rows_of, refs[:count], refs[count : 2 * count], *refs[2 * count :])
    courier.greet()
    for number in range(len(chunks)):
        courier.start(number)
    for step in courier.steps():
        step()
    courier.finish()


def collect(mesh_shape, arrays):
    lines = courier_lines(mesh_shape, arrays)
    if lines is None:
        return [lax.all_gather(a, ("dp", "seq"), axis=0, tiled=True) for a in arrays]
    chunks = cut_chunks(arrays, 2)
    anywhere = pl.BlockSpec(memory_space=pl.ANY)
    count = len(arrays)
    size = sum(a.size for a in arrays)
    return pl.pallas_call(
        functools.partial(collect_kernel, lines, chunks, [a.shape[0] for a in arrays], count),
        name="collect",
        in_specs=[anywhere] * count,
        out_specs=[anywhere] * count,
        out_shape=gathered_shapes(mesh_shape["dp"] * 2, arrays),
        scratch_shapes=courier_scratch(lines, chunks),
        compiler_params=pltpu.CompilerParams(collective_id=1, has_side_effects=True),
        cost_estimate=pl.CostEstimate(
            flops=0, bytes_accessed=64 * mesh_shape["dp"] * size, transcendentals=0
        ),
    )(*arrays)


def qkv_part(part, blocks, gain_ref, shift_ref, weight_ref, bias_ref, down_ref, up_ref, mask_ref,
             heads, mid_ref, act_ref, pause):
    length = act_ref.shape[0]

    @pl.when(part == 0)
    def _():
        part_len = length // len(blocks)
        for index, block in enumerate(blocks):
            place = 0
            if len(blocks) == 2:
                seq = lax.axis_index("seq")
                place = pl.multiple_of((seq if index == 0 else 1 - seq) * part_len, G)
            normed, _ = normalize(block[...].astype(f32))
            act = normed * gain_ref[...].astype(f32) + shift_ref[...].astype(f32)
            act_ref[pl.ds(place, part_len), :] = act.astype(bf16)
        mid_ref[...] = (dot_nn(act_ref[...], down_ref[...]) * mask_ref[...]).astype(bf16)

    rows = min(256, length)
    lane = lax.broadcasted_iota(jnp.int32, (rows, LANES - HEAD_DIM), 1)
    pad = jnp.where((lane == 0) & (part == 2), 1.0, 0.0).astype(bf16)
    for start in range(0, length, rows):
        here = pl.ds(start, rows)
        block = dot_nn(act_ref[here, :], weight_ref[...])
        block = block + bias_ref[...].astype(f32)
        block = block + adapter_scale * dot_nt(mid_ref[here, :], up_ref[...])
        block = block.astype(bf16)
        for head in range(HEADS):
            heads[part, head, here, 0:HEAD_DIM] = block[:, head * HEAD_DIM : (head + 1) * HEAD_DIM]
            heads[part, head, here, HEAD_DIM:LANES] = pad
        pause(start // rows)


def attend_head(head, own, heads, table_ref, spots_ref, att_ref, lse_ref, aux_ref, pause):
    pause(0)
    length = heads.shape[2]
    part_len = att_ref.shape[0]
    lane = lax.broadcasted_iota(jnp.int32, (G, LANES), 1)
    first = lane < LANES // 2
    even = (lane // G) % 2 == 0
    raw = dot_nn(heads[0, head], table_ref[...]) * (HEAD_DIM**0.5)
    for row in range(length // G):
        block = raw[row * G : (row + 1) * G, :]
        high = block.astype(bf16).astype(f32)
        mixed_h = jnp.where(first, high[:, :LANES], block[:, :LANES] - high[:, :LANES])
        mixed_w = jnp.where(first, high[:, LANES:], block[:, LANES:] - high[:, LANES:])
        along_h = pltpu.roll(mixed_h, LANES - G + 1 + row, 1)
        along_w = pltpu.roll(mixed_w, 1, 1, stride=1, stride_axis=0)
        aux_ref[0, pl.ds(row * G, G), :] = jnp.where(even, along_h, along_w).astype(bf16)
    pause(1)
    left = jnp.concatenate([heads[0, head, own, :], aux_ref[0, own, :]], axis=1)
    right = jnp.concatenate([heads[1, head], spots_ref[...]], axis=1)
    scores = dot_nt(left, right)
    top = jnp.max(scores, axis=1, keepdims=True)
    shares = jnp.exp2((scores - top) * exponent_scale).astype(bf16)
    mixed = dot_nn(shares, heads[2, head])
    total = mixed[:, HEAD_DIM : HEAD_DIM + 1]
    att = (mixed[:, :HEAD_DIM] / total).astype(bf16)
    logs = top * exponent_scale + jnp.log2(total)
    lse_ref[0] = jnp.transpose(jnp.broadcast_to(logs, (part_len, LANES)))[0:1, :]
    for slot in range(HALF):

        @pl.when(head % HALF == slot)
        def _():
            att_ref[:, slot * HEAD_DIM : (slot + 1) * HEAD_DIM] = att


def front_kernel(
    lines, chunks, rows_of, count, pair,
    gain_ref, shift_ref, weight_ref, bias_ref, down_ref, up_ref, mask_ref, table_ref,
    spots_ref, *refs,
):
    blocks, refs = refs[:pair], refs[pair:]
    sources = refs[:count]
    heads_out, mid_ref, att_ref, lse_ref, aux_ref = refs[count : count + 5]
    targets = refs[count + 5 : 2 * count + 5]
    heads, act_ref, out_sem = refs[2 * count + 5 : 2 * count + 8]
    step = pl.program_id(0)
    last = pl.num_programs(0) - 1
    courier = None
    plan = {}
    if count:
        courier = Courier(lines, chunks, rows_of, sources, targets, *refs[2 * count + 8 :])

        @pl.when(step == 0)
        def _():
            courier.greet()
            for number in range(len(chunks)):
                courier.start(number)

        pieces = act_ref.shape[0] // min(256, act_ref.shape[0])
        places = [(part, piece, 7.0 / pieces) for part in range(3) for piece in range(pieces)]
        places += [(3 + head, piece, 1.0) for head in range(HEADS) for piece in range(2)]
        work = courier.steps()
        whole_time = sum(p[2] for p in places)
        done, spent = 0, 0.0
        for at, piece, time in places:
            spent += time
            upto = min(len(work), int(len(work) * spent / whole_time + 1e-6))
            plan[at, piece] = work[done:upto]
            done = upto

    def pause(first, count_of):
        def run(piece):
            for at in range(first, first + count_of):
                items = plan.get((at, piece))
                if items:

                    @pl.when(step == at)
                    def _():
                        for item in items:
                            item()

        return run

    @pl.when(step < 3)
    def _():
        qkv_part(
            step, blocks, gain_ref, shift_ref, weight_ref, bias_ref, down_ref, up_ref, mask_ref,
            heads, mid_ref, act_ref, pause(0, 3),
        )
        pltpu.make_async_copy(heads.at[step], heads_out.at[step], out_sem.at[step]).start()

    part_len = att_ref.shape[0]
    own = pl.ds(pl.multiple_of(lax.axis_index("seq") * part_len, G), part_len)

    @pl.when(step >= 3)
    def _():
        attend_head(
            step - 3, own, heads, table_ref, spots_ref, att_ref, lse_ref, aux_ref, pause(3, HEADS)
        )

    @pl.when(step == last)
    def _():
        for part in range(3):
            pltpu.make_async_copy(heads.at[part], heads_out.at[part], out_sem.at[part]).wait()
        if courier is not None:
            courier.finish()


def front_call(
    mesh_shape, part_len, tokens, gain, shift, weight, bias, down, up, mask, table, spots, arrays
):
    length = sum(t.shape[0] for t in tokens)
    features = weight.shape[0]
    lines = courier_lines(mesh_shape, arrays)
    later = []
    if lines is None:
        axes = ("dp", "seq")
        later = [lax.all_gather(a, axes, axis=0, tiled=True) for a in arrays]
        arrays = []
    chunks = cut_chunks(arrays)
    count = len(arrays)
    anywhere = pl.BlockSpec(memory_space=pl.ANY)

    def head(i):
        return jnp.maximum(i - 3, 0)

    def part(i):
        return jnp.minimum(i, 2)

    def fixed(shape):
        zeros = (0,) * len(shape)
        return pl.BlockSpec(shape, lambda i: zeros, pipeline_mode=pl.Buffered(1))

    options = dict(collective_id=2, has_side_effects=True) if count else {}
    out = pl.pallas_call(
        functools.partial(
            front_kernel, lines, chunks, [a.shape[0] for a in arrays], count, len(tokens)
        ),
        name="front",
        grid=(3 + HEADS,),
        in_specs=[
            fixed((1, features)),
            fixed((1, features)),
            pl.BlockSpec((features, features), lambda i: (0, part(i))),
            pl.BlockSpec((1, features), lambda i: (0, part(i))),
            fixed((features, LANES)),
            pl.BlockSpec((features, LANES), lambda i: (part(i), 0)),
            fixed((1, LANES)),
            fixed((LANES, 2 * LANES)),
            fixed((length, LANES)),
        ]
        + [fixed(t.shape) for t in tokens]
        + [anywhere] * count,
        out_specs=[
            anywhere,
            whole((length, LANES)),
            pl.BlockSpec((part_len, features // 2), lambda i: (0, head(i) // HALF)),
            pl.BlockSpec((1, 1, part_len), lambda i: (head(i), 0, 0)),
            pl.BlockSpec((1, length, LANES), lambda i: (head(i), 0, 0)),
        ]
        + [anywhere] * count,
        out_shape=[
            jax.ShapeDtypeStruct((3, HEADS, length, LANES), bf16),
            jax.ShapeDtypeStruct((length, LANES), bf16),
            jax.ShapeDtypeStruct((part_len, features), bf16),
            jax.ShapeDtypeStruct((HEADS, 1, part_len), f32),
            jax.ShapeDtypeStruct((HEADS, length, LANES), bf16),
        ]
        + gathered_shapes(mesh_shape["dp"] * mesh_shape["seq"], arrays),
        scratch_shapes=[
            pltpu.VMEM((3, HEADS, length, LANES), bf16),
            pltpu.VMEM((length, features), bf16),
            pltpu.SemaphoreType.DMA((3,)),
        ]
        + (courier_scratch(lines, chunks) if count else []),
        compiler_params=pltpu.CompilerParams(
            dimension_semantics=("arbitrary",), vmem_limit_bytes=58 * 1024 * 1024, **options
        ),
        cost_estimate=pl.CostEstimate(
            flops=6 * length * features * features
            + 8 * HEADS * part_len * length * LANES,
            bytes_accessed=2 * (3 * features * features + 8 * length * features),
            transcendentals=HEADS * part_len * length,
        ),
    )(gain, shift, weight, bias, down, up, mask, table, spots, *tokens, *arrays)
    return out[:5], list(out[5:]) + later


def own_kernel(
    place_ref, q_ref, aux_ref, k_ref, v_ref, spots_ref, turned_spots_ref, table_ref, grad_ref,
    lse_ref, inner_ref, dq_ref, dk_ref, dv_ref, shares_ref, dscores_ref, padded,
):
    part_len = q_ref.shape[2]
    lane = lax.broadcasted_iota(jnp.int32, (G, LANES), 1)
    start = place_ref[0] * (part_len // G)
    here = pl.ds(pl.multiple_of(place_ref[0] * part_len, G), part_len)
    for slot in range(HALF):
        cols = slice(slot * HEAD_DIM, (slot + 1) * HEAD_DIM)
        spare = slot % 2
        padded[spare, :, HEAD_DIM:LANES] = jnp.zeros((part_len, LANES - HEAD_DIM), bf16)
        padded[spare, :, 0:HEAD_DIM] = grad_ref[:, cols]
        queries = q_ref[0, slot]
        keys = k_ref[0, slot]
        left = jnp.concatenate([keys, spots_ref[...]], axis=1)
        right = jnp.concatenate([queries, aux_ref[slot]], axis=1)
        shares = jnp.exp2(dot_nt(left, right) * exponent_scale - lse_ref[slot])
        grad_shares = dot_nt(v_ref[0, slot], padded[spare])
        shares_ref[spare] = shares.astype(bf16)
        dscores_ref[spare] = (shares * (grad_shares - inner_ref[slot])).astype(bf16)
        flat = dot_tn(
            jnp.concatenate([keys, turned_spots_ref[...]], axis=1), dscores_ref[spare]
        )
        turned = jnp.transpose(flat)
        spread = []
        for row in range(part_len // G):
            sums = turned[row * G : (row + 1) * G, LANES:]
            along_h = pltpu.roll(jnp.where(lane < G, sums, 0.0), start + row, 1)
            along_w = pltpu.roll(
                jnp.where((lane >= G) & (lane < 2 * G), sums, 0.0), G, 1, stride=1, stride_axis=0
            )
            spread.append((along_h + along_w).astype(bf16))
        spread = jnp.concatenate(spread, axis=0)
        grad_query = turned[:, :LANES] * score_scale + dot_nn(spread, table_ref[...])
        dq_ref[:, cols] = grad_query[:, :HEAD_DIM].astype(bf16)
        dk_ref[slot] = dot_nn(dscores_ref[spare, here, :], queries)
        dv_ref[slot] = dot_nn(shares_ref[spare, here, :], padded[spare])


def own_call(place, heads, aux, spots, turned_spots, table, grad, lse, inner):
    length = heads.shape[2]
    part_len, features = grad.shape

    def part(index):
        return pl.BlockSpec((1, HALF, length, LANES), lambda n, s: (index, n, 0, 0))

    return pl.pallas_call(
        own_kernel,
        name="back_own",
        grid_spec=pltpu.PrefetchScalarGridSpec(
            num_scalar_prefetch=1,
            grid=(HEADS // HALF,),
            in_specs=[
                pl.BlockSpec((1, HALF, part_len, LANES), lambda n, s: (0, n, s[0], 0)),
                pl.BlockSpec((HALF, part_len, LANES), lambda n, s: (n, s[0], 0)),
                part(1),
                part(2),
                whole((length, LANES)),
                whole((length, LANES)),
                whole((LANES, LANES)),
                pl.BlockSpec((part_len, features // 2), lambda n, s: (0, n)),
                pl.BlockSpec((HALF, 1, part_len), lambda n, s: (n, 0, 0)),
                pl.BlockSpec((HALF, 1, part_len), lambda n, s: (n, 0, 0)),
            ],
            out_specs=[
                pl.BlockSpec((part_len, features // 2), lambda n, s: (0, n)),
                pl.BlockSpec((HALF, part_len, LANES), lambda n, s: (n, 0, 0)),
                pl.BlockSpec((HALF, part_len, LANES), lambda n, s: (n, 0, 0)),
            ],
            scratch_shapes=[
                pltpu.VMEM((2, length, part_len), bf16),
                pltpu.VMEM((2, length, part_len), bf16),
                pltpu.VMEM((2, part_len, LANES), bf16),
            ],
        ),
        out_shape=[
            jax.ShapeDtypeStruct((part_len, features), bf16),
            jax.ShapeDtypeStruct((HEADS, part_len, LANES), f32),
            jax.ShapeDtypeStruct((HEADS, part_len, LANES), f32),
        ],
        compiler_params=params(("arbitrary",), 60),
        cost_estimate=pl.CostEstimate(
            flops=8 * HEADS * part_len * length * LANES * 2,
            bytes_accessed=12 * HEADS * length * LANES,
            transcendentals=HEADS * part_len * length,
        ),
    )(place, heads, aux, heads, heads, spots, turned_spots, table, grad, lse, inner)


def other_kernel(
    steps, place_ref, q_ref, aux_ref, k_ref, v_ref, spots_ref, grad_ref, lse_ref, inner_ref,
    dk_in, dv_in, dk_ref, dv_ref, padded, *sums,
):
    step = pl.program_id(1)
    part_len = q_ref.shape[2]
    if sums:
        dk_sum, dv_sum = sums

        @pl.when(step == 0)
        def _():
            dk_sum[...] = dk_in[...]
            dv_sum[...] = dv_in[...]

    for slot in range(HALF):
        cols = slice(slot * HEAD_DIM, (slot + 1) * HEAD_DIM)
        spare = slot % 2
        padded[spare, :, HEAD_DIM:LANES] = jnp.zeros((part_len, LANES - HEAD_DIM), bf16)
        padded[spare, :, 0:HEAD_DIM] = grad_ref[0, :, cols]
        queries = q_ref[0, slot]
        left = jnp.concatenate([k_ref[0, slot], spots_ref[...]], axis=1)
        right = jnp.concatenate([queries, aux_ref[slot]], axis=1)
        shares = jnp.exp2(dot_nt(left, right) * exponent_scale - lse_ref[0, slot])
        grad_shares = dot_nt(v_ref[0, slot], padded[spare])
        dscores = (shares * (grad_shares - inner_ref[0, slot])).astype(bf16)
        grad_key = dot_nn(dscores, queries)
        grad_value = dot_nn(shares.astype(bf16), padded[spare])
        if sums:
            dk_sum[slot] += grad_key
            dv_sum[slot] += grad_value
        else:
            grad_key = (grad_key + dk_in[slot])[:, :HEAD_DIM] * score_scale
            grad_value = (grad_value + dv_in[slot])[:, :HEAD_DIM]
            dk_ref[:, cols] = grad_key.astype(bf16)
            dv_ref[:, cols] = grad_value.astype(bf16)

    if sums:

        @pl.when(step == steps - 1)
        def _():
            for slot in range(HALF):
                cols = slice(slot * HEAD_DIM, (slot + 1) * HEAD_DIM)
                dk_ref[:, cols] = (dk_sum[slot, :, :HEAD_DIM] * score_scale).astype(bf16)
                dv_ref[:, cols] = dv_sum[slot, :, :HEAD_DIM].astype(bf16)


def other_call(place, heads, aux, spots, grads, lses, inners, dk, dv):
    length = heads.shape[2]
    blocks, part_len, features = grads.shape
    count = length // part_len

    def theirs(i, s):
        return lax.rem(s[0] + 1 + i, count)

    def given(i, s):
        return theirs(i, s) if blocks > 1 else 0

    def own(index):
        return pl.BlockSpec((1, HALF, part_len, LANES), lambda n, i, s: (index, n, s[0], 0))

    stats = pl.BlockSpec((1, HALF, 1, part_len), lambda n, i, s: (given(i, s), n, 0, 0))
    sums = pl.BlockSpec((HALF, part_len, LANES), lambda n, i, s: (n, 0, 0))
    dense = pl.BlockSpec((part_len, features // 2), lambda n, i, s: (0, n))
    return pl.pallas_call(
        functools.partial(other_kernel, count - 1),
        name="back_other",
        grid_spec=pltpu.PrefetchScalarGridSpec(
            num_scalar_prefetch=1,
            grid=(HEADS // HALF, count - 1),
            in_specs=[
                pl.BlockSpec((1, HALF, part_len, LANES), lambda n, i, s: (0, n, theirs(i, s), 0)),
                pl.BlockSpec((HALF, part_len, LANES), lambda n, i, s: (n, theirs(i, s), 0)),
                own(1),
                own(2),
                pl.BlockSpec((part_len, LANES), lambda n, i, s: (s[0], 0)),
                pl.BlockSpec(
                    (1, part_len, features // 2), lambda n, i, s: (given(i, s), 0, n)
                ),
                stats,
                stats,
                sums,
                sums,
            ],
            out_specs=[dense, dense],
            scratch_shapes=[pltpu.VMEM((2, part_len, LANES), bf16)]
            + [pltpu.VMEM((HALF, part_len, LANES), f32)] * (2 if count > 2 else 0),
        ),
        out_shape=[
            jax.ShapeDtypeStruct((part_len, features), bf16),
            jax.ShapeDtypeStruct((part_len, features), bf16),
        ],
        compiler_params=params(("arbitrary", "arbitrary"), 60),
        cost_estimate=pl.CostEstimate(
            flops=4 * HEADS * part_len * (length - part_len) * LANES * 2,
            bytes_accessed=12 * HEADS * length * LANES,
            transcendentals=HEADS * part_len * (length - part_len),
        ),
    )(place, heads, aux, heads, heads, spots, grads, lses, inners, dk, dv)


def gelu_parts(hidden):
    size = jnp.abs(hidden) * (0.5**0.5)
    bell = jnp.exp2(hidden * hidden * (-0.5 * log2e))
    t = 1.0 / (1.0 + 0.3275911 * size)
    poly = t * (
        0.254829592
        + t * (-0.284496736 + t * (1.421413741 + t * (-1.453152027 + t * 1.061405429)))
    )
    tail = 0.5 * poly * bell
    cumulative = jnp.where(hidden < 0.0, tail, 1.0 - tail)
    return hidden * cumulative, cumulative + hidden * bell * 0.3989422804014327


def before_kernel(
    att_ref, x_ref, og_ref, wp_ref, bp_ref, dp_ref, up_ref, mask_ref, gain_ref, shift_ref,
    w2_ref, down1_ref, down2_ref, up2_ref,
    resid_ref, act_ref, midp_ref, mid1_ref, gm2_ref, grad_act_ref,
):
    mask = mask_ref[...]

    @pl.when(pl.program_id(0) == 0)
    def _():
        att = att_ref[...]
        midp_ref[...] = (dot_nn(att, dp_ref[...]) * mask).astype(bf16)
        branch = dot_nn(att, wp_ref[...]) + bp_ref[...]
        branch = branch + adapter_scale * dot_nt(midp_ref[...], up_ref[...])
        resid = x_ref[...].astype(f32) + branch
        resid_ref[...] = resid
        normed, _ = normalize(resid)
        act_ref[...] = (normed * gain_ref[...] + shift_ref[...]).astype(bf16)
        mid1_ref[...] = (dot_nn(act_ref[...], down1_ref[...]) * mask).astype(bf16)
        middle = adapter_scale * dot_nn(og_ref[...], up2_ref[...]) * mask
        gm2_ref[...] = middle.astype(bf16)

    grad_act_ref[...] = dot_nt(og_ref[...], w2_ref[...]) + dot_nt(gm2_ref[...], down2_ref[...])


def before_call(att, x, og, wp, bp, dp, up, mask, gain, shift, w2, down1, down2, up2):
    rows, features = att.shape
    wide = w2.shape[0]
    block = 1024

    def fixed(shape):
        zeros = (0,) * len(shape)
        return pl.BlockSpec(shape, lambda j: zeros, pipeline_mode=pl.Buffered(1))

    ins = [att, x, og, wp, bp, dp, up, mask, gain, shift, w2, down1, down2, up2]
    specs = [fixed(a.shape) for a in ins]
    specs[10] = pl.BlockSpec((block, features), lambda j: (j, 0))
    specs[12] = pl.BlockSpec((block, LANES), lambda j: (j, 0))
    shapes = [
        jax.ShapeDtypeStruct((rows, features), f32),
        jax.ShapeDtypeStruct((rows, features), bf16),
        jax.ShapeDtypeStruct((rows, LANES), bf16),
        jax.ShapeDtypeStruct((rows, LANES), bf16),
        jax.ShapeDtypeStruct((rows, LANES), bf16),
        jax.ShapeDtypeStruct((rows, wide), f32),
    ]
    return pl.pallas_call(
        before_kernel,
        name="before",
        grid=(wide // block,),
        in_specs=specs,
        out_specs=[fixed(a.shape) for a in shapes[:5]]
        + [pl.BlockSpec((rows, block), lambda j: (0, j))],
        out_shape=shapes,
        compiler_params=params(("arbitrary",), 56),
        cost_estimate=pl.CostEstimate(
            flops=2 * rows * features * (wide + features),
            bytes_accessed=2 * features * wide + 4 * rows * wide + 16 * rows * features,
            transcendentals=0,
        ),
    )(*ins)


def feed_kernel(
    act_ref, mid1_ref, gm2_ref, grad_act_ref, mask_ref, gain_ref,
    w1_ref, b1_ref, w2_ref, b2_ref, down1_ref, up1_ref, down2_ref, up2_ref,
    dp_ref, up_ref, midp_ref, sums_ref, *refs,
):
    late = refs[:4]
    (out_ref, grad_ref, grad_att_ref, inner_ref, gd1_ref, gu1_ref, gd2_ref, gu2_ref, gdp_ref,
     gup_ref) = refs[4:14]
    total, back, mid2_sum, gm1_sum, gm2_t, mid1_t, late_sem, acts, grads = refs[14:23]
    held = refs[23:]
    resid_ref, og_ref, att_ref, wp_ref = held

    step = pl.program_id(0)
    steps = pl.num_programs(0)
    mask = mask_ref[...]

    def copies():
        return [
            pltpu.make_async_copy(source, target, late_sem.at[index])
            for index, (source, target) in enumerate(zip(late, held))
        ]

    @pl.when(step == 0)
    def _():
        for copy in copies():
            copy.start()
        total[...] = jnp.zeros_like(total)
        back[...] = jnp.zeros_like(back)
        mid2_sum[...] = jnp.zeros_like(mid2_sum)
        gm1_sum[...] = jnp.zeros_like(gm1_sum)
        gm2_t[...] = chosen_rows(mask, gm2_ref[...])
        mid1_t[...] = chosen_rows(mask, mid1_ref[...])

    wide = w2_ref.shape[0] // 4

    def first(at):
        cols = pl.ds(at, wide)
        hidden = dot_nn(act_ref[...], w1_ref[:, cols]) + b1_ref[:, cols]
        return hidden + adapter_scale * dot_nt(mid1_ref[...], up1_ref[cols, :])

    sums = []
    coming = first(0)
    for at in range(0, w2_ref.shape[0], wide):
        cols = pl.ds(at, wide)
        hidden = coming
        if at + wide < w2_ref.shape[0]:
            coming = first(at + wide)
        value, slope = gelu_parts(hidden)
        activated = value.astype(bf16)
        grad_hidden = (grad_act_ref[:, cols] * slope).astype(bf16)
        acts[:, cols] = activated
        grads[:, cols] = grad_hidden
    activated, grad_hidden = acts[...], grads[...]
    total[...] += dot_nn(activated, w2_ref[...])
    mid2_sum[...] += dot_nn(activated, down2_ref[...])
    back[...] += dot_nt(grad_hidden, w1_ref[...])
    gm1_sum[...] += dot_nn(grad_hidden, up1_ref[...])
    gd2_ref[...] = dot_nn(gm2_t[...], activated).astype(bf16)
    gu1_ref[...] = (adapter_scale * dot_nn(mid1_t[...], grad_hidden)).astype(bf16)

    @pl.when(step == steps - 1)
    def _():
        for copy in copies():
            copy.wait()
        mid2 = mid2_sum[...] * mask
        mid2_low = mid2.astype(bf16)
        resid = resid_ref[...]
        final = resid + total[...] + b2_ref[...]
        final = final + adapter_scale * dot_nt(mid2_low, up2_ref[...])
        out_ref[...] = final.astype(bf16)
        gm1 = adapter_scale * gm1_sum[...] * mask
        gm1_low = gm1.astype(bf16)
        upstream = back[...] + dot_nt(gm1_low, down1_ref[...])
        normed, inverse = normalize(resid)
        grad = og_ref[...].astype(f32) + norm_back(upstream * gain_ref[...], normed, inverse)
        grad_ref[...] = grad
        branch = grad.astype(bf16)
        gd1_ref[...] = dot_nn(chosen_rows(mask, gm1_low), act_ref[...]).astype(bf16)
        gu2_ref[...] = (adapter_scale * dot_nn(chosen_rows(mask, mid2_low), og_ref[...])).astype(bf16)
        middle = (adapter_scale * dot_nn(branch, up_ref[...]) * mask).astype(bf16)
        grad_att = dot_nt(branch, wp_ref[...]) + dot_nt(middle, dp_ref[...])
        grad_att_ref[...] = grad_att.astype(bf16)
        product = grad_att_ref[...].astype(f32) * att_ref[...].astype(f32)
        high = product.astype(bf16)
        low = (product - high.astype(f32)).astype(bf16)
        inner = dot_nt(sums_ref[...], high) + dot_nt(sums_ref[...], low)
        for head in range(HEADS):
            inner_ref[head] = inner[head : head + 1, :]
        gdp_ref[...] = dot_nn(chosen_rows(mask, middle), att_ref[...]).astype(bf16)
        own_t = chosen_rows(mask, midp_ref[...])
        gup_ref[...] = (adapter_scale * dot_nn(own_t, branch)).astype(bf16)


def feed_call(
    act, mid1, gm2, grad_act, mask, gain, w1, b1, w2, b2, down1, up1, down2, up2, dp, up, midp,
    sums, late,
):
    rows, features = act.shape
    wide = b1.shape[1]
    block = 1024

    def fixed(shape):
        zeros = (0,) * len(shape)
        return pl.BlockSpec(shape, lambda j: zeros, pipeline_mode=pl.Buffered(1))

    def by_columns(height):
        return pl.BlockSpec((height, block), lambda j: (0, j))

    def by_rows(width):
        return pl.BlockSpec((block, width), lambda j: (j, 0))

    ins = [
        act, mid1, gm2, grad_act, mask, gain, w1, b1, w2, b2, down1, up1, down2, up2, dp, up,
        midp, sums,
    ]
    specs = [fixed(a.shape) for a in ins]
    specs[3] = by_columns(rows)
    specs[6] = by_columns(features)
    specs[7] = by_columns(1)
    specs[8] = by_rows(features)
    specs[11] = by_rows(LANES)
    specs[12] = by_rows(LANES)
    specs += [pl.BlockSpec(memory_space=pl.ANY)] * len(late)
    return pl.pallas_call(
        feed_kernel,
        name="feed",
        grid=(wide // block,),
        in_specs=specs,
        out_specs=[
            fixed((rows, features)),
            fixed((rows, features)),
            fixed((rows, features)),
            fixed((HEADS, 1, rows)),
            fixed((RANK, features)),
            by_columns(RANK),
            by_columns(RANK),
            fixed((RANK, features)),
            fixed((RANK, features)),
            fixed((RANK, features)),
        ],
        scratch_shapes=[
            pltpu.VMEM((rows, features), f32),
            pltpu.VMEM((rows, features), f32),
            pltpu.VMEM((rows, LANES), f32),
            pltpu.VMEM((rows, LANES), f32),
            pltpu.VMEM((RANK, rows), bf16),
            pltpu.VMEM((RANK, rows), bf16),
            pltpu.SemaphoreType.DMA((len(late),)),
            pltpu.VMEM((rows, block), bf16),
            pltpu.VMEM((rows, block), bf16),
        ]
        + [pltpu.VMEM(a.shape, a.dtype) for a in late],
        out_shape=[
            jax.ShapeDtypeStruct((rows, features), bf16),
            jax.ShapeDtypeStruct((rows, features), f32),
            jax.ShapeDtypeStruct((rows, features), bf16),
            jax.ShapeDtypeStruct((HEADS, 1, rows), f32),
            jax.ShapeDtypeStruct((RANK, features), bf16),
            jax.ShapeDtypeStruct((RANK, wide), bf16),
            jax.ShapeDtypeStruct((RANK, wide), bf16),
            jax.ShapeDtypeStruct((RANK, features), bf16),
            jax.ShapeDtypeStruct((RANK, features), bf16),
            jax.ShapeDtypeStruct((RANK, features), bf16),
        ],
        compiler_params=params(("arbitrary",), 60),
        cost_estimate=pl.CostEstimate(
            flops=6 * rows * features * wide,
            bytes_accessed=4 * features * wide + 4 * rows * wide + 24 * rows * features,
            transcendentals=2 * rows * wide,
        ),
    )(*ins, *late)


def close_kernel(
    shape, widths, dq_ref, dk_ref, dv_ref, weight_ref, down_ref, up_ref, mid_ref,
    mask_ref, x_ref, gain_ref, shift_ref, *refs,
):
    count, parts = shape
    devices = count * parts
    remote = courier_lines(dict(dp=count, seq=parts), []) is not None
    terms, refs = refs[:6], refs[6:]
    part_ref, out_ref = refs[:2]
    refs = refs[2:]
    total, grad_up, grad_down, stage = refs[:4]
    step = pl.program_id(0)
    features = x_ref.shape[1]
    if remote:
        landed, sends, arrivals = refs[4:]
        me = lax.axis_index("dp") * parts + lax.axis_index("seq")
        barrier = pltpu.get_barrier_semaphore()

        def peer(k):
            at = lax.rem(me + k, devices)
            return (at // parts, at % parts)

        def rows(at):
            return pl.ds(pl.multiple_of(at * RANK, RANK), RANK)

        def copy_to(k):
            at = lax.rem(me + k, devices)
            return pltpu.make_async_remote_copy(
                src_ref=stage.at[rows(at), :],
                dst_ref=landed.at[rows(me), :],
                send_sem=sends.at[k],
                recv_sem=arrivals.at[k],
                device_id=peer(k),
                device_id_type=pl.DeviceIdType.MESH,
            )

    @pl.when(step == 0)
    def _():
        if remote:

            def greet(k, carry):
                pl.semaphore_signal(
                    barrier, inc=1, device_id=peer(k), device_id_type=pl.DeviceIdType.MESH
                )
                return carry

            lax.fori_loop(1, devices, greet, 0)
        total[...] = jnp.zeros_like(total)
        own_t = chosen_rows(mask_ref[...], mid_ref[...])
        middle = jnp.zeros((x_ref.shape[0], LANES), f32)
        for index, source in enumerate((dq_ref, dk_ref, dv_ref)):
            at = pl.ds(index * features, features)
            middle += dot_nn(source[...], up_ref[at, :])
            grad_up[:, at] = (adapter_scale * dot_nn(own_t, source[...])).astype(bf16)
        middle = (adapter_scale * middle * mask_ref[...]).astype(bf16)
        normed, _ = normalize(x_ref[...].astype(f32))
        act = (normed * gain_ref[...].astype(f32) + shift_ref[...].astype(f32)).astype(bf16)
        total[...] = dot_nt(middle, down_ref[...])
        grad_down[...] = dot_nn(chosen_rows(mask_ref[...], middle), act).astype(bf16)
        at = 0
        for source, width in zip((grad_down, *terms[:3], grad_up, *terms[3:]), widths):
            for device in range(devices):
                stage[device * RANK : (device + 1) * RANK, at : at + width] = source[
                    :, device * width : (device + 1) * width
                ]
            at += width
        if remote:
            pl.semaphore_wait(barrier, devices - 1)

            def send(k, carry):
                copy_to(k).start()
                return carry

            lax.fori_loop(1, devices, send, 0)
            landed[rows(me), :] = stage[rows(me), :]
        else:
            out_ref[...] = stage[...]

    for index, source in enumerate((dq_ref, dk_ref, dv_ref)):

        @pl.when(step == index)
        def _():
            total[...] += dot_nt(source[...], weight_ref[...])

    @pl.when(step == 2)
    def _():
        part_ref[...] = total[...]
        if remote:

            def wait(k, carry):
                copy_to(k).wait()
                return carry

            lax.fori_loop(1, devices, wait, 0)
            out_ref[...] = landed[...]


def close_call(
    mesh_shape, widths, dq, dk, dv, weight, down, up, mid, mask, x, gain, shift, terms,
):
    rows, features = dq.shape
    devices = mesh_shape["dp"] * mesh_shape["seq"]
    remote = courier_lines(mesh_shape, []) is not None
    span = sum(widths)

    def fixed(shape):
        zeros = (0,) * len(shape)
        return pl.BlockSpec(shape, lambda j: zeros, pipeline_mode=pl.Buffered(1))

    ins = [dq, dk, dv, weight, down, up, mid, mask, x, gain, shift, *terms]
    specs = [fixed(a.shape) for a in ins]
    specs[3] = pl.BlockSpec((features, features), lambda j: (0, j))
    shapes = [
        jax.ShapeDtypeStruct((rows, features), f32),
        jax.ShapeDtypeStruct((devices * RANK, span), bf16),
    ]
    scratch = [
        pltpu.VMEM((rows, features), f32),
        pltpu.VMEM((RANK, 3 * features), bf16),
        pltpu.VMEM((RANK, features), bf16),
        pltpu.VMEM((devices * RANK, span), bf16),
    ]
    options = {}
    if remote:
        scratch += [
            pltpu.VMEM((devices * RANK, span), bf16),
            pltpu.SemaphoreType.DMA((devices,)),
            pltpu.SemaphoreType.DMA((devices,)),
        ]
        options = dict(collective_id=4, has_side_effects=True)
    out = pl.pallas_call(
        functools.partial(close_kernel, (mesh_shape["dp"], mesh_shape["seq"]), widths),
        name="close",
        grid=(3,),
        in_specs=specs,
        out_specs=[fixed(a.shape) for a in shapes],
        scratch_shapes=scratch,
        out_shape=shapes,
        compiler_params=pltpu.CompilerParams(
            dimension_semantics=("arbitrary",), vmem_limit_bytes=56 * 1024 * 1024, **options
        ),
        cost_estimate=pl.CostEstimate(
            flops=6 * rows * features * features,
            bytes_accessed=6 * features * features + 20 * rows * features,
            transcendentals=0,
        ),
    )(*ins)
    if remote:
        return out
    landed = lax.all_to_all(
        out[1].reshape(devices, RANK, span), ("dp", "seq"), 0, 0, tiled=True
    ).reshape(devices * RANK, span)
    return out[0], landed


def last_kernel(
    devices, widths, upstream_ref, x_ref, gain_ref, resid_ref, landed_ref, packs_ref, out_ref,
    *grads,
):
    normed, inverse = normalize(x_ref[...].astype(f32))
    out_ref[...] = resid_ref[...] + norm_back(
        upstream_ref[...] * gain_ref[...].astype(f32), normed, inverse
    )

    @pl.when(pl.program_id(0) == 0)
    def _():
        every = packs_ref.shape[0]
        row = lax.broadcasted_iota(jnp.int32, (devices * RANK, every), 0)
        column = lax.broadcasted_iota(jnp.int32, (devices * RANK, every), 1)
        chosen = (column == row // RANK * (every // devices) + VECTORS).astype(bf16)
        adapter = dot_nn(chosen, packs_ref[:, :LANES])[:, 0:1]
        row = lax.broadcasted_iota(jnp.int32, (devices * RANK, LANES), 0)
        column = lax.broadcasted_iota(jnp.int32, (devices * RANK, LANES), 1)
        same = (column // RANK).astype(f32) == adapter
        spread = jnp.where(same & (row % RANK == column % RANK), 1.0, 0.0).astype(bf16)
        sums = dot_tn(landed_ref[...], spread)
        at = 0
        for target, width in zip(grads, widths):
            target[...] = sums[at : at + width, :]
            at += width


def last_call(devices, widths, upstream, x, gain, resid, landed, packs):
    rows, features = x.shape
    tall = rows // 4 if rows % 64 == 0 else rows
    by_rows = pl.BlockSpec((tall, features), lambda i: (i, 0))
    return pl.pallas_call(
        functools.partial(last_kernel, devices, widths),
        name="last",
        grid=(rows // tall,),
        in_specs=[
            by_rows,
            by_rows,
            whole((1, features)),
            by_rows,
            whole(landed.shape),
            whole(packs.shape),
        ],
        out_specs=[by_rows] + [whole((width, LANES)) for width in widths],
        out_shape=[jax.ShapeDtypeStruct((rows, features), f32)]
        + [jax.ShapeDtypeStruct((width, LANES), f32) for width in widths],
        compiler_params=params(("arbitrary",), 50),
    )(upstream, x, gain, resid, landed, packs)


def position_tables(rel_h, rel_w, length):
    wide = ((0, LANES // 2 - (2 * G - 1)), (0, LANES - HEAD_DIM))
    h = jnp.pad(rel_h, wide)
    w = jnp.pad(rel_w, wide)
    h_back = jnp.pad(rel_h[::-1], wide)
    w_back = jnp.pad(rel_w[::-1], wide)
    forward = jnp.concatenate([h_back, h_back, w_back, w_back], axis=0).T
    backward = jnp.concatenate([h, w], axis=0)
    spot = np.arange(length)[:, None]
    lane = np.arange(LANES)[None, :]
    at = np.where((lane // G) % 2 == 0, spot // G, spot % G)
    spots = jnp.asarray(lane % G == at, bf16)
    turned = jnp.asarray(lane % G == G - 1 - at, bf16)
    return forward, backward, spots, turned


def vectors_kernel(devices, sizes, source, target):
    rows = source.shape[0] // devices
    target[...] = jnp.zeros_like(target)
    packs = source[...].astype(f32)
    for line, size in enumerate(sizes):
        for device in range(devices):
            at = device * rows + line
            target[line : line + 1, device * size : (device + 1) * size] = packs[
                at : at + 1, 0:size
            ]


def vectors_call(gathered, devices, sizes):
    return pl.pallas_call(
        functools.partial(vectors_kernel, devices, sizes),
        name="vectors",
        out_shape=jax.ShapeDtypeStruct((VECTORS, devices * max(sizes)), f32),
        compiler_params=params(None, 16),
    )(gathered)


def per_device(
    mesh_shape,
    tokens,
    adapter_index,
    norm1_gain,
    norm1_bias,
    qkv_weight,
    qkv_bias,
    proj_weight,
    proj_bias,
    norm2_gain,
    norm2_bias,
    fc1_weight,
    fc1_bias,
    fc2_weight,
    fc2_bias,
    rel_pos_h,
    rel_pos_w,
    qkv_down,
    qkv_up,
    proj_down,
    proj_up,
    fc1_down,
    fc1_up,
    fc2_down,
    fc2_up,
    out_grad,
):
    axes = ("dp", "seq")
    part_count = mesh_shape["seq"]
    devices = mesh_shape["dp"] * part_count
    images, part_len, features = tokens.shape
    length = part_len * part_count
    own_tokens = tokens[0]
    og = out_grad[0]
    place = lax.axis_index("seq").astype(jnp.int32).reshape(1)

    small = [
        norm1_gain, norm1_bias, qkv_bias, proj_bias, norm2_gain, norm2_bias, fc1_bias, fc2_bias,
        adapter_index.astype(bf16),
    ]
    sizes = [a.shape[0] for a in small]
    pack = jnp.concatenate([jnp.pad(a, (0, 2 * LANES - a.shape[0])) for a in small])
    pack = jnp.pad(pack.reshape(len(small), 2 * LANES), ((0, 16 - len(small)), (0, 0)))

    columns = jnp.arange(LANES, dtype=jnp.int32) // RANK
    mask = (columns[None, :] == adapter_index[:, None]).astype(f32)
    forward_table, back_table, spots, turned_spots = position_tables(rel_pos_h, rel_pos_w, length)
    head_of = np.arange(features)[None, :] // HEAD_DIM
    head_sums = jnp.asarray(head_of == np.arange(HEADS)[:, None], bf16)

    w_fc2 = lax.all_gather(fc2_weight, axes, axis=0, tiled=True)
    w_fc1 = lax.all_gather(fc1_weight, axes, axis=0, tiled=True)
    if part_count == 2:
        image_tokens = [own_tokens, lax.ppermute(own_tokens, "seq", [(0, 1), (1, 0)])]
    else:
        image_tokens = [lax.all_gather(own_tokens, "seq", axis=0, tiled=True)]
    w_qkv, d_qkv, u_qkv, all_small = collect(mesh_shape, [qkv_weight, qkv_down, qkv_up.T, pack])
    vectors = vectors_call(all_small, devices, sizes[:VECTORS])
    g1, s1, b_qkv, b_proj, g2, s2, b_fc1, b_fc2 = (
        vectors[i : i + 1, : devices * sizes[i]] for i in range(VECTORS)
    )
    (heads, mid_qkv, att, lse, aux), rest = front_call(
        mesh_shape, part_len, image_tokens, g1, s1, w_qkv, b_qkv, d_qkv, u_qkv, mask,
        forward_table, spots,
        [proj_weight, proj_down, fc1_down, fc2_down, proj_up.T, fc1_up.T, fc2_up.T],
    )
    w_proj, d_proj, d_fc1, d_fc2, u_proj, u_fc1, u_fc2 = rest
    resid, act_two, mid_proj, mid_fc1, gm_fc2, grad_act = before_call(
        att, own_tokens, og, w_proj, b_proj, d_proj, u_proj, mask, g2, s2, w_fc2, d_fc1, d_fc2,
        u_fc2,
    )
    (block_out, grad_resid, grad_att, inner, gd_fc1, gu_fc1, gd_fc2, gu_fc2, gd_proj,
     gu_proj) = feed_call(
        act_two, mid_fc1, gm_fc2, grad_act, mask, g2, w_fc1, b_fc1, w_fc2, b_fc2, d_fc1, u_fc1,
        d_fc2, u_fc2, d_proj, u_proj, mid_proj, head_sums, [resid, og, att, w_proj],
    )
    if part_count == 2:
        swap = [(0, 1), (1, 0)]
        their_grad, their_lse, their_inner = (
            lax.ppermute(a, "seq", swap)[None] for a in (grad_att, lse, inner)
        )
    else:
        their_grad, their_lse, their_inner = (
            lax.all_gather(a, "seq", axis=0) for a in (grad_att, lse, inner)
        )
    dq, dk_own, dv_own = own_call(
        place, heads, aux, spots, turned_spots, back_table, grad_att, lse, inner
    )
    dk, dv = other_call(
        place, heads, aux, spots, their_grad, their_lse, their_inner, dk_own, dv_own
    )
    mid_own = lax.dynamic_slice_in_dim(mid_qkv, place[0] * part_len, part_len, 0)
    widths = [a.shape[0] for a in (qkv_down, proj_down, fc1_down, fc2_down)]
    widths += [a.shape[1] for a in (qkv_up, proj_up, fc1_up, fc2_up)]
    upstream, landed = close_call(
        mesh_shape, widths, dq, dk, dv, w_qkv, d_qkv, u_qkv, mid_own, mask, own_tokens, g1, s1,
        [gd_proj, gd_fc1, gd_fc2, gu_proj, gu_fc1, gu_fc2],
    )
    input_grad, *grads = last_call(
        devices, widths, upstream, own_tokens, g1, grad_resid, landed, all_small
    )
    return (
        block_out[None],
        input_grad[None],
        grads[0],
        grads[4].T,
        grads[1],
        grads[5].T,
        grads[2],
        grads[6].T,
        grads[3],
        grads[7].T,
    )


def solution(mesh):
    both = ("dp", "seq")
    return jax.shard_map(
        functools.partial(per_device, dict(mesh.shape)),
        mesh=mesh,
        in_specs=(
            P("dp", "seq", None),
            P("dp"),
            P(both),
            P(both),
            P(both, None),
            P(both),
            P(both, None),
            P(both),
            P(both),
            P(both),
            P(both, None),
            P(both),
            P(both, None),
            P(both),
            P(),
            P(),
            P(both, None),
            P(None, both),
            P(both, None),
            P(None, both),
            P(both, None),
            P(None, both),
            P(both, None),
            P(None, both),
            P("dp", "seq", None),
        ),
        out_specs=(
            P("dp", "seq", None),
            P("dp", "seq", None),
            P(both, None),
            P(None, both),
            P(both, None),
            P(None, both),
            P(both, None),
            P(None, both),
            P(both, None),
            P(None, both),
        ),
        check_vma=False,
    )
```

```python
import functools

import jax
import jax.numpy as jnp
import numpy as np
from jax import lax
from jax.experimental import pallas as pl
from jax.experimental.pallas import tpu as pltpu
from jax.sharding import PartitionSpec as P

HEADS = 16
HEAD_DIM = 80
ADAPTERS = 8
RANK = 16
G = 32
LANES = 128
VECTORS = 8
HALF = HEADS // 2

epsilon = 1e-06
adapter_scale = 0.5
log2e = 1.4426950408889634
score_scale = HEAD_DIM ** (-0.5)
exponent_scale = score_scale * log2e
f32 = jnp.float32
bf16 = jnp.bfloat16


def dot_nn(left, right):
    return lax.dot_general(left, right, (((1,), (0,)), ((), ())), preferred_element_type=f32)


def dot_nt(left, right):
    return lax.dot_general(left, right, (((1,), (1,)), ((), ())), preferred_element_type=f32)


def dot_tn(left, right):
    return lax.dot_general(left, right, (((0,), (0,)), ((), ())), preferred_element_type=f32)


def normalize(values):
    average = jnp.mean(values, axis=-1, keepdims=True)
    centered = values - average
    variance = jnp.mean(centered * centered, axis=-1, keepdims=True)
    inverse = lax.rsqrt(variance + epsilon)
    return centered * inverse, inverse


def norm_back(scaled, normed, inverse):
    return inverse * (
        scaled
        - jnp.mean(scaled, axis=-1, keepdims=True)
        - normed * jnp.mean(scaled * normed, axis=-1, keepdims=True)
    )


def chosen_rows(mask, middle):
    rank = lax.broadcasted_iota(jnp.int32, (RANK, LANES), 0)
    column = lax.broadcasted_iota(jnp.int32, (RANK, LANES), 1)
    pick = jnp.where(column % RANK == rank, jnp.broadcast_to(mask, (RANK, LANES)), 0.0)
    return dot_nt(pick.astype(bf16), middle).astype(bf16)


def params(semantics, megabytes):
    return pltpu.CompilerParams(
        dimension_semantics=semantics, vmem_limit_bytes=megabytes * 1024 * 1024
    )


def whole(shape):
    zeros = (0,) * len(shape)
    return pl.BlockSpec(shape, lambda *_: zeros)


Z, X, Y, S, XD, YD, SX, SY, SD = range(9)


class Courier:
    def __init__(self, lines, chunks, rows_of, sources, targets, local, sends, arrivals):
        self.lines = lines
        self.chunks = chunks
        self.rows_of = rows_of
        self.sources, self.targets = sources, targets
        self.local, self.sends, self.arrivals = local, sends, arrivals
        dp = lax.axis_index("dp")
        self.seq = lax.axis_index("seq")
        self.dp = dp
        self.line, self.column, self.core = dp // 4, (dp // 2) % 2, dp % 2
        line, column, core, seq = self.line, self.column, self.core, self.seq
        self.ahead = [
            self.device(lax.rem(line + k, lines), column, core, seq) for k in range(1, lines)
        ]
        self.across = self.device(line, 1 - column, core, seq)
        self.partner = self.device(line, column, core, 1 - seq)
        self.sibling = self.device(line, column, 1 - core, seq)

    @staticmethod
    def device(z, x, c, y):
        return (z * 4 + x * 2 + c, y)

    def owner(self, k, x, c, y):
        return self.device(lax.rem(self.line + self.lines - k, self.lines), x, c, y)

    def greet(self):
        peers = self.ahead + [self.across, self.partner, self.sibling]
        barrier = pltpu.get_barrier_semaphore()
        for peer in peers:
            pl.semaphore_signal(
                barrier, inc=1, device_id=peer, device_id_type=pl.DeviceIdType.MESH
            )
        pl.semaphore_wait(barrier, len(peers))

    def slot(self, number, kind, k):
        return (number * 9 + kind) * self.lines + k

    def part(self, number, half):
        _, row, height, col, width, share = self.chunks[number]
        if half is None:
            return row, height, col, width
        if width >= 2 * LANES:
            cut = width // LANES * share // 4 * LANES
            return (row, height, col, cut) if half == 0 else (row, height, col + cut, width - cut)
        cut = height // 8 * share // 4 * 8
        return (row, cut, col, width) if half == 0 else (row + cut, height - cut, col, width)

    def place(self, number, owner, half=None):
        array = self.chunks[number][0]
        row, height, col, width = self.part(number, half)
        if height == 0 or width == 0:
            return None
        start = (owner[0] * 2 + owner[1]) * self.rows_of[array] + row
        return self.targets[array].at[pl.ds(pl.multiple_of(start, 8), height), pl.ds(col, width)]

    def like(self, number, half=None):
        array = self.chunks[number][0]
        row, height, col, width = self.part(number, half)
        if height == 0 or width == 0:
            return None
        return self.targets[array].at[pl.ds(row, height), pl.ds(col, width)]

    def send(self, source, target, peer, number, kind, k):
        at = self.slot(number, kind, k)
        pltpu.make_async_remote_copy(
            src_ref=source,
            dst_ref=target,
            send_sem=self.sends.at[at],
            recv_sem=self.arrivals.at[at],
            device_id=peer,
            device_id_type=pl.DeviceIdType.MESH,
        ).start()

    def arrive(self, place, number, kind, k):
        pltpu.make_async_copy(place, place, self.arrivals.at[self.slot(number, kind, k)]).wait()

    def start(self, number):
        array, row, height, col, width, _ = self.chunks[number]
        own = self.sources[array].at[pl.ds(row, height), pl.ds(col, width)]
        place = self.place(number, (self.dp, self.seq))
        for k in range(1, self.lines):
            self.send(own, place, self.ahead[k - 1], number, Z, k)
        self.send(own, place, self.across, number, X, 0)
        self.send(own, place, self.partner, number, Y, 0)
        self.send(own, place, self.sibling, number, S, 0)
        pltpu.make_async_copy(own, place, self.local.at[number]).start()

    def stage_one(self, number, k):
        place = self.place(number, self.owner(k, self.column, self.core, self.seq))
        self.arrive(place, number, Z, k)
        self.send(place, place, self.across, number, X, k)
        self.send(place, place, self.partner, number, Y, k)
        self.send(place, place, self.sibling, number, S, k)

    def stage_two(self, number, k):
        owner = self.owner(k, 1 - self.column, self.core, self.seq)
        place = self.place(number, owner)
        self.arrive(place, number, X, k)
        half = self.place(number, owner, 0)
        if half is not None:
            self.send(half, half, self.partner, number, YD, k)
        self.send(place, place, self.sibling, number, SX, k)
        owner = self.owner(k, self.column, self.core, 1 - self.seq)
        place = self.place(number, owner)
        self.arrive(place, number, Y, k)
        half = self.place(number, owner, 1)
        if half is not None:
            self.send(half, half, self.across, number, XD, k)
        self.send(place, place, self.sibling, number, SY, k)

    def stage_three(self, number, k):
        owner = self.owner(k, 1 - self.column, self.core, 1 - self.seq)
        for half, kind in ((0, YD), (1, XD)):
            piece = self.place(number, owner, half)
            if piece is not None:
                self.arrive(piece, number, kind, k)
        place = self.place(number, owner)
        self.send(place, place, self.sibling, number, SD, k)

    def stage_four(self, number, k):
        for kind, x, y in (
            (S, self.column, self.seq),
            (SX, 1 - self.column, self.seq),
            (SY, self.column, 1 - self.seq),
            (SD, 1 - self.column, 1 - self.seq),
        ):
            place = self.place(number, self.owner(k, x, 1 - self.core, y))
            self.arrive(place, number, kind, k)

    def steps(self):
        stages = (self.stage_one, self.stage_two, self.stage_three, self.stage_four)
        order = []
        for tick in range(len(self.chunks) + 3):
            for lag, stage in enumerate(stages):
                if 0 <= tick - lag < len(self.chunks):
                    for k in range(1 if lag == 0 else 0, self.lines):
                        order.append(functools.partial(stage, tick - lag, k))
        return order

    def finish(self):
        for number in range(len(self.chunks)):
            like = self.like(number)
            pltpu.make_async_copy(like, like, self.local.at[number]).wait()
            for kind in range(9):
                half = {YD: 0, XD: 1}.get(kind)
                like = self.like(number, half)
                for k in range(self.lines):
                    if like is not None and not (kind == Z and k == 0):
                        sem = self.sends.at[self.slot(number, kind, k)]
                        pltpu.make_async_copy(like, like, sem).wait()


def cut_chunks(arrays, share=2):
    chunks = []
    for index, array in enumerate(arrays):
        height, width = array.shape
        wide, tall = width, height
        if height * wide * 2 > 120_000 and wide > 1280:
            wide = next(w for w in range(1280, 0, -LANES) if width % w == 0)
        while tall * wide * 2 > 120_000 and tall % 16 == 0:
            tall //= 2
        for row in range(0, height, tall):
            for col in range(0, width, wide):
                chunks.append((index, row, tall, col, wide, share))
    return chunks


def courier_lines(mesh_shape, arrays):
    lines = mesh_shape["dp"] // 4
    fits = mesh_shape["seq"] == 2 and mesh_shape["dp"] == 4 * lines and 2 <= lines <= 4
    return lines if fits and not any(a.shape[0] % 8 for a in arrays) else None


def courier_scratch(lines, chunks):
    slots = len(chunks) * 9 * lines
    return [
        pltpu.SemaphoreType.DMA((len(chunks),)),
        pltpu.SemaphoreType.DMA((slots,)),
        pltpu.SemaphoreType.DMA((slots,)),
    ]


def gathered_shapes(devices, arrays):
    return [jax.ShapeDtypeStruct((devices * a.shape[0], a.shape[1]), a.dtype) for a in arrays]


def collect_kernel(lines, chunks, rows_of, count, *refs):
    courier = Courier(lines, chunks, rows_of, refs[:count], refs[count : 2 * count], *refs[2 * count :])
    courier.greet()
    for number in range(len(chunks)):
        courier.start(number)
    for step in courier.steps():
        step()
    courier.finish()


def collect(mesh_shape, arrays):
    lines = courier_lines(mesh_shape, arrays)
    if lines is None:
        return [lax.all_gather(a, ("dp", "seq"), axis=0, tiled=True) for a in arrays]
    chunks = cut_chunks(arrays, 2)
    anywhere = pl.BlockSpec(memory_space=pl.ANY)
    count = len(arrays)
    size = sum(a.size for a in arrays)
    return pl.pallas_call(
        functools.partial(collect_kernel, lines, chunks, [a.shape[0] for a in arrays], count),
        name="collect",
        in_specs=[anywhere] * count,
        out_specs=[anywhere] * count,
        out_shape=gathered_shapes(mesh_shape["dp"] * 2, arrays),
        scratch_shapes=courier_scratch(lines, chunks),
        compiler_params=pltpu.CompilerParams(collective_id=1, has_side_effects=True),
        cost_estimate=pl.CostEstimate(
            flops=0, bytes_accessed=64 * mesh_shape["dp"] * size, transcendentals=0
        ),
    )(*arrays)


def qkv_part(part, blocks, gain_ref, shift_ref, weight_ref, bias_ref, down_ref, up_ref, mask_ref,
             heads, mid_ref, act_ref, pause):
    length = act_ref.shape[0]

    @pl.when(part == 0)
    def _():
        part_len = length // len(blocks)
        for index, block in enumerate(blocks):
            place = 0
            if len(blocks) == 2:
                seq = lax.axis_index("seq")
                place = pl.multiple_of((seq if index == 0 else 1 - seq) * part_len, G)
            normed, _ = normalize(block[...].astype(f32))
            act = normed * gain_ref[...].astype(f32) + shift_ref[...].astype(f32)
            act_ref[pl.ds(place, part_len), :] = act.astype(bf16)
        mid_ref[...] = (dot_nn(act_ref[...], down_ref[...]) * mask_ref[...]).astype(bf16)

    rows = min(256, length)
    lane = lax.broadcasted_iota(jnp.int32, (rows, LANES - HEAD_DIM), 1)
    pad = jnp.where((lane == 0) & (part == 2), 1.0, 0.0).astype(bf16)
    for start in range(0, length, rows):
        here = pl.ds(start, rows)
        block = dot_nn(act_ref[here, :], weight_ref[...])
        block = block + bias_ref[...].astype(f32)
        block = block + adapter_scale * dot_nt(mid_ref[here, :], up_ref[...])
        block = block.astype(bf16)
        for head in range(HEADS):
            heads[part, head, here, 0:HEAD_DIM] = block[:, head * HEAD_DIM : (head + 1) * HEAD_DIM]
            heads[part, head, here, HEAD_DIM:LANES] = pad
        pause(start // rows)


def attend_head(head, own, heads, table_ref, spots_ref, att_ref, lse_ref, aux_ref, pause):
    pause(0)
    length = heads.shape[2]
    part_len = att_ref.shape[0]
    lane = lax.broadcasted_iota(jnp.int32, (G, LANES), 1)
    first = lane < LANES // 2
    even = (lane // G) % 2 == 0
    raw = dot_nn(heads[0, head], table_ref[...]) * (HEAD_DIM**0.5)
    for row in range(length // G):
        block = raw[row * G : (row + 1) * G, :]
        high = block.astype(bf16).astype(f32)
        mixed_h = jnp.where(first, high[:, :LANES], block[:, :LANES] - high[:, :LANES])
        mixed_w = jnp.where(first, high[:, LANES:], block[:, LANES:] - high[:, LANES:])
        along_h = pltpu.roll(mixed_h, LANES - G + 1 + row, 1)
        along_w = pltpu.roll(mixed_w, 1, 1, stride=1, stride_axis=0)
        aux_ref[0, pl.ds(row * G, G), :] = jnp.where(even, along_h, along_w).astype(bf16)
    pause(1)
    left = jnp.concatenate([heads[0, head, own, :], aux_ref[0, own, :]], axis=1)
    right = jnp.concatenate([heads[1, head], spots_ref[...]], axis=1)
    scores = dot_nt(left, right)
    top = jnp.max(scores, axis=1, keepdims=True)
    shares = jnp.exp2((scores - top) * exponent_scale).astype(bf16)
    mixed = dot_nn(shares, heads[2, head])
    total = mixed[:, HEAD_DIM : HEAD_DIM + 1]
    att = (mixed[:, :HEAD_DIM] / total).astype(bf16)
    logs = top * exponent_scale + jnp.log2(total)
    lse_ref[0] = jnp.transpose(jnp.broadcast_to(logs, (part_len, LANES)))[0:1, :]
    for slot in range(HALF):

        @pl.when(head % HALF == slot)
        def _():
            att_ref[:, slot * HEAD_DIM : (slot + 1) * HEAD_DIM] = att


def front_kernel(
    lines, chunks, rows_of, count, pair,
    gain_ref, shift_ref, weight_ref, bias_ref, down_ref, up_ref, mask_ref, table_ref,
    spots_ref, *refs,
):
    blocks, refs = refs[:pair], refs[pair:]
    sources = refs[:count]
    heads_out, mid_ref, att_ref, lse_ref, aux_ref = refs[count : count + 5]
    targets = refs[count + 5 : 2 * count + 5]
    heads, act_ref, out_sem = refs[2 * count + 5 : 2 * count + 8]
    step = pl.program_id(0)
    last = pl.num_programs(0) - 1
    courier = None
    plan = {}
    if count:
        courier = Courier(lines, chunks, rows_of, sources, targets, *refs[2 * count + 8 :])

        @pl.when(step == 3)
        def _():
            courier.greet()
            for number in range(len(chunks)):
                courier.start(number)

        places = [(3 + head, piece, 1.0) for head in range(HEADS) for piece in range(2)]
        work = courier.steps()
        whole_time = sum(p[2] for p in places)
        done, spent = 0, 0.0
        for at, piece, time in places:
            spent += time
            upto = min(len(work), int(len(work) * spent / whole_time + 1e-6))
            plan[at, piece] = work[done:upto]
            done = upto

    def pause(first, count_of):
        def run(piece):
            for at in range(first, first + count_of):
                items = plan.get((at, piece))
                if items:

                    @pl.when(step == at)
                    def _():
                        for item in items:
                            item()

        return run

    @pl.when(step < 3)
    def _():
        qkv_part(
            step, blocks, gain_ref, shift_ref, weight_ref, bias_ref, down_ref, up_ref, mask_ref,
            heads, mid_ref, act_ref, pause(0, 3),
        )
        pltpu.make_async_copy(heads.at[step], heads_out.at[step], out_sem.at[step]).start()

    part_len = att_ref.shape[0]
    own = pl.ds(pl.multiple_of(lax.axis_index("seq") * part_len, G), part_len)

    @pl.when(step >= 3)
    def _():
        attend_head(
            step - 3, own, heads, table_ref, spots_ref, att_ref, lse_ref, aux_ref, pause(3, HEADS)
        )

    @pl.when(step == last)
    def _():
        for part in range(3):
            pltpu.make_async_copy(heads.at[part], heads_out.at[part], out_sem.at[part]).wait()
        if courier is not None:
            courier.finish()


def front_call(
    mesh_shape, part_len, tokens, gain, shift, weight, bias, down, up, mask, table, spots, arrays
):
    length = sum(t.shape[0] for t in tokens)
    features = weight.shape[0]
    lines = courier_lines(mesh_shape, arrays)
    later = []
    if lines is None:
        axes = ("dp", "seq")
        later = [lax.all_gather(a, axes, axis=0, tiled=True) for a in arrays]
        arrays = []
    chunks = cut_chunks(arrays)
    count = len(arrays)
    anywhere = pl.BlockSpec(memory_space=pl.ANY)

    def head(i):
        return jnp.maximum(i - 3, 0)

    def part(i):
        return jnp.minimum(i, 2)

    def fixed(shape):
        zeros = (0,) * len(shape)
        return pl.BlockSpec(shape, lambda i: zeros, pipeline_mode=pl.Buffered(1))

    options = dict(collective_id=2, has_side_effects=True) if count else {}
    out = pl.pallas_call(
        functools.partial(
            front_kernel, lines, chunks, [a.shape[0] for a in arrays], count, len(tokens)
        ),
        name="front",
        grid=(3 + HEADS,),
        in_specs=[
            fixed((1, features)),
            fixed((1, features)),
            pl.BlockSpec((features, features), lambda i: (0, part(i))),
            pl.BlockSpec((1, features), lambda i: (0, part(i))),
            fixed((features, LANES)),
            pl.BlockSpec((features, LANES), lambda i: (part(i), 0)),
            fixed((1, LANES)),
            fixed((LANES, 2 * LANES)),
            fixed((length, LANES)),
        ]
        + [fixed(t.shape) for t in tokens]
        + [anywhere] * count,
        out_specs=[
            anywhere,
            whole((length, LANES)),
            pl.BlockSpec((part_len, features // 2), lambda i: (0, head(i) // HALF)),
            pl.BlockSpec((1, 1, part_len), lambda i: (head(i), 0, 0)),
            pl.BlockSpec((1, length, LANES), lambda i: (head(i), 0, 0)),
        ]
        + [anywhere] * count,
        out_shape=[
            jax.ShapeDtypeStruct((3, HEADS, length, LANES), bf16),
            jax.ShapeDtypeStruct((length, LANES), bf16),
            jax.ShapeDtypeStruct((part_len, features), bf16),
            jax.ShapeDtypeStruct((HEADS, 1, part_len), f32),
            jax.ShapeDtypeStruct((HEADS, length, LANES), bf16),
        ]
        + gathered_shapes(mesh_shape["dp"] * mesh_shape["seq"], arrays),
        scratch_shapes=[
            pltpu.VMEM((3, HEADS, length, LANES), bf16),
            pltpu.VMEM((length, features), bf16),
            pltpu.SemaphoreType.DMA((3,)),
        ]
        + (courier_scratch(lines, chunks) if count else []),
        compiler_params=pltpu.CompilerParams(
            dimension_semantics=("arbitrary",), vmem_limit_bytes=58 * 1024 * 1024, **options
        ),
        cost_estimate=pl.CostEstimate(
            flops=6 * length * features * features
            + 8 * HEADS * part_len * length * LANES,
            bytes_accessed=2 * (3 * features * features + 8 * length * features),
            transcendentals=HEADS * part_len * length,
        ),
    )(gain, shift, weight, bias, down, up, mask, table, spots, *tokens, *arrays)
    return out[:5], list(out[5:]) + later


def own_kernel(
    place_ref, q_ref, aux_ref, k_ref, v_ref, spots_ref, turned_spots_ref, table_ref, grad_ref,
    lse_ref, inner_ref, dq_ref, dk_ref, dv_ref, shares_ref, dscores_ref, padded,
):
    part_len = q_ref.shape[2]
    lane = lax.broadcasted_iota(jnp.int32, (G, LANES), 1)
    start = place_ref[0] * (part_len // G)
    here = pl.ds(pl.multiple_of(place_ref[0] * part_len, G), part_len)
    for slot in range(HALF):
        cols = slice(slot * HEAD_DIM, (slot + 1) * HEAD_DIM)
        spare = slot % 2
        padded[spare, :, HEAD_DIM:LANES] = jnp.zeros((part_len, LANES - HEAD_DIM), bf16)
        padded[spare, :, 0:HEAD_DIM] = grad_ref[:, cols]
        queries = q_ref[0, slot]
        keys = k_ref[0, slot]
        left = jnp.concatenate([keys, spots_ref[...]], axis=1)
        right = jnp.concatenate([queries, aux_ref[slot]], axis=1)
        shares = jnp.exp2(dot_nt(left, right) * exponent_scale - lse_ref[slot])
        grad_shares = dot_nt(v_ref[0, slot], padded[spare])
        shares_ref[spare] = shares.astype(bf16)
        dscores_ref[spare] = (shares * (grad_shares - inner_ref[slot])).astype(bf16)
        flat = dot_tn(
            jnp.concatenate([keys, turned_spots_ref[...]], axis=1), dscores_ref[spare]
        )
        turned = jnp.transpose(flat)
        spread = []
        for row in range(part_len // G):
            sums = turned[row * G : (row + 1) * G, LANES:]
            along_h = pltpu.roll(jnp.where(lane < G, sums, 0.0), start + row, 1)
            along_w = pltpu.roll(
                jnp.where((lane >= G) & (lane < 2 * G), sums, 0.0), G, 1, stride=1, stride_axis=0
            )
            spread.append((along_h + along_w).astype(bf16))
        spread = jnp.concatenate(spread, axis=0)
        grad_query = turned[:, :LANES] * score_scale + dot_nn(spread, table_ref[...])
        dq_ref[:, cols] = grad_query[:, :HEAD_DIM].astype(bf16)
        dk_ref[slot] = dot_nn(dscores_ref[spare, here, :], queries)
        dv_ref[slot] = dot_nn(shares_ref[spare, here, :], padded[spare])


def own_call(place, heads, aux, spots, turned_spots, table, grad, lse, inner):
    length = heads.shape[2]
    part_len, features = grad.shape

    def part(index):
        return pl.BlockSpec((1, HALF, length, LANES), lambda n, s: (index, n, 0, 0))

    return pl.pallas_call(
        own_kernel,
        name="back_own",
        grid_spec=pltpu.PrefetchScalarGridSpec(
            num_scalar_prefetch=1,
            grid=(HEADS // HALF,),
            in_specs=[
                pl.BlockSpec((1, HALF, part_len, LANES), lambda n, s: (0, n, s[0], 0)),
                pl.BlockSpec((HALF, part_len, LANES), lambda n, s: (n, s[0], 0)),
                part(1),
                part(2),
                whole((length, LANES)),
                whole((length, LANES)),
                whole((LANES, LANES)),
                pl.BlockSpec((part_len, features // 2), lambda n, s: (0, n)),
                pl.BlockSpec((HALF, 1, part_len), lambda n, s: (n, 0, 0)),
                pl.BlockSpec((HALF, 1, part_len), lambda n, s: (n, 0, 0)),
            ],
            out_specs=[
                pl.BlockSpec((part_len, features // 2), lambda n, s: (0, n)),
                pl.BlockSpec((HALF, part_len, LANES), lambda n, s: (n, 0, 0)),
                pl.BlockSpec((HALF, part_len, LANES), lambda n, s: (n, 0, 0)),
            ],
            scratch_shapes=[
                pltpu.VMEM((2, length, part_len), bf16),
                pltpu.VMEM((2, length, part_len), bf16),
                pltpu.VMEM((2, part_len, LANES), bf16),
            ],
        ),
        out_shape=[
            jax.ShapeDtypeStruct((part_len, features), bf16),
            jax.ShapeDtypeStruct((HEADS, part_len, LANES), f32),
            jax.ShapeDtypeStruct((HEADS, part_len, LANES), f32),
        ],
        compiler_params=params(("arbitrary",), 60),
        cost_estimate=pl.CostEstimate(
            flops=8 * HEADS * part_len * length * LANES * 2,
            bytes_accessed=12 * HEADS * length * LANES,
            transcendentals=HEADS * part_len * length,
        ),
    )(place, heads, aux, heads, heads, spots, turned_spots, table, grad, lse, inner)


def other_kernel(
    steps, place_ref, q_ref, aux_ref, k_ref, v_ref, spots_ref, grad_ref, lse_ref, inner_ref,
    dk_in, dv_in, dk_ref, dv_ref, padded, *sums,
):
    step = pl.program_id(1)
    part_len = q_ref.shape[2]
    if sums:
        dk_sum, dv_sum = sums

        @pl.when(step == 0)
        def _():
            dk_sum[...] = dk_in[...]
            dv_sum[...] = dv_in[...]

    for slot in range(HALF):
        cols = slice(slot * HEAD_DIM, (slot + 1) * HEAD_DIM)
        spare = slot % 2
        padded[spare, :, HEAD_DIM:LANES] = jnp.zeros((part_len, LANES - HEAD_DIM), bf16)
        padded[spare, :, 0:HEAD_DIM] = grad_ref[0, :, cols]
        queries = q_ref[0, slot]
        left = jnp.concatenate([k_ref[0, slot], spots_ref[...]], axis=1)
        right = jnp.concatenate([queries, aux_ref[slot]], axis=1)
        shares = jnp.exp2(dot_nt(left, right) * exponent_scale - lse_ref[0, slot])
        grad_shares = dot_nt(v_ref[0, slot], padded[spare])
        dscores = (shares * (grad_shares - inner_ref[0, slot])).astype(bf16)
        grad_key = dot_nn(dscores, queries)
        grad_value = dot_nn(shares.astype(bf16), padded[spare])
        if sums:
            dk_sum[slot] += grad_key
            dv_sum[slot] += grad_value
        else:
            grad_key = (grad_key + dk_in[slot])[:, :HEAD_DIM] * score_scale
            grad_value = (grad_value + dv_in[slot])[:, :HEAD_DIM]
            dk_ref[:, cols] = grad_key.astype(bf16)
            dv_ref[:, cols] = grad_value.astype(bf16)

    if sums:

        @pl.when(step == steps - 1)
        def _():
            for slot in range(HALF):
                cols = slice(slot * HEAD_DIM, (slot + 1) * HEAD_DIM)
                dk_ref[:, cols] = (dk_sum[slot, :, :HEAD_DIM] * score_scale).astype(bf16)
                dv_ref[:, cols] = dv_sum[slot, :, :HEAD_DIM].astype(bf16)


def other_call(place, heads, aux, spots, grads, lses, inners, dk, dv):
    length = heads.shape[2]
    blocks, part_len, features = grads.shape
    count = length // part_len

    def theirs(i, s):
        return lax.rem(s[0] + 1 + i, count)

    def given(i, s):
        return theirs(i, s) if blocks > 1 else 0

    def own(index):
        return pl.BlockSpec((1, HALF, part_len, LANES), lambda n, i, s: (index, n, s[0], 0))

    stats = pl.BlockSpec((1, HALF, 1, part_len), lambda n, i, s: (given(i, s), n, 0, 0))
    sums = pl.BlockSpec((HALF, part_len, LANES), lambda n, i, s: (n, 0, 0))
    dense = pl.BlockSpec((part_len, features // 2), lambda n, i, s: (0, n))
    return pl.pallas_call(
        functools.partial(other_kernel, count - 1),
        name="back_other",
        grid_spec=pltpu.PrefetchScalarGridSpec(
            num_scalar_prefetch=1,
            grid=(HEADS // HALF, count - 1),
            in_specs=[
                pl.BlockSpec((1, HALF, part_len, LANES), lambda n, i, s: (0, n, theirs(i, s), 0)),
                pl.BlockSpec((HALF, part_len, LANES), lambda n, i, s: (n, theirs(i, s), 0)),
                own(1),
                own(2),
                pl.BlockSpec((part_len, LANES), lambda n, i, s: (s[0], 0)),
                pl.BlockSpec(
                    (1, part_len, features // 2), lambda n, i, s: (given(i, s), 0, n)
                ),
                stats,
                stats,
                sums,
                sums,
            ],
            out_specs=[dense, dense],
            scratch_shapes=[pltpu.VMEM((2, part_len, LANES), bf16)]
            + [pltpu.VMEM((HALF, part_len, LANES), f32)] * (2 if count > 2 else 0),
        ),
        out_shape=[
            jax.ShapeDtypeStruct((part_len, features), bf16),
            jax.ShapeDtypeStruct((part_len, features), bf16),
        ],
        compiler_params=params(("arbitrary", "arbitrary"), 60),
        cost_estimate=pl.CostEstimate(
            flops=4 * HEADS * part_len * (length - part_len) * LANES * 2,
            bytes_accessed=12 * HEADS * length * LANES,
            transcendentals=HEADS * part_len * (length - part_len),
        ),
    )(place, heads, aux, heads, heads, spots, grads, lses, inners, dk, dv)


def gelu_parts(hidden):
    size = jnp.abs(hidden) * (0.5**0.5)
    bell = jnp.exp2(hidden * hidden * (-0.5 * log2e))
    t = 1.0 / (1.0 + 0.3275911 * size)
    poly = t * (
        0.254829592
        + t * (-0.284496736 + t * (1.421413741 + t * (-1.453152027 + t * 1.061405429)))
    )
    tail = 0.5 * poly * bell
    cumulative = jnp.where(hidden < 0.0, tail, 1.0 - tail)
    return hidden * cumulative, cumulative + hidden * bell * 0.3989422804014327


def before_kernel(
    att_ref, x_ref, og_ref, wp_ref, bp_ref, dp_ref, up_ref, mask_ref, gain_ref, shift_ref,
    w2_ref, down1_ref, down2_ref, up2_ref,
    resid_ref, act_ref, midp_ref, mid1_ref, gm2_ref, grad_act_ref,
):
    mask = mask_ref[...]

    @pl.when(pl.program_id(0) == 0)
    def _():
        att = att_ref[...]
        midp_ref[...] = (dot_nn(att, dp_ref[...]) * mask).astype(bf16)
        branch = dot_nn(att, wp_ref[...]) + bp_ref[...]
        branch = branch + adapter_scale * dot_nt(midp_ref[...], up_ref[...])
        resid = x_ref[...].astype(f32) + branch
        resid_ref[...] = resid
        normed, _ = normalize(resid)
        act_ref[...] = (normed * gain_ref[...] + shift_ref[...]).astype(bf16)
        mid1_ref[...] = (dot_nn(act_ref[...], down1_ref[...]) * mask).astype(bf16)
        middle = adapter_scale * dot_nn(og_ref[...], up2_ref[...]) * mask
        gm2_ref[...] = middle.astype(bf16)

    grad_act_ref[...] = dot_nt(og_ref[...], w2_ref[...]) + dot_nt(gm2_ref[...], down2_ref[...])


def before_call(att, x, og, wp, bp, dp, up, mask, gain, shift, w2, down1, down2, up2):
    rows, features = att.shape
    wide = w2.shape[0]
    block = 1024

    def fixed(shape):
        zeros = (0,) * len(shape)
        return pl.BlockSpec(shape, lambda j: zeros, pipeline_mode=pl.Buffered(1))

    ins = [att, x, og, wp, bp, dp, up, mask, gain, shift, w2, down1, down2, up2]
    specs = [fixed(a.shape) for a in ins]
    specs[10] = pl.BlockSpec((block, features), lambda j: (j, 0))
    specs[12] = pl.BlockSpec((block, LANES), lambda j: (j, 0))
    shapes = [
        jax.ShapeDtypeStruct((rows, features), f32),
        jax.ShapeDtypeStruct((rows, features), bf16),
        jax.ShapeDtypeStruct((rows, LANES), bf16),
        jax.ShapeDtypeStruct((rows, LANES), bf16),
        jax.ShapeDtypeStruct((rows, LANES), bf16),
        jax.ShapeDtypeStruct((rows, wide), f32),
    ]
    return pl.pallas_call(
        before_kernel,
        name="before",
        grid=(wide // block,),
        in_specs=specs,
        out_specs=[fixed(a.shape) for a in shapes[:5]]
        + [pl.BlockSpec((rows, block), lambda j: (0, j))],
        out_shape=shapes,
        compiler_params=params(("arbitrary",), 56),
        cost_estimate=pl.CostEstimate(
            flops=2 * rows * features * (wide + features),
            bytes_accessed=2 * features * wide + 4 * rows * wide + 16 * rows * features,
            transcendentals=0,
        ),
    )(*ins)


def feed_kernel(
    act_ref, mid1_ref, gm2_ref, grad_act_ref, mask_ref, gain_ref,
    w1_ref, b1_ref, w2_ref, b2_ref, down1_ref, up1_ref, down2_ref, up2_ref,
    dp_ref, up_ref, midp_ref, sums_ref, *refs,
):
    late = refs[:4]
    (out_ref, grad_ref, grad_att_ref, inner_ref, gd1_ref, gu1_ref, gd2_ref, gu2_ref, gdp_ref,
     gup_ref) = refs[4:14]
    total, back, mid2_sum, gm1_sum, gm2_t, mid1_t, late_sem, acts, grads = refs[14:23]
    held = refs[23:]
    resid_ref, og_ref, att_ref, wp_ref = held

    step = pl.program_id(0)
    steps = pl.num_programs(0)
    mask = mask_ref[...]

    def copies():
        return [
            pltpu.make_async_copy(source, target, late_sem.at[index])
            for index, (source, target) in enumerate(zip(late, held))
        ]

    @pl.when(step == 0)
    def _():
        for copy in copies():
            copy.start()
        total[...] = jnp.zeros_like(total)
        back[...] = jnp.zeros_like(back)
        mid2_sum[...] = jnp.zeros_like(mid2_sum)
        gm1_sum[...] = jnp.zeros_like(gm1_sum)
        gm2_t[...] = chosen_rows(mask, gm2_ref[...])
        mid1_t[...] = chosen_rows(mask, mid1_ref[...])

    wide = w2_ref.shape[0] // 4

    def first(at):
        cols = pl.ds(at, wide)
        hidden = dot_nn(act_ref[...], w1_ref[:, cols]) + b1_ref[:, cols]
        return hidden + adapter_scale * dot_nt(mid1_ref[...], up1_ref[cols, :])

    sums = []
    coming = first(0)
    for at in range(0, w2_ref.shape[0], wide):
        cols = pl.ds(at, wide)
        hidden = coming
        if at + wide < w2_ref.shape[0]:
            coming = first(at + wide)
        value, slope = gelu_parts(hidden)
        activated = value.astype(bf16)
        grad_hidden = (grad_act_ref[:, cols] * slope).astype(bf16)
        acts[:, cols] = activated
        grads[:, cols] = grad_hidden
    activated, grad_hidden = acts[...], grads[...]
    total[...] += dot_nn(activated, w2_ref[...])
    mid2_sum[...] += dot_nn(activated, down2_ref[...])
    back[...] += dot_nt(grad_hidden, w1_ref[...])
    gm1_sum[...] += dot_nn(grad_hidden, up1_ref[...])
    gd2_ref[...] = dot_nn(gm2_t[...], activated).astype(bf16)
    gu1_ref[...] = (adapter_scale * dot_nn(mid1_t[...], grad_hidden)).astype(bf16)

    @pl.when(step == steps - 1)
    def _():
        for copy in copies():
            copy.wait()
        mid2 = mid2_sum[...] * mask
        mid2_low = mid2.astype(bf16)
        resid = resid_ref[...]
        final = resid + total[...] + b2_ref[...]
        final = final + adapter_scale * dot_nt(mid2_low, up2_ref[...])
        out_ref[...] = final.astype(bf16)
        gm1 = adapter_scale * gm1_sum[...] * mask
        gm1_low = gm1.astype(bf16)
        upstream = back[...] + dot_nt(gm1_low, down1_ref[...])
        normed, inverse = normalize(resid)
        grad = og_ref[...].astype(f32) + norm_back(upstream * gain_ref[...], normed, inverse)
        grad_ref[...] = grad
        branch = grad.astype(bf16)
        gd1_ref[...] = dot_nn(chosen_rows(mask, gm1_low), act_ref[...]).astype(bf16)
        gu2_ref[...] = (adapter_scale * dot_nn(chosen_rows(mask, mid2_low), og_ref[...])).astype(bf16)
        middle = (adapter_scale * dot_nn(branch, up_ref[...]) * mask).astype(bf16)
        grad_att = dot_nt(branch, wp_ref[...]) + dot_nt(middle, dp_ref[...])
        grad_att_ref[...] = grad_att.astype(bf16)
        product = grad_att_ref[...].astype(f32) * att_ref[...].astype(f32)
        high = product.astype(bf16)
        low = (product - high.astype(f32)).astype(bf16)
        inner = dot_nt(sums_ref[...], high) + dot_nt(sums_ref[...], low)
        for head in range(HEADS):
            inner_ref[head] = inner[head : head + 1, :]
        gdp_ref[...] = dot_nn(chosen_rows(mask, middle), att_ref[...]).astype(bf16)
        own_t = chosen_rows(mask, midp_ref[...])
        gup_ref[...] = (adapter_scale * dot_nn(own_t, branch)).astype(bf16)


def feed_call(
    act, mid1, gm2, grad_act, mask, gain, w1, b1, w2, b2, down1, up1, down2, up2, dp, up, midp,
    sums, late,
):
    rows, features = act.shape
    wide = b1.shape[1]
    block = 1024

    def fixed(shape):
        zeros = (0,) * len(shape)
        return pl.BlockSpec(shape, lambda j: zeros, pipeline_mode=pl.Buffered(1))

    def by_columns(height):
        return pl.BlockSpec((height, block), lambda j: (0, j))

    def by_rows(width):
        return pl.BlockSpec((block, width), lambda j: (j, 0))

    ins = [
        act, mid1, gm2, grad_act, mask, gain, w1, b1, w2, b2, down1, up1, down2, up2, dp, up,
        midp, sums,
    ]
    specs = [fixed(a.shape) for a in ins]
    specs[3] = by_columns(rows)
    specs[6] = by_columns(features)
    specs[7] = by_columns(1)
    specs[8] = by_rows(features)
    specs[11] = by_rows(LANES)
    specs[12] = by_rows(LANES)
    specs += [pl.BlockSpec(memory_space=pl.ANY)] * len(late)
    return pl.pallas_call(
        feed_kernel,
        name="feed",
        grid=(wide // block,),
        in_specs=specs,
        out_specs=[
            fixed((rows, features)),
            fixed((rows, features)),
            fixed((rows, features)),
            fixed((HEADS, 1, rows)),
            fixed((RANK, features)),
            by_columns(RANK),
            by_columns(RANK),
            fixed((RANK, features)),
            fixed((RANK, features)),
            fixed((RANK, features)),
        ],
        scratch_shapes=[
            pltpu.VMEM((rows, features), f32),
            pltpu.VMEM((rows, features), f32),
            pltpu.VMEM((rows, LANES), f32),
            pltpu.VMEM((rows, LANES), f32),
            pltpu.VMEM((RANK, rows), bf16),
            pltpu.VMEM((RANK, rows), bf16),
            pltpu.SemaphoreType.DMA((len(late),)),
            pltpu.VMEM((rows, block), bf16),
            pltpu.VMEM((rows, block), bf16),
        ]
        + [pltpu.VMEM(a.shape, a.dtype) for a in late],
        out_shape=[
            jax.ShapeDtypeStruct((rows, features), bf16),
            jax.ShapeDtypeStruct((rows, features), f32),
            jax.ShapeDtypeStruct((rows, features), bf16),
            jax.ShapeDtypeStruct((HEADS, 1, rows), f32),
            jax.ShapeDtypeStruct((RANK, features), bf16),
            jax.ShapeDtypeStruct((RANK, wide), bf16),
            jax.ShapeDtypeStruct((RANK, wide), bf16),
            jax.ShapeDtypeStruct((RANK, features), bf16),
            jax.ShapeDtypeStruct((RANK, features), bf16),
            jax.ShapeDtypeStruct((RANK, features), bf16),
        ],
        compiler_params=params(("arbitrary",), 60),
        cost_estimate=pl.CostEstimate(
            flops=6 * rows * features * wide,
            bytes_accessed=4 * features * wide + 4 * rows * wide + 24 * rows * features,
            transcendentals=2 * rows * wide,
        ),
    )(*ins, *late)


def close_kernel(
    shape, widths, dq_ref, dk_ref, dv_ref, weight_ref, down_ref, up_ref, mid_ref,
    mask_ref, x_ref, gain_ref, shift_ref, *refs,
):
    count, parts = shape
    devices = count * parts
    remote = courier_lines(dict(dp=count, seq=parts), []) is not None
    terms, refs = refs[:6], refs[6:]
    part_ref, out_ref = refs[:2]
    refs = refs[2:]
    total, grad_up, grad_down, stage = refs[:4]
    step = pl.program_id(0)
    features = x_ref.shape[1]
    if remote:
        landed, sends, arrivals = refs[4:]
        me = lax.axis_index("dp") * parts + lax.axis_index("seq")
        barrier = pltpu.get_barrier_semaphore()

        def peer(k):
            at = lax.rem(me + k, devices)
            return (at // parts, at % parts)

        def rows(at):
            return pl.ds(pl.multiple_of(at * RANK, RANK), RANK)

        def copy_to(k):
            at = lax.rem(me + k, devices)
            return pltpu.make_async_remote_copy(
                src_ref=stage.at[rows(at), :],
                dst_ref=landed.at[rows(me), :],
                send_sem=sends.at[k],
                recv_sem=arrivals.at[k],
                device_id=peer(k),
                device_id_type=pl.DeviceIdType.MESH,
            )

    @pl.when(step == 0)
    def _():
        if remote:

            def greet(k, carry):
                pl.semaphore_signal(
                    barrier, inc=1, device_id=peer(k), device_id_type=pl.DeviceIdType.MESH
                )
                return carry

            lax.fori_loop(1, devices, greet, 0)
        total[...] = jnp.zeros_like(total)
        own_t = chosen_rows(mask_ref[...], mid_ref[...])
        middle = jnp.zeros((x_ref.shape[0], LANES), f32)
        for index, source in enumerate((dq_ref, dk_ref, dv_ref)):
            at = pl.ds(index * features, features)
            middle += dot_nn(source[...], up_ref[at, :])
            grad_up[:, at] = (adapter_scale * dot_nn(own_t, source[...])).astype(bf16)
        middle = (adapter_scale * middle * mask_ref[...]).astype(bf16)
        normed, _ = normalize(x_ref[...].astype(f32))
        act = (normed * gain_ref[...].astype(f32) + shift_ref[...].astype(f32)).astype(bf16)
        total[...] = dot_nt(middle, down_ref[...])
        grad_down[...] = dot_nn(chosen_rows(mask_ref[...], middle), act).astype(bf16)
        at = 0
        for source, width in zip((grad_down, *terms[:3], grad_up, *terms[3:]), widths):
            for device in range(devices):
                stage[device * RANK : (device + 1) * RANK, at : at + width] = source[
                    :, device * width : (device + 1) * width
                ]
            at += width
        if remote:
            pl.semaphore_wait(barrier, devices - 1)

            def send(k, carry):
                copy_to(k).start()
                return carry

            lax.fori_loop(1, devices, send, 0)
            landed[rows(me), :] = stage[rows(me), :]
        else:
            out_ref[...] = stage[...]

    for index, source in enumerate((dq_ref, dk_ref, dv_ref)):

        @pl.when(step == index)
        def _():
            total[...] += dot_nt(source[...], weight_ref[...])

    @pl.when(step == 2)
    def _():
        part_ref[...] = total[...]
        if remote:

            def wait(k, carry):
                copy_to(k).wait()
                return carry

            lax.fori_loop(1, devices, wait, 0)
            out_ref[...] = landed[...]


def close_call(
    mesh_shape, widths, dq, dk, dv, weight, down, up, mid, mask, x, gain, shift, terms,
):
    rows, features = dq.shape
    devices = mesh_shape["dp"] * mesh_shape["seq"]
    remote = courier_lines(mesh_shape, []) is not None
    span = sum(widths)

    def fixed(shape):
        zeros = (0,) * len(shape)
        return pl.BlockSpec(shape, lambda j: zeros, pipeline_mode=pl.Buffered(1))

    ins = [dq, dk, dv, weight, down, up, mid, mask, x, gain, shift, *terms]
    specs = [fixed(a.shape) for a in ins]
    specs[3] = pl.BlockSpec((features, features), lambda j: (0, j))
    shapes = [
        jax.ShapeDtypeStruct((rows, features), f32),
        jax.ShapeDtypeStruct((devices * RANK, span), bf16),
    ]
    scratch = [
        pltpu.VMEM((rows, features), f32),
        pltpu.VMEM((RANK, 3 * features), bf16),
        pltpu.VMEM((RANK, features), bf16),
        pltpu.VMEM((devices * RANK, span), bf16),
    ]
    options = {}
    if remote:
        scratch += [
            pltpu.VMEM((devices * RANK, span), bf16),
            pltpu.SemaphoreType.DMA((devices,)),
            pltpu.SemaphoreType.DMA((devices,)),
        ]
        options = dict(collective_id=4, has_side_effects=True)
    out = pl.pallas_call(
        functools.partial(close_kernel, (mesh_shape["dp"], mesh_shape["seq"]), widths),
        name="close",
        grid=(3,),
        in_specs=specs,
        out_specs=[fixed(a.shape) for a in shapes],
        scratch_shapes=scratch,
        out_shape=shapes,
        compiler_params=pltpu.CompilerParams(
            dimension_semantics=("arbitrary",), vmem_limit_bytes=56 * 1024 * 1024, **options
        ),
        cost_estimate=pl.CostEstimate(
            flops=6 * rows * features * features,
            bytes_accessed=6 * features * features + 20 * rows * features,
            transcendentals=0,
        ),
    )(*ins)
    if remote:
        return out
    landed = lax.all_to_all(
        out[1].reshape(devices, RANK, span), ("dp", "seq"), 0, 0, tiled=True
    ).reshape(devices * RANK, span)
    return out[0], landed


def last_kernel(
    devices, widths, upstream_ref, x_ref, gain_ref, resid_ref, landed_ref, packs_ref, out_ref,
    *grads,
):
    normed, inverse = normalize(x_ref[...].astype(f32))
    out_ref[...] = resid_ref[...] + norm_back(
        upstream_ref[...] * gain_ref[...].astype(f32), normed, inverse
    )

    @pl.when(pl.program_id(0) == 0)
    def _():
        every = packs_ref.shape[0]
        row = lax.broadcasted_iota(jnp.int32, (devices * RANK, every), 0)
        column = lax.broadcasted_iota(jnp.int32, (devices * RANK, every), 1)
        chosen = (column == row // RANK * (every // devices) + VECTORS).astype(bf16)
        adapter = dot_nn(chosen, packs_ref[:, :LANES])[:, 0:1]
        row = lax.broadcasted_iota(jnp.int32, (devices * RANK, LANES), 0)
        column = lax.broadcasted_iota(jnp.int32, (devices * RANK, LANES), 1)
        same = (column // RANK).astype(f32) == adapter
        spread = jnp.where(same & (row % RANK == column % RANK), 1.0, 0.0).astype(bf16)
        sums = dot_tn(landed_ref[...], spread)
        at = 0
        for target, width in zip(grads, widths):
            target[...] = sums[at : at + width, :]
            at += width


def last_call(devices, widths, upstream, x, gain, resid, landed, packs):
    rows, features = x.shape
    tall = rows // 4 if rows % 64 == 0 else rows
    by_rows = pl.BlockSpec((tall, features), lambda i: (i, 0))
    return pl.pallas_call(
        functools.partial(last_kernel, devices, widths),
        name="last",
        grid=(rows // tall,),
        in_specs=[
            by_rows,
            by_rows,
            whole((1, features)),
            by_rows,
            whole(landed.shape),
            whole(packs.shape),
        ],
        out_specs=[by_rows] + [whole((width, LANES)) for width in widths],
        out_shape=[jax.ShapeDtypeStruct((rows, features), f32)]
        + [jax.ShapeDtypeStruct((width, LANES), f32) for width in widths],
        compiler_params=params(("arbitrary",), 50),
    )(upstream, x, gain, resid, landed, packs)


def position_tables(rel_h, rel_w, length):
    wide = ((0, LANES // 2 - (2 * G - 1)), (0, LANES - HEAD_DIM))
    h = jnp.pad(rel_h, wide)
    w = jnp.pad(rel_w, wide)
    h_back = jnp.pad(rel_h[::-1], wide)
    w_back = jnp.pad(rel_w[::-1], wide)
    forward = jnp.concatenate([h_back, h_back, w_back, w_back], axis=0).T
    backward = jnp.concatenate([h, w], axis=0)
    spot = np.arange(length)[:, None]
    lane = np.arange(LANES)[None, :]
    at = np.where((lane // G) % 2 == 0, spot // G, spot % G)
    spots = jnp.asarray(lane % G == at, bf16)
    turned = jnp.asarray(lane % G == G - 1 - at, bf16)
    return forward, backward, spots, turned


def vectors_kernel(devices, sizes, source, target):
    rows = source.shape[0] // devices
    target[...] = jnp.zeros_like(target)
    packs = source[...].astype(f32)
    for line, size in enumerate(sizes):
        for device in range(devices):
            at = device * rows + line
            target[line : line + 1, device * size : (device + 1) * size] = packs[
                at : at + 1, 0:size
            ]


def vectors_call(gathered, devices, sizes):
    return pl.pallas_call(
        functools.partial(vectors_kernel, devices, sizes),
        name="vectors",
        out_shape=jax.ShapeDtypeStruct((VECTORS, devices * max(sizes)), f32),
        compiler_params=params(None, 16),
    )(gathered)


def per_device(
    mesh_shape,
    tokens,
    adapter_index,
    norm1_gain,
    norm1_bias,
    qkv_weight,
    qkv_bias,
    proj_weight,
    proj_bias,
    norm2_gain,
    norm2_bias,
    fc1_weight,
    fc1_bias,
    fc2_weight,
    fc2_bias,
    rel_pos_h,
    rel_pos_w,
    qkv_down,
    qkv_up,
    proj_down,
    proj_up,
    fc1_down,
    fc1_up,
    fc2_down,
    fc2_up,
    out_grad,
):
    axes = ("dp", "seq")
    part_count = mesh_shape["seq"]
    devices = mesh_shape["dp"] * part_count
    images, part_len, features = tokens.shape
    length = part_len * part_count
    own_tokens = tokens[0]
    og = out_grad[0]
    place = lax.axis_index("seq").astype(jnp.int32).reshape(1)

    small = [
        norm1_gain, norm1_bias, qkv_bias, proj_bias, norm2_gain, norm2_bias, fc1_bias, fc2_bias,
        adapter_index.astype(bf16),
    ]
    sizes = [a.shape[0] for a in small]
    pack = jnp.concatenate([jnp.pad(a, (0, 2 * LANES - a.shape[0])) for a in small])
    pack = jnp.pad(pack.reshape(len(small), 2 * LANES), ((0, 16 - len(small)), (0, 0)))

    columns = jnp.arange(LANES, dtype=jnp.int32) // RANK
    mask = (columns[None, :] == adapter_index[:, None]).astype(f32)
    forward_table, back_table, spots, turned_spots = position_tables(rel_pos_h, rel_pos_w, length)
    head_of = np.arange(features)[None, :] // HEAD_DIM
    head_sums = jnp.asarray(head_of == np.arange(HEADS)[:, None], bf16)

    w_fc2 = lax.all_gather(fc2_weight, axes, axis=0, tiled=True)
    w_fc1 = lax.all_gather(fc1_weight, axes, axis=0, tiled=True)
    if part_count == 2:
        image_tokens = [own_tokens, lax.ppermute(own_tokens, "seq", [(0, 1), (1, 0)])]
    else:
        image_tokens = [lax.all_gather(own_tokens, "seq", axis=0, tiled=True)]
    w_qkv, d_qkv, u_qkv, all_small = collect(mesh_shape, [qkv_weight, qkv_down, qkv_up.T, pack])
    vectors = vectors_call(all_small, devices, sizes[:VECTORS])
    g1, s1, b_qkv, b_proj, g2, s2, b_fc1, b_fc2 = (
        vectors[i : i + 1, : devices * sizes[i]] for i in range(VECTORS)
    )
    (heads, mid_qkv, att, lse, aux), rest = front_call(
        mesh_shape, part_len, image_tokens, g1, s1, w_qkv, b_qkv, d_qkv, u_qkv, mask,
        forward_table, spots,
        [proj_weight, proj_down, fc1_down, fc2_down, proj_up.T, fc1_up.T, fc2_up.T],
    )
    w_proj, d_proj, d_fc1, d_fc2, u_proj, u_fc1, u_fc2 = rest
    resid, act_two, mid_proj, mid_fc1, gm_fc2, grad_act = before_call(
        att, own_tokens, og, w_proj, b_proj, d_proj, u_proj, mask, g2, s2, w_fc2, d_fc1, d_fc2,
        u_fc2,
    )
    (block_out, grad_resid, grad_att, inner, gd_fc1, gu_fc1, gd_fc2, gu_fc2, gd_proj,
     gu_proj) = feed_call(
        act_two, mid_fc1, gm_fc2, grad_act, mask, g2, w_fc1, b_fc1, w_fc2, b_fc2, d_fc1, u_fc1,
        d_fc2, u_fc2, d_proj, u_proj, mid_proj, head_sums, [resid, og, att, w_proj],
    )
    if part_count == 2:
        swap = [(0, 1), (1, 0)]
        their_grad, their_lse, their_inner = (
            lax.ppermute(a, "seq", swap)[None] for a in (grad_att, lse, inner)
        )
    else:
        their_grad, their_lse, their_inner = (
            lax.all_gather(a, "seq", axis=0) for a in (grad_att, lse, inner)
        )
    dq, dk_own, dv_own = own_call(
        place, heads, aux, spots, turned_spots, back_table, grad_att, lse, inner
    )
    dk, dv = other_call(
        place, heads, aux, spots, their_grad, their_lse, their_inner, dk_own, dv_own
    )
    mid_own = lax.dynamic_slice_in_dim(mid_qkv, place[0] * part_len, part_len, 0)
    widths = [a.shape[0] for a in (qkv_down, proj_down, fc1_down, fc2_down)]
    widths += [a.shape[1] for a in (qkv_up, proj_up, fc1_up, fc2_up)]
    upstream, landed = close_call(
        mesh_shape, widths, dq, dk, dv, w_qkv, d_qkv, u_qkv, mid_own, mask, own_tokens, g1, s1,
        [gd_proj, gd_fc1, gd_fc2, gu_proj, gu_fc1, gu_fc2],
    )
    input_grad, *grads = last_call(
        devices, widths, upstream, own_tokens, g1, grad_resid, landed, all_small
    )
    return (
        block_out[None],
        input_grad[None],
        grads[0],
        grads[4].T,
        grads[1],
        grads[5].T,
        grads[2],
        grads[6].T,
        grads[3],
        grads[7].T,
    )


def solution(mesh):
    both = ("dp", "seq")
    return jax.shard_map(
        functools.partial(per_device, dict(mesh.shape)),
        mesh=mesh,
        in_specs=(
            P("dp", "seq", None),
            P("dp"),
            P(both),
            P(both),
            P(both, None),
            P(both),
            P(both, None),
            P(both),
            P(both),
            P(both),
            P(both, None),
            P(both),
            P(both, None),
            P(both),
            P(),
            P(),
            P(both, None),
            P(None, both),
            P(both, None),
            P(None, both),
            P(both, None),
            P(None, both),
            P(both, None),
            P(None, both),
            P("dp", "seq", None),
        ),
        out_specs=(
            P("dp", "seq", None),
            P("dp", "seq", None),
            P(both, None),
            P(None, both),
            P(both, None),
            P(None, both),
            P(both, None),
            P(None, both),
            P(both, None),
            P(None, both),
        ),
        check_vma=False,
    )
```
